256 devices in a mesh: order: 8 (over y, core), slab: 32 (over x, z).
Axes of the slice: x: 4, y: 4, z: 8, core: 2. Of those that a mesh axis runs over, the one named last changes fastest.
Arguments:
- previous: float32 [64, 384, 256], P('slab'), may hold values from 1 to 3
- fibre_tensor: float32 [6, 64, 384, 256], P(None, 'slab'), may hold values from -4.6 to 9.6, as said below
- tissue: int32 [64, 384, 256], P('slab'), may hold values 0 or 1
- stim_sites: int32 [16], replicated, may hold values from 0 to 6291455, as said below
- stim_times: float32 [16], replicated, may hold values from 0 to 0.5
Outputs:
- merged: float32 [64, 384, 256], P('slab')
- ordering_fields: float32 [8, 64, 384, 256], P('order', 'slab')
The draws below stay inside these ranges and needn't reach their ends.
Inputs may be any that keep to these rules, and one draw needn't show every extreme that they name: `fibre_tensor`: each voxel's six entries form a symmetric matrix with eigenvalues between 0.4 and 9.6. `stim_sites`: flat indices of voxels of the grid.
All inputs are finite; a program needn't handle non-finite values. No bound on the sum of `tissue` on one device may be relied on, other than what follows from the above.
Results may differ from the reference program's by a relative error of at most 0.00002.
Values sent between devices are 32-bit elements; how exact they have to be, the bound alone decides.
A program may use at most 128 MiB of HBM per device.

```python
import jax
import jax.numpy as jnp
from jax import lax

NY = 384
NZ = 256
NSTIM = 16
NX = 64
N_ORDER = 8


def stimulus_corner(key):
    corner_key = jax.random.fold_in(key, 4049)
    first_key, second_key = jax.random.split(corner_key)
    corner_y = jax.random.randint(first_key, (), 0, NY, jnp.int32)
    corner_z = jax.random.randint(second_key, (), 0, NZ, jnp.int32)
    return (corner_y, corner_z)


def draw_previous(key, part):
    grid_shape = (NX, NY, NZ)
    base_draw = jax.random.uniform(jax.random.fold_in(key, 17), grid_shape, jnp.float32, 0.0, 1.0)
    end_draw = jax.random.uniform(jax.random.fold_in(key, 18), grid_shape, jnp.float32, 0.0, 1.0)
    spot_draw = jax.random.uniform(jax.random.fold_in(key, 19), grid_shape, jnp.float32, 0.0, 1.0)
    spot_level = jax.random.uniform(jax.random.fold_in(key, 20), grid_shape, jnp.float32, 0.0, 1.0)
    interior = 2.4 + 0.6 * base_draw
    end_field = 1.0 + 0.4 * end_draw
    spot_field = 1.0 + spot_level
    plane = jnp.arange(NX, dtype=jnp.int32)[:, None, None]
    at_end = (plane == 0) | (plane == NX - 1)
    field = jnp.where(spot_draw < 0.02, spot_field, interior)
    field = jnp.where(at_end, end_field, field)
    return field.astype(jnp.float32)


def draw_fibre_tensor(key, part):
    subkeys = jax.random.split(key, 4)
    grid_shape = (NX, NY, NZ)
    azimuth = jax.random.uniform(subkeys[0], grid_shape, jnp.float32, -0.4, 0.4)
    height = jax.random.uniform(subkeys[1], grid_shape, jnp.float32, -0.3, 0.3)
    along_draw = jax.random.uniform(subkeys[2], grid_shape, jnp.float32, 0.0, 1.0)
    across_cond = jax.random.uniform(subkeys[3], grid_shape, jnp.float32, 0.4, 1.0)
    along_cond = 6.0 + 3.6 * along_draw
    excess = along_cond - across_cond
    radial = jnp.sqrt(jnp.maximum(1.0 - height * height, 0.0))
    fibre_x = radial * jnp.cos(azimuth)
    fibre_y = radial * jnp.sin(azimuth)
    fibre_z = height
    entries = [across_cond + excess * fibre_x * fibre_x, across_cond + excess * fibre_y * fibre_y, across_cond + excess * fibre_z * fibre_z, excess * fibre_x * fibre_y, excess * fibre_x * fibre_z, excess * fibre_y * fibre_z]
    return jnp.stack(entries).astype(jnp.float32)


def draw_stim_sites(key, part):
    corner_y, corner_z = stimulus_corner(key)
    site_key = jax.random.fold_in(key, 23)
    first_key, second_key = jax.random.split(site_key)
    offset_y = jax.random.randint(first_key, (NSTIM,), 0, max(NY // 8, 1), jnp.int32)
    offset_z = jax.random.randint(second_key, (NSTIM,), 0, max(NZ // 8, 1), jnp.int32)
    stim_rows = jnp.mod(corner_y + 3 * NY // 16 + offset_y, NY)
    stim_columns = jnp.mod(corner_z + 3 * NZ // 16 + offset_z, NZ)
    stim_planes = jnp.where(jnp.arange(NSTIM, dtype=jnp.int32) < NSTIM // 2, 0, NX - 1).astype(jnp.int32)
    return (stim_planes * (NY * NZ) + stim_rows * NZ + stim_columns).astype(jnp.int32)


def touch_ends(values, own_key, least, high):
    longest = values.shape.index(max(values.shape))
    spots = []
    for shift in (0, 1):
        where = [jax.random.randint(jax.random.fold_in(own_key, axis), (), 0, length) for axis, length in enumerate(values.shape)]
        where[longest] = (where[longest] + shift) % values.shape[longest]
        spots.append(tuple(where))
    return values.at[spots[0]].set(least).at[spots[1]].set(high)


def setup_inputs(seed: int = 0) -> dict:
    keys = jax.random.split(jax.random.key(seed), 6)
    return {
        "previous": draw_previous(jax.random.fold_in(keys[5], 71), 0),
        "fibre_tensor": draw_fibre_tensor(jax.random.fold_in(keys[5], 71), 0),
        "tissue": touch_ends((jax.random.randint(keys[2], (NX, NY, NZ), 0, 20) < 17).astype(jnp.int32), jax.random.fold_in(keys[2], 1), 0, 1),
        "stim_sites": draw_stim_sites(jax.random.fold_in(keys[5], 71), 0),
        "stim_times": jnp.clip(jax.random.uniform(keys[4], (NSTIM,), jnp.float32, 0.0, 0.5), 0.0, 0.5),
    }


def compose(earlier, later):
    earlier_add, earlier_min = earlier
    later_add, later_min = later
    return (earlier_add + later_add, jnp.minimum(earlier_min + later_add, later_min))

def slowness(fibre_tensor, tissue, grid_step):
    tensor_xx, tensor_yy, tensor_zz = (fibre_tensor[0], fibre_tensor[1], fibre_tensor[2])
    tensor_xy, tensor_xz, tensor_yz = (fibre_tensor[3], fibre_tensor[4], fibre_tensor[5])
    cofactor_x = tensor_yy * tensor_zz - tensor_yz * tensor_yz
    cofactor_y = tensor_xx * tensor_zz - tensor_xz * tensor_xz
    cofactor_z = tensor_xx * tensor_yy - tensor_xy * tensor_xy
    determinant = tensor_xx * cofactor_x - tensor_xy * (tensor_xy * tensor_zz - tensor_yz * tensor_xz) + tensor_xz * (tensor_xy * tensor_yz - tensor_yy * tensor_xz)
    factor = jnp.where(tissue == 1, 1.0, 4.0).astype(fibre_tensor.dtype) * grid_step
    return (jnp.sqrt(cofactor_x / determinant) * factor, jnp.sqrt(cofactor_y / determinant) * factor, jnp.sqrt(cofactor_z / determinant) * factor)

def line_sweep(step_cost, seeded, along_axis, backward):
    return lax.associative_scan(compose, (step_cost, seeded), reverse=backward, axis=along_axis)[1]

def reference(previous, fibre_tensor, tissue, stim_sites, stim_times):
    grid_step = 2.0 / NX
    cost_x, cost_y, cost_z = slowness(fibre_tensor, tissue, grid_step)
    seeded = previous.reshape(-1).at[stim_sites].min(stim_times).reshape(previous.shape)
    sweeps = []
    for group_index in range(N_ORDER):
        sweep_field = line_sweep(cost_z, seeded, 2, group_index >> 2 & 1 == 1)
        sweep_field = line_sweep(cost_y, sweep_field, 1, group_index >> 1 & 1 == 1)
        sweep_field = line_sweep(cost_x, sweep_field, 0, group_index & 1 == 1)
        sweeps.append(sweep_field)
    ordering_fields = jnp.stack(sweeps)
    merged = lax.optimization_barrier(jnp.min(ordering_fields, axis=0))
    return (merged, ordering_fields)
```

```python
import functools

import jax
import jax.numpy as jnp
from jax import lax
from jax.experimental import pallas as pl
from jax.experimental.pallas import tpu as pltpu
from jax.sharding import PartitionSpec as P

ROWS = 8


def scan_step(a, m, k, axis, reverse, last):
    n = a.shape[axis]
    index = lax.broadcasted_iota(jnp.int32, a.shape, axis)
    shift = n - k if reverse else k
    source = pltpu.roll(index, shift, axis)
    valid = source == (index + k if reverse else index - k)
    a_src = pltpu.roll(a, shift, axis)
    m_src = pltpu.roll(m, shift, axis)
    m = jnp.where(valid, jnp.minimum(m_src + a, m), m)
    if not last:
        a = jnp.where(valid, a_src + a, a)
    return a, m


def block_scan(a, m, axis, reverse, need_sum):
    n = a.shape[axis]
    k = 1
    while k < n:
        a, m = scan_step(a, m, k, axis, reverse, last=(2 * k >= n) and not need_sum)
        k *= 2
    return a, m


def local_kernel(flags, fibre, tissue, seeded, line_add, line_min, cost_x, cost_y, field,
                 *, grid_step):
    planes, cells_y, cells_z = seeded.shape
    blocks = cells_y // ROWS
    inf = jnp.float32(jnp.inf)

    def costs_and_z(reverse):
        def body(i, carry):
            p = i // blocks
            rows = pl.ds(pl.multiple_of((i % blocks) * ROWS, ROWS), ROWS)
            xx = fibre[0, p, rows, :]
            yy = fibre[1, p, rows, :]
            zz = fibre[2, p, rows, :]
            xy = fibre[3, p, rows, :]
            xz = fibre[4, p, rows, :]
            yz = fibre[5, p, rows, :]
            cx = yy * zz - yz * yz
            cy = xx * zz - xz * xz
            cz = xx * yy - xy * xy
            det = xx * cx - xy * (xy * zz - yz * xz) + xz * (xy * yz - yy * xz)
            factor = jnp.where(tissue[p, rows, :] == 1, 1.0, 4.0).astype(jnp.float32) * grid_step
            cost_x[p, rows, :] = jnp.sqrt(cx / det) * factor
            cost_y[p, rows, :] = jnp.sqrt(cy / det) * factor
            step_z = jnp.sqrt(cz / det) * factor
            _, u = block_scan(step_z, seeded[p, rows, :], 1, reverse, False)
            field[p, rows, :] = u
            return carry

        lax.fori_loop(0, planes * blocks, body, 0)

    def sweep_y(reverse):
        def body(j, carry):
            i = blocks - 1 - j if reverse else j
            rows = pl.ds(pl.multiple_of(i * ROWS, ROWS), ROWS)
            out = []
            for p in range(planes):
                a, m = block_scan(cost_y[p, rows, :], field[p, rows, :], 0, reverse, True)
                u = jnp.minimum(carry[p] + a, m)
                field[p, rows, :] = u
                edge = u[0:1, :] if reverse else u[ROWS - 1:ROWS, :]
                out.append(jnp.broadcast_to(edge, u.shape))
            return tuple(out)

        start = tuple(jnp.full((ROWS, cells_z), inf, jnp.float32) for _ in range(planes))
        lax.fori_loop(0, blocks, body, start)

    def sweep_x(reverse):
        def body(i, carry):
            rows = pl.ds(pl.multiple_of(i * ROWS, ROWS), ROWS)
            order = range(planes - 1, -1, -1) if reverse else range(planes)
            a = None
            m = None
            for p in order:
                c = cost_x[p, rows, :]
                u = field[p, rows, :]
                if a is None:
                    a, m = c, u
                else:
                    a, m = a + c, jnp.minimum(m + c, u)
                line_add[p, rows, :] = a
                line_min[p, rows, :] = m
            return carry

        lax.fori_loop(0, blocks, body, 0)

    for flag, fn in ((flags[2], costs_and_z), (flags[1], sweep_y), (flags[0], sweep_x)):
        pl.when(flag == 1)(functools.partial(fn, True))
        pl.when(flag != 1)(functools.partial(fn, False))


def local_sweeps(flags, fibre, tissue, seeded, grid_step):
    planes, cells_y, cells_z = seeded.shape
    plane = jax.ShapeDtypeStruct(seeded.shape, jnp.float32)
    vmem = pl.BlockSpec(memory_space=pltpu.VMEM)
    elements = planes * cells_y * cells_z
    return pl.pallas_call(
        functools.partial(local_kernel, grid_step=grid_step),
        out_shape=(plane, plane),
        in_specs=[pl.BlockSpec(memory_space=pltpu.SMEM), vmem, vmem, vmem],
        out_specs=(vmem, vmem),
        scratch_shapes=[pltpu.VMEM(seeded.shape, jnp.float32) for _ in range(3)],
        compiler_params=pltpu.CompilerParams(vmem_limit_bytes=48 * 1024 * 1024),
        cost_estimate=pl.CostEstimate(
            flops=300 * elements, transcendentals=6 * elements, bytes_accessed=44 * elements
        ),
    )(flags, fibre, tissue, seeded)


def shifted(value, distance, orders, slabs):
    route = []
    for g in range(orders):
        for s in range(slabs):
            t = s + distance if g % 2 == 0 else s - distance
            if 0 <= t < slabs:
                route.append((g * slabs + s, g * slabs + t))
    return lax.ppermute(value, ("order", "slab"), route)


def shards(previous, fibre_tensor, tissue, stim_sites, stim_times):
    planes, cells_y, cells_z = previous.shape
    slabs = lax.axis_size("slab")
    orders = lax.axis_size("order")
    slab_index = lax.axis_index("slab")
    group_index = lax.axis_index("order")
    grid_step = 2.0 / (planes * slabs)

    plane_index = stim_sites // (cells_y * cells_z) - slab_index * planes
    inside = (plane_index >= 0) & (plane_index < planes)
    plane_index = jnp.where(inside, plane_index, planes)
    row_index = stim_sites // cells_z % cells_y
    column_index = stim_sites % cells_z
    seeded = previous.at[plane_index, row_index, column_index].min(stim_times, mode="drop")

    bits = jnp.stack([group_index % 2, group_index // 2 % 2, group_index // 4 % 2]).astype(jnp.int32)
    line_add, line_min = local_sweeps(bits, fibre_tensor, tissue, seeded, grid_step)

    backward_x = group_index % 2 == 1
    rank = jnp.where(backward_x, slabs - 1 - slab_index, slab_index)
    edge = jnp.where(backward_x, 0, planes - 1)
    total_add = lax.dynamic_index_in_dim(line_add, edge, 0, keepdims=False)
    total_min = lax.dynamic_index_in_dim(line_min, edge, 0, keepdims=False)

    distance = 1
    while distance < slabs:
        if 2 * distance < slabs:
            got = shifted(jnp.stack([total_add, total_min]), distance, orders, slabs)
            take = rank >= distance
            total_min = jnp.where(take, jnp.minimum(got[1] + total_add, total_min), total_min)
            total_add = jnp.where(take, got[0] + total_add, total_add)
        else:
            got = shifted(total_min, distance, orders, slabs)
            total_min = jnp.where(rank >= distance, jnp.minimum(got + total_add, total_min), total_min)
        distance *= 2
    got = shifted(total_min, 1, orders, slabs)
    incoming = jnp.where(rank >= 1, got, jnp.inf)

    sweep_field = jnp.minimum(incoming[None] + line_add, line_min)
    merged = sweep_field
    mask = 1
    while mask < orders:
        got = lax.ppermute(merged, "order", [(g, g ^ mask) for g in range(orders)])
        merged = jnp.minimum(merged, got)
        mask *= 2
    return (merged, sweep_field[None])


def solution(mesh):
    placed = (P("slab", None, None), P(None, "slab", None, None), P("slab", None, None), P(), P())
    return jax.shard_map(
        shards,
        mesh=mesh,
        in_specs=placed,
        out_specs=(P("slab", None, None), P("order", "slab", None, None)),
        check_vma=False,
    )
```

```python
import functools

import jax
import jax.numpy as jnp
from jax import lax
from jax.experimental import pallas as pl
from jax.experimental.pallas import tpu as pltpu
from jax.sharding import PartitionSpec as P

ROWS = 8
CHUNK = 32


def scan_step(a, m, k, axis, reverse, last):
    n = a.shape[axis]
    index = lax.broadcasted_iota(jnp.int32, a.shape, axis)
    shift = n - k if reverse else k
    valid = index < n - k if reverse else index >= k
    a_src = pltpu.roll(a, shift, axis)
    m_src = pltpu.roll(m, shift, axis)
    m = jnp.where(valid, jnp.minimum(m_src + a, m), m)
    if not last:
        a = jnp.where(valid, a_src + a, a)
    return a, m


def block_scan(a, m, axis, reverse, need_sum):
    n = a.shape[axis]
    k = 1
    while k < n:
        a, m = scan_step(a, m, k, axis, reverse, last=(2 * k >= n) and not need_sum)
        k *= 2
    return a, m


def local_kernel(flags, fibre, tissue, seeded, cost_x, field, cost_y, *, grid_step):
    planes, cells_y, cells_z = seeded.shape
    chunks = cells_y // CHUNK
    inf = jnp.float32(jnp.inf)

    def costs_and_z(reverse):
        def body(i, carry):
            p = i // chunks
            rows = pl.ds(pl.multiple_of((i % chunks) * CHUNK, CHUNK), CHUNK)
            xx = fibre[0, p, rows, :]
            yy = fibre[1, p, rows, :]
            zz = fibre[2, p, rows, :]
            xy = fibre[3, p, rows, :]
            xz = fibre[4, p, rows, :]
            yz = fibre[5, p, rows, :]
            cx = yy * zz - yz * yz
            cy = xx * zz - xz * xz
            cz = xx * yy - xy * xy
            det = xx * cx - xy * (xy * zz - yz * xz) + xz * (xy * yz - yy * xz)
            factor = jnp.where(tissue[p, rows, :] == 1, 1.0, 4.0).astype(jnp.float32) * grid_step
            cost_x[p, rows, :] = jnp.sqrt(cx / det) * factor
            cost_y[p, rows, :] = jnp.sqrt(cy / det) * factor
            step_z = jnp.sqrt(cz / det) * factor
            _, u = block_scan(step_z, seeded[p, rows, :], 1, reverse, False)
            field[p, rows, :] = u
            return carry

        lax.fori_loop(0, planes * chunks, body, 0)

    def sweep_y(reverse):
        def body(j, carry):
            i = chunks - 1 - j if reverse else j
            rows = pl.ds(pl.multiple_of(i * CHUNK, CHUNK), CHUNK)
            out = []
            for p in range(planes):
                a, m = block_scan(cost_y[p, rows, :], field[p, rows, :], 0, reverse, True)
                u = jnp.minimum(carry[p] + a, m)
                field[p, rows, :] = u
                edge = u[0:1, :] if reverse else u[CHUNK - 1:CHUNK, :]
                out.append(jnp.broadcast_to(edge, u.shape))
            return tuple(out)

        start = tuple(jnp.full((CHUNK, cells_z), inf, jnp.float32) for _ in range(planes))
        lax.fori_loop(0, chunks, body, start)

    for flag, fn in ((flags[2], costs_and_z), (flags[1], sweep_y)):
        pl.when(flag == 1)(functools.partial(fn, True))
        pl.when(flag != 1)(functools.partial(fn, False))


def local_sweeps(flags, fibre, tissue, seeded, grid_step):
    planes, cells_y, cells_z = seeded.shape
    plane = jax.ShapeDtypeStruct(seeded.shape, jnp.float32)
    vmem = pl.BlockSpec(memory_space=pltpu.VMEM)
    elements = planes * cells_y * cells_z
    return pl.pallas_call(
        functools.partial(local_kernel, grid_step=grid_step),
        out_shape=(plane, plane),
        in_specs=[pl.BlockSpec(memory_space=pltpu.SMEM), vmem, vmem, vmem],
        out_specs=(vmem, vmem),
        scratch_shapes=[pltpu.VMEM(seeded.shape, jnp.float32)],
        compiler_params=pltpu.CompilerParams(vmem_limit_bytes=48 * 1024 * 1024),
        cost_estimate=pl.CostEstimate(
            flops=300 * elements, transcendentals=6 * elements, bytes_accessed=40 * elements
        ),
    )(flags, fibre, tissue, seeded)


def shifted(value, distance, orders, slabs):
    route = []
    for g in range(orders):
        for s in range(slabs):
            t = s + distance if g % 2 == 0 else s - distance
            if 0 <= t < slabs:
                route.append((g * slabs + s, g * slabs + t))
    return lax.ppermute(value, ("order", "slab"), route)


def shards(previous, fibre_tensor, tissue, stim_sites, stim_times):
    planes, cells_y, cells_z = previous.shape
    slabs = lax.axis_size("slab")
    orders = lax.axis_size("order")
    slab_index = lax.axis_index("slab")
    group_index = lax.axis_index("order")
    grid_step = 2.0 / (planes * slabs)

    plane_index = stim_sites // (cells_y * cells_z) - slab_index * planes
    inside = (plane_index >= 0) & (plane_index < planes)
    plane_index = jnp.where(inside, plane_index, planes)
    row_index = stim_sites // cells_z % cells_y
    column_index = stim_sites % cells_z
    seeded = previous.at[plane_index, row_index, column_index].min(stim_times, mode="drop")

    bits = jnp.stack([group_index % 2, group_index // 2 % 2, group_index // 4 % 2]).astype(jnp.int32)
    cost_x, field = local_sweeps(bits, fibre_tensor, tissue, seeded, grid_step)

    up_add = jnp.stack([cost_x[0], cost_x[0] + cost_x[1]])
    up_min = jnp.stack([field[0], jnp.minimum(field[0] + cost_x[1], field[1])])
    down_add = jnp.stack([cost_x[1] + cost_x[0], cost_x[1]])
    down_min = jnp.stack([jnp.minimum(field[1] + cost_x[0], field[0]), field[1]])

    backward_x = group_index % 2 == 1
    line_add = jnp.where(backward_x, down_add, up_add)
    line_min = jnp.where(backward_x, down_min, up_min)

    core = group_index % 2
    own_plane = lax.dynamic_index_in_dim(field, core, 0, keepdims=False)
    for mask in [m for m in (2, 4, 8, 16) if m < orders]:
        got = lax.ppermute(own_plane, "order", [(g, g ^ mask) for g in range(orders)])
        own_plane = jnp.minimum(own_plane, got)
    other_plane = lax.ppermute(own_plane, "order", [(g, g ^ 1) for g in range(orders)])
    least0 = jnp.where(core == 0, own_plane, other_plane)
    least1 = jnp.where(core == 0, other_plane, own_plane)
    least_local = jnp.stack([
        jnp.minimum(least0, least1 + cost_x[0]),
        jnp.minimum(least1, least0 + cost_x[1]),
    ])

    rank = jnp.where(backward_x, slabs - 1 - slab_index, slab_index)
    total_add = jnp.where(backward_x, line_add[0], line_add[planes - 1])
    total_min = jnp.where(backward_x, line_min[0], line_min[planes - 1])

    distance = 1
    while distance < slabs:
        if 2 * distance < slabs:
            got = shifted(jnp.stack([total_add, total_min]), distance, orders, slabs)
            take = rank >= distance
            total_min = jnp.where(take, jnp.minimum(got[1] + total_add, total_min), total_min)
            total_add = jnp.where(take, got[0] + total_add, total_add)
        else:
            got = shifted(total_min, distance, orders, slabs)
            total_min = jnp.where(rank >= distance, jnp.minimum(got + total_add, total_min), total_min)
        distance *= 2
    got = shifted(total_min, 1, orders, slabs)
    incoming = jnp.where(rank >= 1, got, jnp.inf)

    sweep_field = jnp.minimum(incoming[None] + line_add, line_min)

    least_in = incoming
    for mask in [m for m in (2, 4, 8, 16) if m < orders]:
        got = lax.ppermute(least_in, "order", [(g, g ^ mask) for g in range(orders)])
        least_in = jnp.minimum(least_in, got)
    other_in = lax.ppermute(least_in, "order", [(g, g ^ 1) for g in range(orders)])
    up_in = jnp.where(core == 0, least_in, other_in)
    down_in = jnp.where(core == 0, other_in, least_in)
    merged = jnp.minimum(
        least_local,
        jnp.minimum(up_in[None] + up_add, down_in[None] + down_add),
    )
    return (merged, sweep_field[None])


def solution(mesh):
    placed = (P("slab", None, None), P(None, "slab", None, None), P("slab", None, None), P(), P())
    return jax.shard_map(
        shards,
        mesh=mesh,
        in_specs=placed,
        out_specs=(P("slab", None, None), P("order", "slab", None, None)),
        check_vma=False,
    )
```

```python
import functools

import jax
import jax.numpy as jnp
from jax import lax
from jax.experimental import pallas as pl
from jax.experimental.pallas import tpu as pltpu
from jax.sharding import PartitionSpec as P

ROWS = 8
CHUNK = 32


def scan_step(a, m, k, axis, reverse, last):
    n = a.shape[axis]
    index = lax.broadcasted_iota(jnp.int32, a.shape, axis)
    shift = n - k if reverse else k
    valid = index < n - k if reverse else index >= k
    a_src = pltpu.roll(a, shift, axis)
    m_src = pltpu.roll(m, shift, axis)
    m = jnp.where(valid, jnp.minimum(m_src + a, m), m)
    if not last:
        a = jnp.where(valid, a_src + a, a)
    return a, m


def block_scan(a, m, axis, reverse, need_sum):
    n = a.shape[axis]
    k = 1
    while k < n:
        a, m = scan_step(a, m, k, axis, reverse, last=(2 * k >= n) and not need_sum)
        k *= 2
    return a, m


def local_kernel(flags, fibre, tissue, seeded, cost_x, field, cost_y, *, grid_step):
    planes, cells_y, cells_z = seeded.shape
    chunks = cells_y // CHUNK
    inf = jnp.float32(jnp.inf)

    def costs_and_z(reverse):
        def body(i, carry):
            p = i // chunks
            rows = pl.ds(pl.multiple_of((i % chunks) * CHUNK, CHUNK), CHUNK)
            xx = fibre[0, p, rows, :]
            yy = fibre[1, p, rows, :]
            zz = fibre[2, p, rows, :]
            xy = fibre[3, p, rows, :]
            xz = fibre[4, p, rows, :]
            yz = fibre[5, p, rows, :]
            cx = yy * zz - yz * yz
            cy = xx * zz - xz * xz
            cz = xx * yy - xy * xy
            det = xx * cx - xy * (xy * zz - yz * xz) + xz * (xy * yz - yy * xz)
            factor = jnp.where(tissue[p, rows, :] == 1, 1.0, 4.0).astype(jnp.float32) * grid_step
            cost_x[p, rows, :] = jnp.sqrt(cx / det) * factor
            cost_y[p, rows, :] = jnp.sqrt(cy / det) * factor
            step_z = jnp.sqrt(cz / det) * factor
            _, u = block_scan(step_z, seeded[p, rows, :], 1, reverse, False)
            field[p, rows, :] = u
            return carry

        lax.fori_loop(0, planes * chunks, body, 0)

    def sweep_y(reverse):
        def body(j, carry):
            i = chunks - 1 - j if reverse else j
            rows = pl.ds(pl.multiple_of(i * CHUNK, CHUNK), CHUNK)
            out = []
            for p in range(planes):
                a, m = block_scan(cost_y[p, rows, :], field[p, rows, :], 0, reverse, True)
                u = jnp.minimum(carry[p] + a, m)
                field[p, rows, :] = u
                edge = u[0:1, :] if reverse else u[CHUNK - 1:CHUNK, :]
                out.append(jnp.broadcast_to(edge, u.shape))
            return tuple(out)

        start = tuple(jnp.full((CHUNK, cells_z), inf, jnp.float32) for _ in range(planes))
        lax.fori_loop(0, chunks, body, start)

    for flag, fn in ((flags[2], costs_and_z), (flags[1], sweep_y)):
        pl.when(flag == 1)(functools.partial(fn, True))
        pl.when(flag != 1)(functools.partial(fn, False))


def local_sweeps(flags, fibre, tissue, seeded, grid_step):
    planes, cells_y, cells_z = seeded.shape
    plane = jax.ShapeDtypeStruct(seeded.shape, jnp.float32)
    vmem = pl.BlockSpec(memory_space=pltpu.VMEM)
    elements = planes * cells_y * cells_z
    return pl.pallas_call(
        functools.partial(local_kernel, grid_step=grid_step),
        out_shape=(plane, plane),
        in_specs=[pl.BlockSpec(memory_space=pltpu.SMEM), vmem, vmem, vmem],
        out_specs=(vmem, vmem),
        scratch_shapes=[pltpu.VMEM(seeded.shape, jnp.float32)],
        compiler_params=pltpu.CompilerParams(vmem_limit_bytes=48 * 1024 * 1024),
        cost_estimate=pl.CostEstimate(
            flops=300 * elements, transcendentals=6 * elements, bytes_accessed=40 * elements
        ),
    )(flags, fibre, tissue, seeded)


RELAY_ROWS = 16


def relay_kernel(total_add, total_min, incoming, inbox, outbox, send_sems, recv_sems):
    cells_y, cells_z = incoming.shape
    chunks = cells_y // RELAY_ROWS
    slabs = lax.axis_size("slab")
    slab = lax.axis_index("slab")
    group = lax.axis_index("order")
    step = 1 - 2 * (group % 2)
    rank = jnp.where(group % 2 == 1, slabs - 1 - slab, slab)
    has_prev = rank > 0
    has_next = rank < slabs - 1
    prev_slab = slab - step
    next_slab = slab + step

    barrier = pltpu.get_barrier_semaphore()

    @pl.when(has_prev)
    def _():
        pl.semaphore_signal(barrier, 1, device_id=(group, prev_slab), device_id_type=pl.DeviceIdType.MESH)

    @pl.when(has_next)
    def _():
        pl.semaphore_signal(barrier, 1, device_id=(group, next_slab), device_id_type=pl.DeviceIdType.MESH)

    @pl.when(has_prev & has_next)
    def _():
        pl.semaphore_wait(barrier, 2)

    @pl.when(has_prev != has_next)
    def _():
        pl.semaphore_wait(barrier, 1)

    def send(c):
        return pltpu.make_async_remote_copy(
            src_ref=outbox.at[c],
            dst_ref=inbox.at[c],
            send_sem=send_sems.at[c],
            recv_sem=recv_sems.at[c],
            device_id=(group, next_slab),
            device_id_type=pl.DeviceIdType.MESH,
        )

    def body(c, carry):
        rows = pl.ds(pl.multiple_of(c * RELAY_ROWS, RELAY_ROWS), RELAY_ROWS)

        @pl.when(has_prev)
        def _():
            send(c).wait_recv()
            incoming[rows, :] = inbox[c]

        @pl.when(jnp.logical_not(has_prev))
        def _():
            incoming[rows, :] = jnp.full((RELAY_ROWS, cells_z), jnp.inf, jnp.float32)

        @pl.when(has_next)
        def _():
            outbox[c] = jnp.minimum(incoming[rows, :] + total_add[rows, :], total_min[rows, :])
            send(c).start()

        return carry

    lax.fori_loop(0, chunks, body, 0)

    def drain(c, carry):
        @pl.when(has_next)
        def _():
            send(c).wait_send()

        return carry

    lax.fori_loop(0, chunks, drain, 0)


def relay(total_add, total_min):
    cells_y, cells_z = total_add.shape
    chunks = cells_y // RELAY_ROWS
    vmem = pl.BlockSpec(memory_space=pltpu.VMEM)
    return pl.pallas_call(
        relay_kernel,
        out_shape=jax.ShapeDtypeStruct(total_add.shape, jnp.float32),
        in_specs=[vmem, vmem],
        out_specs=vmem,
        scratch_shapes=[
            pltpu.VMEM((chunks, RELAY_ROWS, cells_z), jnp.float32),
            pltpu.VMEM((chunks, RELAY_ROWS, cells_z), jnp.float32),
            pltpu.SemaphoreType.DMA((chunks,)),
            pltpu.SemaphoreType.DMA((chunks,)),
        ],
        compiler_params=pltpu.CompilerParams(collective_id=0, has_side_effects=True),
    )(total_add, total_min)


def shards(previous, fibre_tensor, tissue, stim_sites, stim_times):
    planes, cells_y, cells_z = previous.shape
    slabs = lax.axis_size("slab")
    orders = lax.axis_size("order")
    slab_index = lax.axis_index("slab")
    group_index = lax.axis_index("order")
    grid_step = 2.0 / (planes * slabs)

    plane_index = stim_sites // (cells_y * cells_z) - slab_index * planes
    inside = (plane_index >= 0) & (plane_index < planes)
    plane_index = jnp.where(inside, plane_index, planes)
    row_index = stim_sites // cells_z % cells_y
    column_index = stim_sites % cells_z
    seeded = previous.at[plane_index, row_index, column_index].min(stim_times, mode="drop")

    bits = jnp.stack([group_index % 2, group_index // 2 % 2, group_index // 4 % 2]).astype(jnp.int32)
    cost_x, field = local_sweeps(bits, fibre_tensor, tissue, seeded, grid_step)

    up_add = jnp.stack([cost_x[0], cost_x[0] + cost_x[1]])
    up_min = jnp.stack([field[0], jnp.minimum(field[0] + cost_x[1], field[1])])
    down_add = jnp.stack([cost_x[1] + cost_x[0], cost_x[1]])
    down_min = jnp.stack([jnp.minimum(field[1] + cost_x[0], field[0]), field[1]])

    backward_x = group_index % 2 == 1
    line_add = jnp.where(backward_x, down_add, up_add)
    line_min = jnp.where(backward_x, down_min, up_min)

    core = group_index % 2
    own_plane = lax.dynamic_index_in_dim(field, core, 0, keepdims=False)
    for mask in [m for m in (2, 4, 8, 16) if m < orders]:
        got = lax.ppermute(own_plane, "order", [(g, g ^ mask) for g in range(orders)])
        own_plane = jnp.minimum(own_plane, got)
    other_plane = lax.ppermute(own_plane, "order", [(g, g ^ 1) for g in range(orders)])
    least0 = jnp.where(core == 0, own_plane, other_plane)
    least1 = jnp.where(core == 0, other_plane, own_plane)
    least_local = jnp.stack([
        jnp.minimum(least0, least1 + cost_x[0]),
        jnp.minimum(least1, least0 + cost_x[1]),
    ])

    total_add = jnp.where(backward_x, line_add[0], line_add[planes - 1])
    total_min = jnp.where(backward_x, line_min[0], line_min[planes - 1])

    incoming = relay(total_add, total_min)

    sweep_field = jnp.minimum(incoming[None] + line_add, line_min)

    least_in = incoming
    for mask in [m for m in (2, 4, 8, 16) if m < orders]:
        got = lax.ppermute(least_in, "order", [(g, g ^ mask) for g in range(orders)])
        least_in = jnp.minimum(least_in, got)
    other_in = lax.ppermute(least_in, "order", [(g, g ^ 1) for g in range(orders)])
    up_in = jnp.where(core == 0, least_in, other_in)
    down_in = jnp.where(core == 0, other_in, least_in)
    merged = jnp.minimum(
        least_local,
        jnp.minimum(up_in[None] + up_add, down_in[None] + down_add),
    )
    return (merged, sweep_field[None])


def solution(mesh):
    placed = (P("slab", None, None), P(None, "slab", None, None), P("slab", None, None), P(), P())
    return jax.shard_map(
        shards,
        mesh=mesh,
        in_specs=placed,
        out_specs=(P("slab", None, None), P("order", "slab", None, None)),
        check_vma=False,
    )
```

```python
import functools

import jax
import jax.numpy as jnp
from jax import lax
from jax.experimental import pallas as pl
from jax.experimental.pallas import tpu as pltpu
from jax.sharding import PartitionSpec as P

ROWS = 8
CHUNK = 32


def scan_step(a, m, k, axis, reverse, last):
    n = a.shape[axis]
    index = lax.broadcasted_iota(jnp.int32, a.shape, axis)
    shift = n - k if reverse else k
    valid = index < n - k if reverse else index >= k
    a_src = pltpu.roll(a, shift, axis)
    m_src = pltpu.roll(m, shift, axis)
    m = jnp.where(valid, jnp.minimum(m_src + a, m), m)
    if not last:
        a = jnp.where(valid, a_src + a, a)
    return a, m


def block_scan(a, m, axis, reverse, need_sum):
    n = a.shape[axis]
    k = 1
    while k < n:
        a, m = scan_step(a, m, k, axis, reverse, last=(2 * k >= n) and not need_sum)
        k *= 2
    return a, m


def local_kernel(flags, fibre, tissue, seeded, cost_x, field, cost_y, *, grid_step):
    planes, cells_y, cells_z = seeded.shape
    chunks = cells_y // CHUNK
    inf = jnp.float32(jnp.inf)

    def costs_and_z(reverse):
        def body(i, carry):
            p = i // chunks
            rows = pl.ds(pl.multiple_of((i % chunks) * CHUNK, CHUNK), CHUNK)
            xx = fibre[0, p, rows, :]
            yy = fibre[1, p, rows, :]
            zz = fibre[2, p, rows, :]
            xy = fibre[3, p, rows, :]
            xz = fibre[4, p, rows, :]
            yz = fibre[5, p, rows, :]
            cx = yy * zz - yz * yz
            cy = xx * zz - xz * xz
            cz = xx * yy - xy * xy
            det = xx * cx - xy * (xy * zz - yz * xz) + xz * (xy * yz - yy * xz)
            factor = jnp.where(tissue[p, rows, :] == 1, 1.0, 4.0).astype(jnp.float32) * grid_step
            cost_x[p, rows, :] = jnp.sqrt(cx / det) * factor
            cost_y[p, rows, :] = jnp.sqrt(cy / det) * factor
            step_z = jnp.sqrt(cz / det) * factor
            _, u = block_scan(step_z, seeded[p, rows, :], 1, reverse, False)
            field[p, rows, :] = u
            return carry

        lax.fori_loop(0, planes * chunks, body, 0)

    def sweep_y(reverse):
        def body(j, carry):
            i = chunks - 1 - j if reverse else j
            rows = pl.ds(pl.multiple_of(i * CHUNK, CHUNK), CHUNK)
            out = []
            for p in range(planes):
                a, m = block_scan(cost_y[p, rows, :], field[p, rows, :], 0, reverse, True)
                u = jnp.minimum(carry[p] + a, m)
                field[p, rows, :] = u
                edge = u[0:1, :] if reverse else u[CHUNK - 1:CHUNK, :]
                out.append(jnp.broadcast_to(edge, u.shape))
            return tuple(out)

        start = tuple(jnp.full((CHUNK, cells_z), inf, jnp.float32) for _ in range(planes))
        lax.fori_loop(0, chunks, body, start)

    for flag, fn in ((flags[2], costs_and_z), (flags[1], sweep_y)):
        pl.when(flag == 1)(functools.partial(fn, True))
        pl.when(flag != 1)(functools.partial(fn, False))


def local_sweeps(flags, fibre, tissue, seeded, grid_step):
    planes, cells_y, cells_z = seeded.shape
    plane = jax.ShapeDtypeStruct(seeded.shape, jnp.float32)
    vmem = pl.BlockSpec(memory_space=pltpu.VMEM)
    elements = planes * cells_y * cells_z
    return pl.pallas_call(
        functools.partial(local_kernel, grid_step=grid_step),
        out_shape=(plane, plane),
        in_specs=[pl.BlockSpec(memory_space=pltpu.SMEM), vmem, vmem, vmem],
        out_specs=(vmem, vmem),
        scratch_shapes=[pltpu.VMEM(seeded.shape, jnp.float32)],
        compiler_params=pltpu.CompilerParams(vmem_limit_bytes=48 * 1024 * 1024),
        cost_estimate=pl.CostEstimate(
            flops=300 * elements, transcendentals=6 * elements, bytes_accessed=40 * elements
        ),
    )(flags, fibre, tissue, seeded)


RELAY_ROWS = 16
LINE = 8


def relay_kernel(total_add, total_min, incoming, before, line_total, box1_in, box1_out, box2_in,
                 box2_out, box3_in, send1, recv1, send2, recv2, send3, recv3, *, line):
    cells_y, cells_z = incoming.shape
    chunks = cells_y // RELAY_ROWS
    slabs = lax.axis_size("slab")
    lines = slabs // line
    half = line // 2
    slab = lax.axis_index("slab")
    group = lax.axis_index("order")
    odd = group % 2
    rank = slab + odd * (slabs - 1 - 2 * slab)
    col = rank // line
    pos = rank % line
    last = line - 1
    mesh_id = pl.DeviceIdType.MESH

    def device(r):
        return (group, r + odd * (slabs - 1 - 2 * r))

    def at(c, p):
        return device(c * line + p)

    first_col = col == 0
    is_end = pos == last
    in_up = pos < half
    in_down = (pos >= half) & (pos < last)
    up_next = pos + 1 < half
    down_next = pos > half

    barrier = pltpu.get_barrier_semaphore()
    neighbours = []
    neighbours.append((pos > 0, at(col, pos - 1)))
    neighbours.append((pos < last, at(col, pos + 1)))
    neighbours.append(((pos == 0) & (col > 0) & (last > 0), at(col, last)))
    neighbours.append((is_end & (col > 0) & (last > 0), at(col, 0)))
    neighbours.append((is_end & (col > 0), at(col - 1, last)))
    neighbours.append((is_end & (col < lines - 1), at(col + 1, last)))
    count = jnp.int32(0)
    for cond, dev in neighbours:
        @pl.when(cond)
        def _():
            pl.semaphore_signal(barrier, 1, device_id=dev, device_id_type=mesh_id)

        count = count + cond.astype(jnp.int32)
    pl.semaphore_wait(barrier, count)

    def copy1(c):
        return pltpu.make_async_remote_copy(box1_out.at[c], box1_in.at[c], send1.at[c], recv1.at[c],
                                            device_id=at(col, pos + 1), device_id_type=mesh_id)

    def copy2(c):
        return pltpu.make_async_remote_copy(box2_out.at[c], box2_in.at[c], send2.at[c], recv2.at[c],
                                            device_id=at(col + 1, last), device_id_type=mesh_id)

    def copy3_from_end(c, k, target):
        return pltpu.make_async_remote_copy(box2_in.at[c], box3_in.at[c], send3.at[c, k], recv3.at[c],
                                            device_id=target, device_id_type=mesh_id)

    def copy3_relay(c, target):
        return pltpu.make_async_remote_copy(box3_in.at[c], box3_in.at[c], send3.at[c, 0], recv3.at[c],
                                            device_id=target, device_id_type=mesh_id)

    def rows_of(c):
        return pl.ds(pl.multiple_of(c * RELAY_ROWS, RELAY_ROWS), RELAY_ROWS)

    def stage1(c, carry):
        rows = rows_of(c)
        own_add = total_add[rows, :]
        own_min = total_min[rows, :]

        @pl.when(pos == 0)
        def _():
            box1_out[c, 0] = own_add
            box1_out[c, 1] = own_min

        @pl.when(pos > 0)
        def _():
            copy1(c).wait_recv()
            got_add = box1_in[c, 0]
            got_min = box1_in[c, 1]
            before[0, rows, :] = got_add
            before[1, rows, :] = got_min
            new_add = got_add + own_add
            new_min = jnp.minimum(got_min + own_add, own_min)

            @pl.when(pos < last)
            def _():
                box1_out[c, 0] = new_add
                box1_out[c, 1] = new_min

            @pl.when(is_end)
            def _():
                line_total[0, rows, :] = new_add
                line_total[1, rows, :] = new_min

        @pl.when((pos == 0) & is_end)
        def _():
            line_total[0, rows, :] = own_add
            line_total[1, rows, :] = own_min

        @pl.when(pos < last)
        def _():
            copy1(c).start()

        return carry

    lax.fori_loop(0, chunks, stage1, 0)

    def stage2(c, carry):
        rows = rows_of(c)

        @pl.when(is_end & first_col)
        def _():
            incoming[rows, :] = jnp.where(pos > 0, before[1, rows, :], jnp.inf)
            box2_out[c] = line_total[1, rows, :]

        @pl.when(is_end & jnp.logical_not(first_col))
        def _():
            copy2(c).wait_recv()
            value = box2_in[c]
            incoming[rows, :] = jnp.where(
                pos > 0, jnp.minimum(value + before[0, rows, :], before[1, rows, :]), value)
            box2_out[c] = jnp.minimum(value + line_total[0, rows, :], line_total[1, rows, :])

            @pl.when(pos > 0)
            def _():
                copy3_from_end(c, 0, at(col, 0)).start()

            @pl.when(half < last)
            def _():
                copy3_from_end(c, 1, at(col, last - 1)).start()

        @pl.when(is_end & (col < lines - 1))
        def _():
            copy2(c).start()

        return carry

    lax.fori_loop(0, chunks, stage2, 0)

    def stage3(c, carry):
        rows = rows_of(c)

        @pl.when(first_col & jnp.logical_not(is_end))
        def _():
            incoming[rows, :] = jnp.where(pos > 0, before[1, rows, :], jnp.inf)

        @pl.when(jnp.logical_not(first_col) & (in_up | in_down))
        def _():
            copy3_relay(c, at(col, 0)).wait_recv()
            value = box3_in[c]
            incoming[rows, :] = jnp.where(
                pos > 0, jnp.minimum(value + before[0, rows, :], before[1, rows, :]), value)

            @pl.when(in_up & up_next)
            def _():
                copy3_relay(c, at(col, pos + 1)).start()

            @pl.when(in_down & down_next)
            def _():
                copy3_relay(c, at(col, pos - 1)).start()

        return carry

    lax.fori_loop(0, chunks, stage3, 0)

    def drain(c, carry):
        @pl.when(pos < last)
        def _():
            copy1(c).wait_send()

        @pl.when(is_end & (col < lines - 1))
        def _():
            copy2(c).wait_send()

        @pl.when(is_end & jnp.logical_not(first_col) & (pos > 0))
        def _():
            copy3_from_end(c, 0, at(col, 0)).wait_send()

        @pl.when(is_end & jnp.logical_not(first_col) & (half < last))
        def _():
            copy3_from_end(c, 1, at(col, last - 1)).wait_send()

        @pl.when(jnp.logical_not(first_col) & ((in_up & up_next) | (in_down & down_next)))
        def _():
            copy3_relay(c, at(col, 0)).wait_send()

        return carry

    lax.fori_loop(0, chunks, drain, 0)


def relay(total_add, total_min, slabs):
    cells_y, cells_z = total_add.shape
    chunks = cells_y // RELAY_ROWS
    line = LINE if slabs % LINE == 0 else slabs
    vmem = pl.BlockSpec(memory_space=pltpu.VMEM)
    box = pltpu.VMEM((chunks, RELAY_ROWS, cells_z), jnp.float32)
    pair_box = pltpu.VMEM((chunks, 2, RELAY_ROWS, cells_z), jnp.float32)
    return pl.pallas_call(
        functools.partial(relay_kernel, line=line),
        out_shape=jax.ShapeDtypeStruct(total_add.shape, jnp.float32),
        in_specs=[vmem, vmem],
        out_specs=vmem,
        scratch_shapes=[
            pltpu.VMEM((2, cells_y, cells_z), jnp.float32),
            pltpu.VMEM((2, cells_y, cells_z), jnp.float32),
            pair_box,
            pair_box,
            box,
            box,
            box,
            pltpu.SemaphoreType.DMA((chunks,)),
            pltpu.SemaphoreType.DMA((chunks,)),
            pltpu.SemaphoreType.DMA((chunks,)),
            pltpu.SemaphoreType.DMA((chunks,)),
            pltpu.SemaphoreType.DMA((chunks, 2)),
            pltpu.SemaphoreType.DMA((chunks,)),
        ],
        compiler_params=pltpu.CompilerParams(collective_id=0, has_side_effects=True),
    )(total_add, total_min)


def shards(previous, fibre_tensor, tissue, stim_sites, stim_times):
    planes, cells_y, cells_z = previous.shape
    slabs = lax.axis_size("slab")
    orders = lax.axis_size("order")
    slab_index = lax.axis_index("slab")
    group_index = lax.axis_index("order")
    grid_step = 2.0 / (planes * slabs)

    plane_index = stim_sites // (cells_y * cells_z) - slab_index * planes
    inside = (plane_index >= 0) & (plane_index < planes)
    plane_index = jnp.where(inside, plane_index, planes)
    row_index = stim_sites // cells_z % cells_y
    column_index = stim_sites % cells_z
    seeded = previous.at[plane_index, row_index, column_index].min(stim_times, mode="drop")

    bits = jnp.stack([group_index % 2, group_index // 2 % 2, group_index // 4 % 2]).astype(jnp.int32)
    cost_x, field = local_sweeps(bits, fibre_tensor, tissue, seeded, grid_step)

    up_add = jnp.stack([cost_x[0], cost_x[0] + cost_x[1]])
    up_min = jnp.stack([field[0], jnp.minimum(field[0] + cost_x[1], field[1])])
    down_add = jnp.stack([cost_x[1] + cost_x[0], cost_x[1]])
    down_min = jnp.stack([jnp.minimum(field[1] + cost_x[0], field[0]), field[1]])

    backward_x = group_index % 2 == 1
    line_add = jnp.where(backward_x, down_add, up_add)
    line_min = jnp.where(backward_x, down_min, up_min)

    core = group_index % 2
    own_plane = lax.dynamic_index_in_dim(field, core, 0, keepdims=False)
    for mask in [m for m in (2, 4, 8, 16) if m < orders]:
        got = lax.ppermute(own_plane, "order", [(g, g ^ mask) for g in range(orders)])
        own_plane = jnp.minimum(own_plane, got)
    other_plane = lax.ppermute(own_plane, "order", [(g, g ^ 1) for g in range(orders)])
    least0 = jnp.where(core == 0, own_plane, other_plane)
    least1 = jnp.where(core == 0, other_plane, own_plane)
    least_local = jnp.stack([
        jnp.minimum(least0, least1 + cost_x[0]),
        jnp.minimum(least1, least0 + cost_x[1]),
    ])

    total_add = jnp.where(backward_x, line_add[0], line_add[planes - 1])
    total_min = jnp.where(backward_x, line_min[0], line_min[planes - 1])

    incoming = relay(total_add, total_min, slabs)

    sweep_field = jnp.minimum(incoming[None] + line_add, line_min)

    least_in = incoming
    for mask in [m for m in (2, 4, 8, 16) if m < orders]:
        got = lax.ppermute(least_in, "order", [(g, g ^ mask) for g in range(orders)])
        least_in = jnp.minimum(least_in, got)
    other_in = lax.ppermute(least_in, "order", [(g, g ^ 1) for g in range(orders)])
    up_in = jnp.where(core == 0, least_in, other_in)
    down_in = jnp.where(core == 0, other_in, least_in)
    merged = jnp.minimum(
        least_local,
        jnp.minimum(up_in[None] + up_add, down_in[None] + down_add),
    )
    return (merged, sweep_field[None])


def solution(mesh):
    placed = (P("slab", None, None), P(None, "slab", None, None), P("slab", None, None), P(), P())
    return jax.shard_map(
        shards,
        mesh=mesh,
        in_specs=placed,
        out_specs=(P("slab", None, None), P("order", "slab", None, None)),
        check_vma=False,
    )
```

```python
import functools

import jax
import jax.numpy as jnp
from jax import lax
from jax.experimental import pallas as pl
from jax.experimental.pallas import tpu as pltpu
from jax.sharding import PartitionSpec as P

ROWS = 8
CHUNK = 32


def scan_step(a, m, k, axis, reverse, last):
    n = a.shape[axis]
    index = lax.broadcasted_iota(jnp.int32, a.shape, axis)
    shift = n - k if reverse else k
    valid = index < n - k if reverse else index >= k
    a_src = pltpu.roll(a, shift, axis)
    m_src = pltpu.roll(m, shift, axis)
    m = jnp.where(valid, jnp.minimum(m_src + a, m), m)
    if not last:
        a = jnp.where(valid, a_src + a, a)
    return a, m


def block_scan(a, m, axis, reverse, need_sum):
    n = a.shape[axis]
    k = 1
    while k < n:
        a, m = scan_step(a, m, k, axis, reverse, last=(2 * k >= n) and not need_sum)
        k *= 2
    return a, m


def local_kernel(flags, stims, stim_times, fibre, tissue, previous, cost_x, field, totals, own,
                 cost_y, *, grid_step):
    planes, cells_y, cells_z = previous.shape
    chunks = cells_y // CHUNK
    inf = jnp.float32(jnp.inf)

    field[...] = previous[...]

    def seed(k, carry):
        p = stims[0, k]
        r = stims[1, k]
        c = stims[2, k]

        @pl.when((p >= 0) & (p < planes))
        def _():
            base = pl.multiple_of(r // ROWS * ROWS, ROWS)
            block = field[p, pl.ds(base, ROWS), :]
            row = lax.broadcasted_iota(jnp.int32, block.shape, 0)
            lane = lax.broadcasted_iota(jnp.int32, block.shape, 1)
            hit = (row == r - base) & (lane == c)
            field[p, pl.ds(base, ROWS), :] = jnp.where(hit, jnp.minimum(block, stim_times[k]), block)

        return carry

    lax.fori_loop(0, stims.shape[1], seed, 0)

    def costs_and_z(reverse):
        def body(i, carry):
            p = i // chunks
            rows = pl.ds(pl.multiple_of((i % chunks) * CHUNK, CHUNK), CHUNK)
            xx = fibre[0, p, rows, :]
            yy = fibre[1, p, rows, :]
            zz = fibre[2, p, rows, :]
            xy = fibre[3, p, rows, :]
            xz = fibre[4, p, rows, :]
            yz = fibre[5, p, rows, :]
            cx = yy * zz - yz * yz
            cy = xx * zz - xz * xz
            cz = xx * yy - xy * xy
            det = xx * cx - xy * (xy * zz - yz * xz) + xz * (xy * yz - yy * xz)
            factor = jnp.where(tissue[p, rows, :] == 1, 1.0, 4.0).astype(jnp.float32) * grid_step
            cost_x[p, rows, :] = jnp.sqrt(cx / det) * factor
            cost_y[p, rows, :] = jnp.sqrt(cy / det) * factor
            step_z = jnp.sqrt(cz / det) * factor
            _, u = block_scan(step_z, field[p, rows, :], 1, reverse, False)
            field[p, rows, :] = u
            return carry

        lax.fori_loop(0, planes * chunks, body, 0)

    def sweep_y(reverse):
        def body(j, carry):
            i = chunks - 1 - j if reverse else j
            rows = pl.ds(pl.multiple_of(i * CHUNK, CHUNK), CHUNK)
            out = []
            for p in range(planes):
                a, m = block_scan(cost_y[p, rows, :], field[p, rows, :], 0, reverse, True)
                u = jnp.minimum(carry[p] + a, m)
                field[p, rows, :] = u
                edge = u[0:1, :] if reverse else u[CHUNK - 1:CHUNK, :]
                out.append(jnp.broadcast_to(edge, u.shape))
            return tuple(out)

        start = tuple(jnp.full((CHUNK, cells_z), inf, jnp.float32) for _ in range(planes))
        lax.fori_loop(0, chunks, body, start)

    for flag, fn in ((flags[2], costs_and_z), (flags[1], sweep_y)):
        pl.when(flag == 1)(functools.partial(fn, True))
        pl.when(flag != 1)(functools.partial(fn, False))

    def edge(i, carry):
        rows = pl.ds(pl.multiple_of(i * CHUNK, CHUNK), CHUNK)
        c0 = cost_x[0, rows, :]
        c1 = cost_x[1, rows, :]
        u0 = field[0, rows, :]
        u1 = field[1, rows, :]
        down = flags[0] == 1
        totals[0, rows, :] = jnp.where(down, c1 + c0, c0 + c1)
        totals[1, rows, :] = jnp.where(down, jnp.minimum(u1 + c0, u0), jnp.minimum(u0 + c1, u1))
        own[rows, :] = jnp.where(down, u1, u0)
        return carry

    lax.fori_loop(0, chunks, edge, 0)


def local_sweeps(flags, stims, stim_times, fibre, tissue, previous, grid_step):
    planes, cells_y, cells_z = previous.shape
    field = jax.ShapeDtypeStruct(previous.shape, jnp.float32)
    totals = jax.ShapeDtypeStruct((2, cells_y, cells_z), jnp.float32)
    own = jax.ShapeDtypeStruct((cells_y, cells_z), jnp.float32)
    vmem = pl.BlockSpec(memory_space=pltpu.VMEM)
    smem = pl.BlockSpec(memory_space=pltpu.SMEM)
    elements = planes * cells_y * cells_z
    return pl.pallas_call(
        functools.partial(local_kernel, grid_step=grid_step),
        out_shape=(field, field, totals, own),
        in_specs=[smem, smem, smem, vmem, vmem, vmem],
        out_specs=(vmem, vmem, vmem, vmem),
        scratch_shapes=[pltpu.VMEM(previous.shape, jnp.float32)],
        compiler_params=pltpu.CompilerParams(vmem_limit_bytes=48 * 1024 * 1024),
        cost_estimate=pl.CostEstimate(
            flops=300 * elements, transcendentals=6 * elements, bytes_accessed=40 * elements
        ),
    )(flags, stims, stim_times, fibre, tissue, previous)


RELAY_ROWS = 16
LINE = 8


def relay_kernel(total_add, total_min, incoming, before, line_total, box1_in, box1_out, box2_in,
                 box2_out, box3_in, send1, recv1, send2, recv2, send3, recv3, *, line):
    cells_y, cells_z = incoming.shape
    chunks = cells_y // RELAY_ROWS
    slabs = lax.axis_size("slab")
    lines = slabs // line
    half = line // 2
    slab = lax.axis_index("slab")
    group = lax.axis_index("order")
    odd = group % 2
    rank = slab + odd * (slabs - 1 - 2 * slab)
    col = rank // line
    pos = rank % line
    last = line - 1
    mesh_id = pl.DeviceIdType.MESH

    def device(r):
        return (group, r + odd * (slabs - 1 - 2 * r))

    def at(c, p):
        return device(c * line + p)

    first_col = col == 0
    is_end = pos == last
    in_up = pos < half
    in_down = (pos >= half) & (pos < last)
    up_next = pos + 1 < half
    down_next = pos > half

    barrier = pltpu.get_barrier_semaphore()
    neighbours = []
    neighbours.append((pos > 0, at(col, pos - 1)))
    neighbours.append((pos < last, at(col, pos + 1)))
    neighbours.append(((pos == 0) & (col > 0) & (last > 0), at(col, last)))
    neighbours.append((is_end & (col > 0) & (last > 0), at(col, 0)))
    neighbours.append((is_end & (col > 0), at(col - 1, last)))
    neighbours.append((is_end & (col < lines - 1), at(col + 1, last)))
    count = jnp.int32(0)
    for cond, dev in neighbours:
        @pl.when(cond)
        def _():
            pl.semaphore_signal(barrier, 1, device_id=dev, device_id_type=mesh_id)

        count = count + cond.astype(jnp.int32)
    pl.semaphore_wait(barrier, count)

    def copy1(c):
        return pltpu.make_async_remote_copy(box1_out.at[c], box1_in.at[c], send1.at[c], recv1.at[c],
                                            device_id=at(col, pos + 1), device_id_type=mesh_id)

    def copy2(c):
        return pltpu.make_async_remote_copy(box2_out.at[c], box2_in.at[c], send2.at[c], recv2.at[c],
                                            device_id=at(col + 1, last), device_id_type=mesh_id)

    def copy3_from_end(c, k, target):
        return pltpu.make_async_remote_copy(box2_in.at[c], box3_in.at[c], send3.at[c, k], recv3.at[c],
                                            device_id=target, device_id_type=mesh_id)

    def copy3_relay(c, target):
        return pltpu.make_async_remote_copy(box3_in.at[c], box3_in.at[c], send3.at[c, 0], recv3.at[c],
                                            device_id=target, device_id_type=mesh_id)

    def rows_of(c):
        return pl.ds(pl.multiple_of(c * RELAY_ROWS, RELAY_ROWS), RELAY_ROWS)

    def stage1(c, carry):
        rows = rows_of(c)
        own_add = total_add[rows, :]
        own_min = total_min[rows, :]

        @pl.when(pos == 0)
        def _():
            box1_out[c, 0] = own_add
            box1_out[c, 1] = own_min

        @pl.when(pos > 0)
        def _():
            copy1(c).wait_recv()
            got_add = box1_in[c, 0]
            got_min = box1_in[c, 1]
            before[0, rows, :] = got_add
            before[1, rows, :] = got_min
            new_add = got_add + own_add
            new_min = jnp.minimum(got_min + own_add, own_min)

            @pl.when(pos < last)
            def _():
                box1_out[c, 0] = new_add
                box1_out[c, 1] = new_min

            @pl.when(is_end)
            def _():
                line_total[0, rows, :] = new_add
                line_total[1, rows, :] = new_min

        @pl.when((pos == 0) & is_end)
        def _():
            line_total[0, rows, :] = own_add
            line_total[1, rows, :] = own_min

        @pl.when(pos < last)
        def _():
            copy1(c).start()

        return carry

    lax.fori_loop(0, chunks, stage1, 0)

    def stage2(c, carry):
        rows = rows_of(c)

        @pl.when(is_end & first_col)
        def _():
            incoming[rows, :] = jnp.where(pos > 0, before[1, rows, :], jnp.inf)
            box2_out[c] = line_total[1, rows, :]

        @pl.when(is_end & jnp.logical_not(first_col))
        def _():
            copy2(c).wait_recv()
            value = box2_in[c]
            incoming[rows, :] = jnp.where(
                pos > 0, jnp.minimum(value + before[0, rows, :], before[1, rows, :]), value)
            box2_out[c] = jnp.minimum(value + line_total[0, rows, :], line_total[1, rows, :])

            @pl.when(pos > 0)
            def _():
                copy3_from_end(c, 0, at(col, 0)).start()

            @pl.when(half < last)
            def _():
                copy3_from_end(c, 1, at(col, last - 1)).start()

        @pl.when(is_end & (col < lines - 1))
        def _():
            copy2(c).start()

        return carry

    lax.fori_loop(0, chunks, stage2, 0)

    def stage3(c, carry):
        rows = rows_of(c)

        @pl.when(first_col & jnp.logical_not(is_end))
        def _():
            incoming[rows, :] = jnp.where(pos > 0, before[1, rows, :], jnp.inf)

        @pl.when(jnp.logical_not(first_col) & (in_up | in_down))
        def _():
            copy3_relay(c, at(col, 0)).wait_recv()
            value = box3_in[c]
            incoming[rows, :] = jnp.where(
                pos > 0, jnp.minimum(value + before[0, rows, :], before[1, rows, :]), value)

            @pl.when(in_up & up_next)
            def _():
                copy3_relay(c, at(col, pos + 1)).start()

            @pl.when(in_down & down_next)
            def _():
                copy3_relay(c, at(col, pos - 1)).start()

        return carry

    lax.fori_loop(0, chunks, stage3, 0)

    def drain(c, carry):
        @pl.when(pos < last)
        def _():
            copy1(c).wait_send()

        @pl.when(is_end & (col < lines - 1))
        def _():
            copy2(c).wait_send()

        @pl.when(is_end & jnp.logical_not(first_col) & (pos > 0))
        def _():
            copy3_from_end(c, 0, at(col, 0)).wait_send()

        @pl.when(is_end & jnp.logical_not(first_col) & (half < last))
        def _():
            copy3_from_end(c, 1, at(col, last - 1)).wait_send()

        @pl.when(jnp.logical_not(first_col) & ((in_up & up_next) | (in_down & down_next)))
        def _():
            copy3_relay(c, at(col, 0)).wait_send()

        return carry

    lax.fori_loop(0, chunks, drain, 0)


def relay(total_add, total_min, slabs):
    cells_y, cells_z = total_add.shape
    chunks = cells_y // RELAY_ROWS
    line = LINE if slabs % LINE == 0 else slabs
    vmem = pl.BlockSpec(memory_space=pltpu.VMEM)
    box = pltpu.VMEM((chunks, RELAY_ROWS, cells_z), jnp.float32)
    pair_box = pltpu.VMEM((chunks, 2, RELAY_ROWS, cells_z), jnp.float32)
    return pl.pallas_call(
        functools.partial(relay_kernel, line=line),
        out_shape=jax.ShapeDtypeStruct(total_add.shape, jnp.float32),
        in_specs=[vmem, vmem],
        out_specs=vmem,
        scratch_shapes=[
            pltpu.VMEM((2, cells_y, cells_z), jnp.float32),
            pltpu.VMEM((2, cells_y, cells_z), jnp.float32),
            pair_box,
            pair_box,
            box,
            box,
            box,
            pltpu.SemaphoreType.DMA((chunks,)),
            pltpu.SemaphoreType.DMA((chunks,)),
            pltpu.SemaphoreType.DMA((chunks,)),
            pltpu.SemaphoreType.DMA((chunks,)),
            pltpu.SemaphoreType.DMA((chunks, 2)),
            pltpu.SemaphoreType.DMA((chunks,)),
        ],
        compiler_params=pltpu.CompilerParams(collective_id=0, has_side_effects=True),
    )(total_add, total_min)


def shards(previous, fibre_tensor, tissue, stim_sites, stim_times):
    planes, cells_y, cells_z = previous.shape
    slabs = lax.axis_size("slab")
    orders = lax.axis_size("order")
    slab_index = lax.axis_index("slab")
    group_index = lax.axis_index("order")
    grid_step = 2.0 / (planes * slabs)

    plane_index = stim_sites // (cells_y * cells_z) - slab_index * planes
    row_index = stim_sites // cells_z % cells_y
    column_index = stim_sites % cells_z
    stims = jnp.stack([plane_index, row_index, column_index]).astype(jnp.int32)

    bits = jnp.stack([group_index % 2, group_index // 2 % 2, group_index // 4 % 2]).astype(jnp.int32)
    cost_x, field, totals, own_plane = local_sweeps(
        bits, stims, stim_times, fibre_tensor, tissue, previous, grid_step)

    partners = [m for m in range(2, orders, 2)]
    core = group_index % 2
    gathered = [lax.ppermute(own_plane, "order", [(g, g ^ m) for g in range(orders)]) for m in partners]

    incoming = relay(totals[0], totals[1], slabs)

    least_plane = own_plane
    for got in gathered:
        least_plane = jnp.minimum(least_plane, got)
    least_in = incoming
    for m in partners:
        least_in = jnp.minimum(least_in, lax.ppermute(incoming, "order", [(g, g ^ m) for g in range(orders)]))
    other = lax.ppermute(jnp.stack([least_plane, least_in]), "order", [(g, g ^ 1) for g in range(orders)])

    least0 = jnp.where(core == 0, least_plane, other[0])
    least1 = jnp.where(core == 0, other[0], least_plane)
    up_in = jnp.where(core == 0, least_in, other[1])
    down_in = jnp.where(core == 0, other[1], least_in)

    up_add = jnp.stack([cost_x[0], cost_x[0] + cost_x[1]])
    up_min = jnp.stack([field[0], jnp.minimum(field[0] + cost_x[1], field[1])])
    down_add = jnp.stack([cost_x[1] + cost_x[0], cost_x[1]])
    down_min = jnp.stack([jnp.minimum(field[1] + cost_x[0], field[0]), field[1]])
    backward_x = core == 1
    line_add = jnp.where(backward_x, down_add, up_add)
    line_min = jnp.where(backward_x, down_min, up_min)
    sweep_field = jnp.minimum(incoming[None] + line_add, line_min)

    least_local = jnp.stack([
        jnp.minimum(least0, least1 + cost_x[0]),
        jnp.minimum(least1, least0 + cost_x[1]),
    ])
    merged = jnp.minimum(
        least_local,
        jnp.minimum(up_in[None] + up_add, down_in[None] + down_add),
    )
    return (merged, sweep_field[None])


def solution(mesh):
    placed = (P("slab", None, None), P(None, "slab", None, None), P("slab", None, None), P(), P())
    return jax.shard_map(
        shards,
        mesh=mesh,
        in_specs=placed,
        out_specs=(P("slab", None, None), P("order", "slab", None, None)),
        check_vma=False,
    )
```

```python
import functools

import jax
import jax.numpy as jnp
from jax import lax
from jax.experimental import pallas as pl
from jax.experimental.pallas import tpu as pltpu
from jax.sharding import PartitionSpec as P

ROWS = 8
CHUNK = 32


def scan_step(a, m, k, axis, reverse, last):
    n = a.shape[axis]
    index = lax.broadcasted_iota(jnp.int32, a.shape, axis)
    shift = n - k if reverse else k
    valid = index < n - k if reverse else index >= k
    a_src = pltpu.roll(a, shift, axis)
    m_src = pltpu.roll(m, shift, axis)
    m = jnp.where(valid, jnp.minimum(m_src + a, m), m)
    if not last:
        a = jnp.where(valid, a_src + a, a)
    return a, m


def block_scan(a, m, axis, reverse, need_sum):
    n = a.shape[axis]
    k = 1
    while k < n:
        a, m = scan_step(a, m, k, axis, reverse, last=(2 * k >= n) and not need_sum)
        k *= 2
    return a, m


def local_kernel(flags, stims, stim_times, fibre, tissue, previous, cost_x, field, totals, own,
                 cost_y, *, grid_step):
    planes, cells_y, cells_z = previous.shape
    chunks = cells_y // CHUNK
    inf = jnp.float32(jnp.inf)

    field[...] = previous[...]

    def seed(k, carry):
        p = stims[0, k]
        r = stims[1, k]
        c = stims[2, k]

        @pl.when((p >= 0) & (p < planes))
        def _():
            base = pl.multiple_of(r // ROWS * ROWS, ROWS)
            block = field[p, pl.ds(base, ROWS), :]
            row = lax.broadcasted_iota(jnp.int32, block.shape, 0)
            lane = lax.broadcasted_iota(jnp.int32, block.shape, 1)
            hit = (row == r - base) & (lane == c)
            field[p, pl.ds(base, ROWS), :] = jnp.where(hit, jnp.minimum(block, stim_times[k]), block)

        return carry

    lax.fori_loop(0, stims.shape[1], seed, 0)

    def costs_and_z(reverse):
        def body(i, carry):
            p = i // chunks
            rows = pl.ds(pl.multiple_of((i % chunks) * CHUNK, CHUNK), CHUNK)
            xx = fibre[0, p, rows, :]
            yy = fibre[1, p, rows, :]
            zz = fibre[2, p, rows, :]
            xy = fibre[3, p, rows, :]
            xz = fibre[4, p, rows, :]
            yz = fibre[5, p, rows, :]
            cx = yy * zz - yz * yz
            cy = xx * zz - xz * xz
            cz = xx * yy - xy * xy
            det = xx * cx - xy * (xy * zz - yz * xz) + xz * (xy * yz - yy * xz)
            factor = jnp.where(tissue[p, rows, :] == 1, 1.0, 4.0).astype(jnp.float32) * grid_step
            cost_x[p, rows, :] = jnp.sqrt(cx / det) * factor
            cost_y[p, rows, :] = jnp.sqrt(cy / det) * factor
            step_z = jnp.sqrt(cz / det) * factor
            _, u = block_scan(step_z, field[p, rows, :], 1, reverse, False)
            field[p, rows, :] = u
            return carry

        lax.fori_loop(0, planes * chunks, body, 0)

    def sweep_y(reverse):
        def body(j, carry):
            i = chunks - 1 - j if reverse else j
            rows = pl.ds(pl.multiple_of(i * CHUNK, CHUNK), CHUNK)
            out = []
            for p in range(planes):
                a, m = block_scan(cost_y[p, rows, :], field[p, rows, :], 0, reverse, True)
                u = jnp.minimum(carry[p] + a, m)
                field[p, rows, :] = u
                edge = u[0:1, :] if reverse else u[CHUNK - 1:CHUNK, :]
                out.append(jnp.broadcast_to(edge, u.shape))
            return tuple(out)

        start = tuple(jnp.full((CHUNK, cells_z), inf, jnp.float32) for _ in range(planes))
        lax.fori_loop(0, chunks, body, start)

    for flag, fn in ((flags[2], costs_and_z), (flags[1], sweep_y)):
        pl.when(flag == 1)(functools.partial(fn, True))
        pl.when(flag != 1)(functools.partial(fn, False))

    def edge(i, carry):
        rows = pl.ds(pl.multiple_of(i * CHUNK, CHUNK), CHUNK)
        c0 = cost_x[0, rows, :]
        c1 = cost_x[1, rows, :]
        u0 = field[0, rows, :]
        u1 = field[1, rows, :]
        down = flags[0] == 1
        totals[0, rows, :] = jnp.where(down, c1 + c0, c0 + c1)
        totals[1, rows, :] = jnp.where(down, jnp.minimum(u1 + c0, u0), jnp.minimum(u0 + c1, u1))
        own[rows, :] = jnp.where(down, u1, u0)
        return carry

    lax.fori_loop(0, chunks, edge, 0)


def local_sweeps(flags, stims, stim_times, fibre, tissue, previous, grid_step):
    planes, cells_y, cells_z = previous.shape
    field = jax.ShapeDtypeStruct(previous.shape, jnp.float32)
    totals = jax.ShapeDtypeStruct((2, cells_y, cells_z), jnp.float32)
    own = jax.ShapeDtypeStruct((cells_y, cells_z), jnp.float32)
    vmem = pl.BlockSpec(memory_space=pltpu.VMEM)
    smem = pl.BlockSpec(memory_space=pltpu.SMEM)
    elements = planes * cells_y * cells_z
    return pl.pallas_call(
        functools.partial(local_kernel, grid_step=grid_step),
        out_shape=(field, field, totals, own),
        in_specs=[smem, smem, smem, vmem, vmem, vmem],
        out_specs=(vmem, vmem, vmem, vmem),
        scratch_shapes=[pltpu.VMEM(previous.shape, jnp.float32)],
        compiler_params=pltpu.CompilerParams(vmem_limit_bytes=48 * 1024 * 1024),
        cost_estimate=pl.CostEstimate(
            flops=300 * elements, transcendentals=6 * elements, bytes_accessed=40 * elements
        ),
    )(flags, stims, stim_times, fibre, tissue, previous)


RELAY_ROWS = 16
LINE = 8


def relay_kernel(total_add, total_min, incoming, before, line_total, box1_in, box1_out, box2_in,
                 box2_out, box3_in, send1, recv1, send2, recv2, send3, recv3, *, line):
    cells_y, cells_z = incoming.shape
    chunks = cells_y // RELAY_ROWS
    slabs = lax.axis_size("slab")
    lines = slabs // line
    half = line // 2
    slab = lax.axis_index("slab")
    group = lax.axis_index("order")
    odd = group % 2
    rank = slab + odd * (slabs - 1 - 2 * slab)
    col = rank // line
    pos = rank % line
    last = line - 1
    mesh_id = pl.DeviceIdType.MESH

    def device(r):
        return (group, r + odd * (slabs - 1 - 2 * r))

    def at(c, p):
        return device(c * line + p)

    first_col = col == 0
    is_end = pos == last
    in_up = pos < half
    in_down = (pos >= half) & (pos < last)
    up_next = pos + 1 < half
    down_next = pos > half

    barrier = pltpu.get_barrier_semaphore()
    neighbours = []
    neighbours.append((pos > 0, at(col, pos - 1)))
    neighbours.append((pos < last, at(col, pos + 1)))
    neighbours.append(((pos == 0) & (col > 0) & (last > 0), at(col, last)))
    neighbours.append((is_end & (col > 0) & (last > 0), at(col, 0)))
    neighbours.append((is_end & (col > 0), at(col - 1, last)))
    neighbours.append((is_end & (col < lines - 1), at(col + 1, last)))
    count = jnp.int32(0)
    for cond, dev in neighbours:
        @pl.when(cond)
        def _():
            pl.semaphore_signal(barrier, 1, device_id=dev, device_id_type=mesh_id)

        count = count + cond.astype(jnp.int32)
    pl.semaphore_wait(barrier, count)

    def copy1(c):
        return pltpu.make_async_remote_copy(box1_out.at[c], box1_in.at[c], send1.at[c], recv1.at[c],
                                            device_id=at(col, pos + 1), device_id_type=mesh_id)

    def copy2(c):
        return pltpu.make_async_remote_copy(box2_out.at[c], box2_in.at[c], send2.at[c], recv2.at[c],
                                            device_id=at(col + 1, last), device_id_type=mesh_id)

    def copy3_from_end(c, k, target):
        return pltpu.make_async_remote_copy(box2_in.at[c], box3_in.at[c], send3.at[c, k], recv3.at[c],
                                            device_id=target, device_id_type=mesh_id)

    def copy3_relay(c, target):
        return pltpu.make_async_remote_copy(box3_in.at[c], box3_in.at[c], send3.at[c, 0], recv3.at[c],
                                            device_id=target, device_id_type=mesh_id)

    def rows_of(c):
        return pl.ds(pl.multiple_of(c * RELAY_ROWS, RELAY_ROWS), RELAY_ROWS)

    def stage1(c, carry):
        rows = rows_of(c)
        own_add = total_add[rows, :]
        own_min = total_min[rows, :]

        @pl.when(pos == 0)
        def _():
            box1_out[c, 0] = own_add
            box1_out[c, 1] = own_min

        @pl.when(pos > 0)
        def _():
            copy1(c).wait_recv()
            got_add = box1_in[c, 0]
            got_min = box1_in[c, 1]
            before[0, rows, :] = got_add
            before[1, rows, :] = got_min
            new_add = got_add + own_add
            new_min = jnp.minimum(got_min + own_add, own_min)

            @pl.when(pos < last)
            def _():
                box1_out[c, 0] = new_add
                box1_out[c, 1] = new_min

            @pl.when(is_end)
            def _():
                line_total[0, rows, :] = new_add
                line_total[1, rows, :] = new_min

        @pl.when((pos == 0) & is_end)
        def _():
            line_total[0, rows, :] = own_add
            line_total[1, rows, :] = own_min

        @pl.when(pos < last)
        def _():
            copy1(c).start()

        return carry

    def stage2(c, carry):
        rows = rows_of(c)

        @pl.when(is_end & first_col)
        def _():
            incoming[rows, :] = jnp.where(pos > 0, before[1, rows, :], jnp.inf)
            box2_out[c] = line_total[1, rows, :]

        @pl.when(is_end & jnp.logical_not(first_col))
        def _():
            copy2(c).wait_recv()
            value = box2_in[c]
            incoming[rows, :] = jnp.where(
                pos > 0, jnp.minimum(value + before[0, rows, :], before[1, rows, :]), value)
            box2_out[c] = jnp.minimum(value + line_total[0, rows, :], line_total[1, rows, :])

            @pl.when(pos > 0)
            def _():
                copy3_from_end(c, 0, at(col, 0)).start()

            @pl.when(half < last)
            def _():
                copy3_from_end(c, 1, at(col, last - 1)).start()

        @pl.when(is_end & (col < lines - 1))
        def _():
            copy2(c).start()

        return carry

    def stages12(c, carry):
        stage1(c, carry)
        return stage2(c, carry)

    lax.fori_loop(0, chunks, stages12, 0)

    def stage3(c, carry):
        rows = rows_of(c)

        @pl.when(first_col & jnp.logical_not(is_end))
        def _():
            incoming[rows, :] = jnp.where(pos > 0, before[1, rows, :], jnp.inf)

        @pl.when(jnp.logical_not(first_col) & (in_up | in_down))
        def _():
            copy3_relay(c, at(col, 0)).wait_recv()
            value = box3_in[c]
            incoming[rows, :] = jnp.where(
                pos > 0, jnp.minimum(value + before[0, rows, :], before[1, rows, :]), value)

            @pl.when(in_up & up_next)
            def _():
                copy3_relay(c, at(col, pos + 1)).start()

            @pl.when(in_down & down_next)
            def _():
                copy3_relay(c, at(col, pos - 1)).start()

        return carry

    lax.fori_loop(0, chunks, stage3, 0)

    def drain(c, carry):
        @pl.when(pos < last)
        def _():
            copy1(c).wait_send()

        @pl.when(is_end & (col < lines - 1))
        def _():
            copy2(c).wait_send()

        @pl.when(is_end & jnp.logical_not(first_col) & (pos > 0))
        def _():
            copy3_from_end(c, 0, at(col, 0)).wait_send()

        @pl.when(is_end & jnp.logical_not(first_col) & (half < last))
        def _():
            copy3_from_end(c, 1, at(col, last - 1)).wait_send()

        @pl.when(jnp.logical_not(first_col) & ((in_up & up_next) | (in_down & down_next)))
        def _():
            copy3_relay(c, at(col, 0)).wait_send()

        return carry

    lax.fori_loop(0, chunks, drain, 0)


def relay(total_add, total_min, slabs):
    cells_y, cells_z = total_add.shape
    chunks = cells_y // RELAY_ROWS
    line = LINE if slabs % LINE == 0 else slabs
    vmem = pl.BlockSpec(memory_space=pltpu.VMEM)
    box = pltpu.VMEM((chunks, RELAY_ROWS, cells_z), jnp.float32)
    pair_box = pltpu.VMEM((chunks, 2, RELAY_ROWS, cells_z), jnp.float32)
    return pl.pallas_call(
        functools.partial(relay_kernel, line=line),
        out_shape=jax.ShapeDtypeStruct(total_add.shape, jnp.float32),
        in_specs=[vmem, vmem],
        out_specs=vmem,
        scratch_shapes=[
            pltpu.VMEM((2, cells_y, cells_z), jnp.float32),
            pltpu.VMEM((2, cells_y, cells_z), jnp.float32),
            pair_box,
            pair_box,
            box,
            box,
            box,
            pltpu.SemaphoreType.DMA((chunks,)),
            pltpu.SemaphoreType.DMA((chunks,)),
            pltpu.SemaphoreType.DMA((chunks,)),
            pltpu.SemaphoreType.DMA((chunks,)),
            pltpu.SemaphoreType.DMA((chunks, 2)),
            pltpu.SemaphoreType.DMA((chunks,)),
        ],
        compiler_params=pltpu.CompilerParams(collective_id=0, has_side_effects=True),
    )(total_add, total_min)


def shards(previous, fibre_tensor, tissue, stim_sites, stim_times):
    planes, cells_y, cells_z = previous.shape
    slabs = lax.axis_size("slab")
    orders = lax.axis_size("order")
    slab_index = lax.axis_index("slab")
    group_index = lax.axis_index("order")
    grid_step = 2.0 / (planes * slabs)

    plane_index = stim_sites // (cells_y * cells_z) - slab_index * planes
    row_index = stim_sites // cells_z % cells_y
    column_index = stim_sites % cells_z
    stims = jnp.stack([plane_index, row_index, column_index]).astype(jnp.int32)

    bits = jnp.stack([group_index % 2, group_index // 2 % 2, group_index // 4 % 2]).astype(jnp.int32)
    cost_x, field, totals, own_plane = local_sweeps(
        bits, stims, stim_times, fibre_tensor, tissue, previous, grid_step)

    partners = [m for m in range(2, orders, 2)]
    core = group_index % 2
    gathered = [lax.ppermute(own_plane, "order", [(g, g ^ m) for g in range(orders)]) for m in partners]

    incoming = relay(totals[0], totals[1], slabs)

    least_plane = own_plane
    for got in gathered:
        least_plane = jnp.minimum(least_plane, got)
    least_in = incoming
    for m in partners:
        least_in = jnp.minimum(least_in, lax.ppermute(incoming, "order", [(g, g ^ m) for g in range(orders)]))
    other = lax.ppermute(jnp.stack([least_plane, least_in]), "order", [(g, g ^ 1) for g in range(orders)])

    least0 = jnp.where(core == 0, least_plane, other[0])
    least1 = jnp.where(core == 0, other[0], least_plane)
    up_in = jnp.where(core == 0, least_in, other[1])
    down_in = jnp.where(core == 0, other[1], least_in)

    up_add = jnp.stack([cost_x[0], cost_x[0] + cost_x[1]])
    up_min = jnp.stack([field[0], jnp.minimum(field[0] + cost_x[1], field[1])])
    down_add = jnp.stack([cost_x[1] + cost_x[0], cost_x[1]])
    down_min = jnp.stack([jnp.minimum(field[1] + cost_x[0], field[0]), field[1]])
    backward_x = core == 1
    line_add = jnp.where(backward_x, down_add, up_add)
    line_min = jnp.where(backward_x, down_min, up_min)
    sweep_field = jnp.minimum(incoming[None] + line_add, line_min)

    least_local = jnp.stack([
        jnp.minimum(least0, least1 + cost_x[0]),
        jnp.minimum(least1, least0 + cost_x[1]),
    ])
    merged = jnp.minimum(
        least_local,
        jnp.minimum(up_in[None] + up_add, down_in[None] + down_add),
    )
    return (merged, sweep_field[None])


def solution(mesh):
    placed = (P("slab", None, None), P(None, "slab", None, None), P("slab", None, None), P(), P())
    return jax.shard_map(
        shards,
        mesh=mesh,
        in_specs=placed,
        out_specs=(P("slab", None, None), P("order", "slab", None, None)),
        check_vma=False,
    )
```

```python
import functools

import jax
import jax.numpy as jnp
from jax import lax
from jax.experimental import pallas as pl
from jax.experimental.pallas import tpu as pltpu
from jax.sharding import PartitionSpec as P

ROWS = 8
CHUNK = 32


def scan_step(a, m, k, axis, reverse, last):
    n = a.shape[axis]
    index = lax.broadcasted_iota(jnp.int32, a.shape, axis)
    shift = n - k if reverse else k
    valid = index < n - k if reverse else index >= k
    a_src = pltpu.roll(a, shift, axis)
    m_src = pltpu.roll(m, shift, axis)
    m = jnp.where(valid, jnp.minimum(m_src + a, m), m)
    if not last:
        a = jnp.where(valid, a_src + a, a)
    return a, m


def block_scan(a, m, axis, reverse, need_sum):
    n = a.shape[axis]
    k = 1
    while k < n:
        a, m = scan_step(a, m, k, axis, reverse, last=(2 * k >= n) and not need_sum)
        k *= 2
    return a, m


def local_kernel(flags, stims, stim_times, fibre, tissue, previous, cost_x, field, totals, own,
                 cost_y, *, grid_step):
    planes, cells_y, cells_z = previous.shape
    chunks = cells_y // CHUNK
    inf = jnp.float32(jnp.inf)

    field[...] = previous[...]

    def seed(k, carry):
        p = stims[0, k]
        r = stims[1, k]
        c = stims[2, k]

        @pl.when((p >= 0) & (p < planes))
        def _():
            base = pl.multiple_of(r // ROWS * ROWS, ROWS)
            block = field[p, pl.ds(base, ROWS), :]
            row = lax.broadcasted_iota(jnp.int32, block.shape, 0)
            lane = lax.broadcasted_iota(jnp.int32, block.shape, 1)
            hit = (row == r - base) & (lane == c)
            field[p, pl.ds(base, ROWS), :] = jnp.where(hit, jnp.minimum(block, stim_times[k]), block)

        return carry

    lax.fori_loop(0, stims.shape[1], seed, 0)

    def costs_and_z(reverse):
        def body(i, carry):
            p = i // chunks
            rows = pl.ds(pl.multiple_of((i % chunks) * CHUNK, CHUNK), CHUNK)
            xx = fibre[0, p, rows, :]
            yy = fibre[1, p, rows, :]
            zz = fibre[2, p, rows, :]
            xy = fibre[3, p, rows, :]
            xz = fibre[4, p, rows, :]
            yz = fibre[5, p, rows, :]
            cx = yy * zz - yz * yz
            cy = xx * zz - xz * xz
            cz = xx * yy - xy * xy
            det = xx * cx - xy * (xy * zz - yz * xz) + xz * (xy * yz - yy * xz)
            factor = jnp.where(tissue[p, rows, :] == 1, 1.0, 4.0).astype(jnp.float32) * grid_step
            cost_x[p, rows, :] = jnp.sqrt(cx / det) * factor
            cost_y[p, rows, :] = jnp.sqrt(cy / det) * factor
            step_z = jnp.sqrt(cz / det) * factor
            _, u = block_scan(step_z, field[p, rows, :], 1, reverse, False)
            field[p, rows, :] = u
            return carry

        lax.fori_loop(0, planes * chunks, body, 0)

    def sweep_y(reverse):
        def body(j, carry):
            i = chunks - 1 - j if reverse else j
            rows = pl.ds(pl.multiple_of(i * CHUNK, CHUNK), CHUNK)
            out = []
            for p in range(planes):
                a, m = block_scan(cost_y[p, rows, :], field[p, rows, :], 0, reverse, True)
                u = jnp.minimum(carry[p] + a, m)
                field[p, rows, :] = u
                edge = u[0:1, :] if reverse else u[CHUNK - 1:CHUNK, :]
                out.append(jnp.broadcast_to(edge, u.shape))
            return tuple(out)

        start = tuple(jnp.full((CHUNK, cells_z), inf, jnp.float32) for _ in range(planes))
        lax.fori_loop(0, chunks, body, start)

    for flag, fn in ((flags[2], costs_and_z), (flags[1], sweep_y)):
        pl.when(flag == 1)(functools.partial(fn, True))
        pl.when(flag != 1)(functools.partial(fn, False))

    def edge(i, carry):
        rows = pl.ds(pl.multiple_of(i * CHUNK, CHUNK), CHUNK)
        c0 = cost_x[0, rows, :]
        c1 = cost_x[1, rows, :]
        u0 = field[0, rows, :]
        u1 = field[1, rows, :]
        down = flags[0] == 1
        totals[0, rows, :] = jnp.where(down, c1 + c0, c0 + c1)
        totals[1, rows, :] = jnp.where(down, jnp.minimum(u1 + c0, u0), jnp.minimum(u0 + c1, u1))
        own[rows, :] = jnp.where(down, u1, u0)
        return carry

    lax.fori_loop(0, chunks, edge, 0)


def local_sweeps(flags, stims, stim_times, fibre, tissue, previous, grid_step):
    planes, cells_y, cells_z = previous.shape
    field = jax.ShapeDtypeStruct(previous.shape, jnp.float32)
    totals = jax.ShapeDtypeStruct((2, cells_y, cells_z), jnp.float32)
    own = jax.ShapeDtypeStruct((cells_y, cells_z), jnp.float32)
    vmem = pl.BlockSpec(memory_space=pltpu.VMEM)
    smem = pl.BlockSpec(memory_space=pltpu.SMEM)
    elements = planes * cells_y * cells_z
    return pl.pallas_call(
        functools.partial(local_kernel, grid_step=grid_step),
        out_shape=(field, field, totals, own),
        in_specs=[smem, smem, smem, vmem, vmem, vmem],
        out_specs=(vmem, vmem, vmem, vmem),
        scratch_shapes=[pltpu.VMEM(previous.shape, jnp.float32)],
        compiler_params=pltpu.CompilerParams(vmem_limit_bytes=48 * 1024 * 1024),
        cost_estimate=pl.CostEstimate(
            flops=300 * elements, transcendentals=6 * elements, bytes_accessed=40 * elements
        ),
    )(flags, stims, stim_times, fibre, tissue, previous)


RELAY_ROWS = 16
LINE = 8


def flip_bits(value, mask, bits):
    out = 0
    for j in range(bits):
        out = out + (2 ** j) * ((value // 2 ** j + (mask >> j) % 2) % 2)
    return out


def relay_kernel(total_add, total_min, incoming, least_in, before, line_total, box1_in, box1_out,
                 box2_in, box2_out, box3_in, box4, send1, recv1, send2, recv2, send3, recv3, send4,
                 recv4, *, line):
    cells_y, cells_z = incoming.shape
    chunks = cells_y // RELAY_ROWS
    slabs = lax.axis_size("slab")
    lines = slabs // line
    half = line // 2
    slab = lax.axis_index("slab")
    group = lax.axis_index("order")
    odd = group % 2
    rank = slab + odd * (slabs - 1 - 2 * slab)
    col = rank // line
    pos = rank % line
    last = line - 1
    mesh_id = pl.DeviceIdType.MESH

    def device(r):
        return (group, r + odd * (slabs - 1 - 2 * r))

    def at(c, p):
        return device(c * line + p)

    orders = lax.axis_size("order")
    masks = list(range(2, orders, 2))
    order_bits = max(orders - 1, 1).bit_length()
    first_col = col == 0
    is_end = pos == last
    in_up = pos < half
    in_down = (pos >= half) & (pos < last)
    up_next = pos + 1 < half
    down_next = pos > half

    barrier = pltpu.get_barrier_semaphore()
    neighbours = []
    neighbours.append((pos > 0, at(col, pos - 1)))
    neighbours.append((pos < last, at(col, pos + 1)))
    neighbours.append(((pos == 0) & (col > 0) & (last > 0), at(col, last)))
    neighbours.append((is_end & (col > 0) & (last > 0), at(col, 0)))
    neighbours.append((is_end & (col > 0), at(col - 1, last)))
    neighbours.append((is_end & (col < lines - 1), at(col + 1, last)))
    for m in masks:
        neighbours.append((slab >= 0, (flip_bits(group, m, order_bits), slab)))
    count = jnp.int32(0)
    for cond, dev in neighbours:
        @pl.when(cond)
        def _():
            pl.semaphore_signal(barrier, 1, device_id=dev, device_id_type=mesh_id)

        count = count + cond.astype(jnp.int32)
    pl.semaphore_wait(barrier, count)

    def copy1(c):
        return pltpu.make_async_remote_copy(box1_out.at[c], box1_in.at[c], send1.at[c], recv1.at[c],
                                            device_id=at(col, pos + 1), device_id_type=mesh_id)

    def copy2(c):
        return pltpu.make_async_remote_copy(box2_out.at[c], box2_in.at[c], send2.at[c], recv2.at[c],
                                            device_id=at(col + 1, last), device_id_type=mesh_id)

    def copy3_from_end(c, k, target):
        return pltpu.make_async_remote_copy(box2_in.at[c], box3_in.at[c], send3.at[c, k], recv3.at[c],
                                            device_id=target, device_id_type=mesh_id)

    def copy3_relay(c, target):
        return pltpu.make_async_remote_copy(box3_in.at[c], box3_in.at[c], send3.at[c, 0], recv3.at[c],
                                            device_id=target, device_id_type=mesh_id)

    def rows_of(c):
        return pl.ds(pl.multiple_of(c * RELAY_ROWS, RELAY_ROWS), RELAY_ROWS)

    def copy4(c, k):
        return pltpu.make_async_remote_copy(incoming.at[rows_of(c)], box4.at[k, c], send4.at[c, k],
                                            recv4.at[c, k], device_id=(flip_bits(group, masks[k], order_bits), slab),
                                            device_id_type=mesh_id)

    def share(c):
        for k in range(len(masks)):
            copy4(c, k).start()

    def stage1(c, carry):
        rows = rows_of(c)
        own_add = total_add[rows, :]
        own_min = total_min[rows, :]

        @pl.when(pos == 0)
        def _():
            box1_out[c, 0] = own_add
            box1_out[c, 1] = own_min

        @pl.when(pos > 0)
        def _():
            copy1(c).wait_recv()
            got_add = box1_in[c, 0]
            got_min = box1_in[c, 1]
            before[0, rows, :] = got_add
            before[1, rows, :] = got_min
            new_add = got_add + own_add
            new_min = jnp.minimum(got_min + own_add, own_min)

            @pl.when(pos < last)
            def _():
                box1_out[c, 0] = new_add
                box1_out[c, 1] = new_min

            @pl.when(is_end)
            def _():
                line_total[0, rows, :] = new_add
                line_total[1, rows, :] = new_min

        @pl.when((pos == 0) & is_end)
        def _():
            line_total[0, rows, :] = own_add
            line_total[1, rows, :] = own_min

        @pl.when(pos < last)
        def _():
            copy1(c).start()

        return carry

    def stage2(c, carry):
        rows = rows_of(c)

        @pl.when(is_end & first_col)
        def _():
            incoming[rows, :] = jnp.where(pos > 0, before[1, rows, :], jnp.inf)
            share(c)
            box2_out[c] = line_total[1, rows, :]

        @pl.when(is_end & jnp.logical_not(first_col))
        def _():
            copy2(c).wait_recv()
            value = box2_in[c]
            incoming[rows, :] = jnp.where(
                pos > 0, jnp.minimum(value + before[0, rows, :], before[1, rows, :]), value)
            share(c)
            box2_out[c] = jnp.minimum(value + line_total[0, rows, :], line_total[1, rows, :])

            @pl.when(pos > 0)
            def _():
                copy3_from_end(c, 0, at(col, 0)).start()

            @pl.when(half < last)
            def _():
                copy3_from_end(c, 1, at(col, last - 1)).start()

        @pl.when(is_end & (col < lines - 1))
        def _():
            copy2(c).start()

        return carry

    def stages12(c, carry):
        stage1(c, carry)
        return stage2(c, carry)

    lax.fori_loop(0, chunks, stages12, 0)

    def stage3(c, carry):
        rows = rows_of(c)

        @pl.when(first_col & jnp.logical_not(is_end))
        def _():
            incoming[rows, :] = jnp.where(pos > 0, before[1, rows, :], jnp.inf)
            share(c)

        @pl.when(jnp.logical_not(first_col) & (in_up | in_down))
        def _():
            copy3_relay(c, at(col, 0)).wait_recv()
            value = box3_in[c]
            incoming[rows, :] = jnp.where(
                pos > 0, jnp.minimum(value + before[0, rows, :], before[1, rows, :]), value)
            share(c)

            @pl.when(in_up & up_next)
            def _():
                copy3_relay(c, at(col, pos + 1)).start()

            @pl.when(in_down & down_next)
            def _():
                copy3_relay(c, at(col, pos - 1)).start()

        return carry

    lax.fori_loop(0, chunks, stage3, 0)

    def gather(c, carry):
        rows = rows_of(c)
        least = incoming[rows, :]
        for k in range(len(masks)):
            copy4(c, k).wait_recv()
            least = jnp.minimum(least, box4[k, c])
        least_in[rows, :] = least
        return carry

    lax.fori_loop(0, chunks, gather, 0)

    def drain(c, carry):
        @pl.when(pos < last)
        def _():
            copy1(c).wait_send()

        @pl.when(is_end & (col < lines - 1))
        def _():
            copy2(c).wait_send()

        @pl.when(is_end & jnp.logical_not(first_col) & (pos > 0))
        def _():
            copy3_from_end(c, 0, at(col, 0)).wait_send()

        @pl.when(is_end & jnp.logical_not(first_col) & (half < last))
        def _():
            copy3_from_end(c, 1, at(col, last - 1)).wait_send()

        @pl.when(jnp.logical_not(first_col) & ((in_up & up_next) | (in_down & down_next)))
        def _():
            copy3_relay(c, at(col, 0)).wait_send()

        for k in range(len(masks)):
            copy4(c, k).wait_send()
        return carry

    lax.fori_loop(0, chunks, drain, 0)


def relay(total_add, total_min, slabs, orders):
    cells_y, cells_z = total_add.shape
    chunks = cells_y // RELAY_ROWS
    sharers = len(range(2, orders, 2))
    plane = jax.ShapeDtypeStruct(total_add.shape, jnp.float32)
    line = LINE if slabs % LINE == 0 else slabs
    vmem = pl.BlockSpec(memory_space=pltpu.VMEM)
    box = pltpu.VMEM((chunks, RELAY_ROWS, cells_z), jnp.float32)
    pair_box = pltpu.VMEM((chunks, 2, RELAY_ROWS, cells_z), jnp.float32)
    return pl.pallas_call(
        functools.partial(relay_kernel, line=line),
        out_shape=(plane, plane),
        in_specs=[vmem, vmem],
        out_specs=(vmem, vmem),
        scratch_shapes=[
            pltpu.VMEM((2, cells_y, cells_z), jnp.float32),
            pltpu.VMEM((2, cells_y, cells_z), jnp.float32),
            pair_box,
            pair_box,
            box,
            box,
            box,
            pltpu.VMEM((max(sharers, 1), chunks, RELAY_ROWS, cells_z), jnp.float32),
            pltpu.SemaphoreType.DMA((chunks,)),
            pltpu.SemaphoreType.DMA((chunks,)),
            pltpu.SemaphoreType.DMA((chunks,)),
            pltpu.SemaphoreType.DMA((chunks,)),
            pltpu.SemaphoreType.DMA((chunks, 2)),
            pltpu.SemaphoreType.DMA((chunks,)),
            pltpu.SemaphoreType.DMA((chunks, max(sharers, 1))),
            pltpu.SemaphoreType.DMA((chunks, max(sharers, 1))),
        ],
        compiler_params=pltpu.CompilerParams(collective_id=0, has_side_effects=True),
    )(total_add, total_min)


def shards(previous, fibre_tensor, tissue, stim_sites, stim_times):
    planes, cells_y, cells_z = previous.shape
    slabs = lax.axis_size("slab")
    orders = lax.axis_size("order")
    slab_index = lax.axis_index("slab")
    group_index = lax.axis_index("order")
    grid_step = 2.0 / (planes * slabs)

    plane_index = stim_sites // (cells_y * cells_z) - slab_index * planes
    row_index = stim_sites // cells_z % cells_y
    column_index = stim_sites % cells_z
    stims = jnp.stack([plane_index, row_index, column_index]).astype(jnp.int32)

    bits = jnp.stack([group_index % 2, group_index // 2 % 2, group_index // 4 % 2]).astype(jnp.int32)
    cost_x, field, totals, own_plane = local_sweeps(
        bits, stims, stim_times, fibre_tensor, tissue, previous, grid_step)

    partners = [m for m in range(2, orders, 2)]
    core = group_index % 2
    gathered = [lax.ppermute(own_plane, "order", [(g, g ^ m) for g in range(orders)]) for m in partners]

    incoming, least_in = relay(totals[0], totals[1], slabs, orders)

    least_plane = own_plane
    for got in gathered:
        least_plane = jnp.minimum(least_plane, got)
    other = lax.ppermute(jnp.stack([least_plane, least_in]), "order", [(g, g ^ 1) for g in range(orders)])

    least0 = jnp.where(core == 0, least_plane, other[0])
    least1 = jnp.where(core == 0, other[0], least_plane)
    up_in = jnp.where(core == 0, least_in, other[1])
    down_in = jnp.where(core == 0, other[1], least_in)

    up_add = jnp.stack([cost_x[0], cost_x[0] + cost_x[1]])
    up_min = jnp.stack([field[0], jnp.minimum(field[0] + cost_x[1], field[1])])
    down_add = jnp.stack([cost_x[1] + cost_x[0], cost_x[1]])
    down_min = jnp.stack([jnp.minimum(field[1] + cost_x[0], field[0]), field[1]])
    backward_x = core == 1
    line_add = jnp.where(backward_x, down_add, up_add)
    line_min = jnp.where(backward_x, down_min, up_min)
    sweep_field = jnp.minimum(incoming[None] + line_add, line_min)

    least_local = jnp.stack([
        jnp.minimum(least0, least1 + cost_x[0]),
        jnp.minimum(least1, least0 + cost_x[1]),
    ])
    merged = jnp.minimum(
        least_local,
        jnp.minimum(up_in[None] + up_add, down_in[None] + down_add),
    )
    return (merged, sweep_field[None])


def solution(mesh):
    placed = (P("slab", None, None), P(None, "slab", None, None), P("slab", None, None), P(), P())
    return jax.shard_map(
        shards,
        mesh=mesh,
        in_specs=placed,
        out_specs=(P("slab", None, None), P("order", "slab", None, None)),
        check_vma=False,
    )
```

```python
import functools

import jax
import jax.numpy as jnp
from jax import lax
from jax.experimental import pallas as pl
from jax.experimental.pallas import tpu as pltpu
from jax.sharding import PartitionSpec as P

ROWS = 8
CHUNK = 32


def scan_step(a, m, k, axis, reverse, last):
    n = a.shape[axis]
    index = lax.broadcasted_iota(jnp.int32, a.shape, axis)
    shift = n - k if reverse else k
    valid = index < n - k if reverse else index >= k
    a_src = pltpu.roll(a, shift, axis)
    m_src = pltpu.roll(m, shift, axis)
    m = jnp.where(valid, jnp.minimum(m_src + a, m), m)
    if not last:
        a = jnp.where(valid, a_src + a, a)
    return a, m


def block_scan(a, m, axis, reverse, need_sum):
    n = a.shape[axis]
    k = 1
    while k < n:
        a, m = scan_step(a, m, k, axis, reverse, last=(2 * k >= n) and not need_sum)
        k *= 2
    return a, m


def local_kernel(flags, stims, stim_times, fibre, tissue, previous, cost_x, field, totals, own,
                 cost_y, *, grid_step):
    planes, cells_y, cells_z = previous.shape
    chunks = cells_y // CHUNK
    inf = jnp.float32(jnp.inf)

    field[...] = previous[...]

    def seed(k, carry):
        p = stims[0, k]
        r = stims[1, k]
        c = stims[2, k]

        @pl.when((p >= 0) & (p < planes))
        def _():
            base = pl.multiple_of(r // ROWS * ROWS, ROWS)
            block = field[p, pl.ds(base, ROWS), :]
            row = lax.broadcasted_iota(jnp.int32, block.shape, 0)
            lane = lax.broadcasted_iota(jnp.int32, block.shape, 1)
            hit = (row == r - base) & (lane == c)
            field[p, pl.ds(base, ROWS), :] = jnp.where(hit, jnp.minimum(block, stim_times[k]), block)

        return carry

    lax.fori_loop(0, stims.shape[1], seed, 0)

    def costs_and_z(reverse):
        def body(i, carry):
            p = i // chunks
            rows = pl.ds(pl.multiple_of((i % chunks) * CHUNK, CHUNK), CHUNK)
            xx = fibre[0, p, rows, :]
            yy = fibre[1, p, rows, :]
            zz = fibre[2, p, rows, :]
            xy = fibre[3, p, rows, :]
            xz = fibre[4, p, rows, :]
            yz = fibre[5, p, rows, :]
            cx = yy * zz - yz * yz
            cy = xx * zz - xz * xz
            cz = xx * yy - xy * xy
            det = xx * cx - xy * (xy * zz - yz * xz) + xz * (xy * yz - yy * xz)
            factor = jnp.where(tissue[p, rows, :] == 1, 1.0, 4.0).astype(jnp.float32) * grid_step
            inverse = 1.0 / det
            cost_x[p, rows, :] = jnp.sqrt(cx * inverse) * factor
            cost_y[p, rows, :] = jnp.sqrt(cy * inverse) * factor
            step_z = jnp.sqrt(cz * inverse) * factor
            _, u = block_scan(step_z, field[p, rows, :], 1, reverse, False)
            field[p, rows, :] = u
            return carry

        lax.fori_loop(0, planes * chunks, body, 0, unroll=2)

    def sweep_y(reverse):
        def body(j, carry):
            i = chunks - 1 - j if reverse else j
            rows = pl.ds(pl.multiple_of(i * CHUNK, CHUNK), CHUNK)
            out = []
            for p in range(planes):
                a, m = block_scan(cost_y[p, rows, :], field[p, rows, :], 0, reverse, True)
                u = jnp.minimum(carry[p] + a, m)
                field[p, rows, :] = u
                edge = u[0:1, :] if reverse else u[CHUNK - 1:CHUNK, :]
                out.append(jnp.broadcast_to(edge, u.shape))
            return tuple(out)

        start = tuple(jnp.full((CHUNK, cells_z), inf, jnp.float32) for _ in range(planes))
        lax.fori_loop(0, chunks, body, start, unroll=2)

    for flag, fn in ((flags[2], costs_and_z), (flags[1], sweep_y)):
        pl.when(flag == 1)(functools.partial(fn, True))
        pl.when(flag != 1)(functools.partial(fn, False))

    def edge(i, carry):
        rows = pl.ds(pl.multiple_of(i * CHUNK, CHUNK), CHUNK)
        c0 = cost_x[0, rows, :]
        c1 = cost_x[1, rows, :]
        u0 = field[0, rows, :]
        u1 = field[1, rows, :]
        down = flags[0] == 1
        totals[0, rows, :] = jnp.where(down, c1 + c0, c0 + c1)
        totals[1, rows, :] = jnp.where(down, jnp.minimum(u1 + c0, u0), jnp.minimum(u0 + c1, u1))
        own[rows, :] = jnp.where(down, u1, u0)
        return carry

    lax.fori_loop(0, chunks, edge, 0)


def local_sweeps(flags, stims, stim_times, fibre, tissue, previous, grid_step):
    planes, cells_y, cells_z = previous.shape
    field = jax.ShapeDtypeStruct(previous.shape, jnp.float32)
    totals = jax.ShapeDtypeStruct((2, cells_y, cells_z), jnp.float32)
    own = jax.ShapeDtypeStruct((cells_y, cells_z), jnp.float32)
    vmem = pl.BlockSpec(memory_space=pltpu.VMEM)
    smem = pl.BlockSpec(memory_space=pltpu.SMEM)
    elements = planes * cells_y * cells_z
    return pl.pallas_call(
        functools.partial(local_kernel, grid_step=grid_step),
        out_shape=(field, field, totals, own),
        in_specs=[smem, smem, smem, vmem, vmem, vmem],
        out_specs=(vmem, vmem, vmem, vmem),
        scratch_shapes=[pltpu.VMEM(previous.shape, jnp.float32)],
        compiler_params=pltpu.CompilerParams(vmem_limit_bytes=48 * 1024 * 1024),
        cost_estimate=pl.CostEstimate(
            flops=300 * elements, transcendentals=6 * elements, bytes_accessed=40 * elements
        ),
    )(flags, stims, stim_times, fibre, tissue, previous)


RELAY_ROWS = 16
LINE = 8


def flip_bits(value, mask, bits):
    out = 0
    for j in range(bits):
        out = out + (2 ** j) * ((value // 2 ** j + (mask >> j) % 2) % 2)
    return out


def relay_kernel(totals, own, incoming, least_in, least_plane, before, line_total, box1_in,
                 box1_out, box2_in, box2_out, box3_in, box4, box5, send1, recv1, send2, recv2, send3,
                 recv3, send4, recv4, send5, recv5, *, line):
    total_add = totals.at[0]
    total_min = totals.at[1]
    cells_y, cells_z = incoming.shape
    chunks = cells_y // RELAY_ROWS
    slabs = lax.axis_size("slab")
    lines = slabs // line
    half = line // 2
    slab = lax.axis_index("slab")
    group = lax.axis_index("order")
    odd = group % 2
    rank = slab + odd * (slabs - 1 - 2 * slab)
    col = rank // line
    pos = rank % line
    last = line - 1
    mesh_id = pl.DeviceIdType.MESH

    def device(r):
        return (group, r + odd * (slabs - 1 - 2 * r))

    def at(c, p):
        return device(c * line + p)

    orders = lax.axis_size("order")
    masks = list(range(2, orders, 2))
    order_bits = max(orders - 1, 1).bit_length()
    first_col = col == 0
    is_end = pos == last
    in_up = pos < half
    in_down = (pos >= half) & (pos < last)
    up_next = pos + 1 < half
    down_next = pos > half

    barrier = pltpu.get_barrier_semaphore()
    neighbours = []
    neighbours.append((pos > 0, at(col, pos - 1)))
    neighbours.append((pos < last, at(col, pos + 1)))
    neighbours.append(((pos == 0) & (col > 0) & (last > 0), at(col, last)))
    neighbours.append((is_end & (col > 0) & (last > 0), at(col, 0)))
    neighbours.append((is_end & (col > 0), at(col - 1, last)))
    neighbours.append((is_end & (col < lines - 1), at(col + 1, last)))
    for m in masks:
        neighbours.append((slab >= 0, (flip_bits(group, m, order_bits), slab)))
    count = jnp.int32(0)
    for cond, dev in neighbours:
        @pl.when(cond)
        def _():
            pl.semaphore_signal(barrier, 1, device_id=dev, device_id_type=mesh_id)

        count = count + cond.astype(jnp.int32)
    pl.semaphore_wait(barrier, count)

    def copy1(c):
        return pltpu.make_async_remote_copy(box1_out.at[c], box1_in.at[c], send1.at[c], recv1.at[c],
                                            device_id=at(col, pos + 1), device_id_type=mesh_id)

    def copy2(c):
        return pltpu.make_async_remote_copy(box2_out.at[c], box2_in.at[c], send2.at[c], recv2.at[c],
                                            device_id=at(col + 1, last), device_id_type=mesh_id)

    def copy3_from_end(c, k, target):
        return pltpu.make_async_remote_copy(box2_in.at[c], box3_in.at[c], send3.at[c, k], recv3.at[c],
                                            device_id=target, device_id_type=mesh_id)

    def copy3_relay(c, target):
        return pltpu.make_async_remote_copy(box3_in.at[c], box3_in.at[c], send3.at[c, 0], recv3.at[c],
                                            device_id=target, device_id_type=mesh_id)

    def rows_of(c):
        return pl.ds(pl.multiple_of(c * RELAY_ROWS, RELAY_ROWS), RELAY_ROWS)

    def copy5(k):
        return pltpu.make_async_remote_copy(own, box5.at[k], send5.at[k], recv5.at[k],
                                            device_id=(flip_bits(group, masks[k], order_bits), slab),
                                            device_id_type=mesh_id)

    for k in range(len(masks)):
        copy5(k).start()

    def copy4(c, k):
        return pltpu.make_async_remote_copy(incoming.at[rows_of(c)], box4.at[k, c], send4.at[c, k],
                                            recv4.at[c, k], device_id=(flip_bits(group, masks[k], order_bits), slab),
                                            device_id_type=mesh_id)

    def share(c):
        for k in range(len(masks)):
            copy4(c, k).start()

    def stage1(c, carry):
        rows = rows_of(c)
        own_add = total_add[rows, :]
        own_min = total_min[rows, :]

        @pl.when(pos == 0)
        def _():
            box1_out[c, 0] = own_add
            box1_out[c, 1] = own_min

        @pl.when(pos > 0)
        def _():
            copy1(c).wait_recv()
            got_add = box1_in[c, 0]
            got_min = box1_in[c, 1]
            before[0, rows, :] = got_add
            before[1, rows, :] = got_min
            new_add = got_add + own_add
            new_min = jnp.minimum(got_min + own_add, own_min)

            @pl.when(pos < last)
            def _():
                box1_out[c, 0] = new_add
                box1_out[c, 1] = new_min

            @pl.when(is_end)
            def _():
                line_total[0, rows, :] = new_add
                line_total[1, rows, :] = new_min

        @pl.when((pos == 0) & is_end)
        def _():
            line_total[0, rows, :] = own_add
            line_total[1, rows, :] = own_min

        @pl.when(pos < last)
        def _():
            copy1(c).start()

        return carry

    def stage2(c, carry):
        rows = rows_of(c)

        @pl.when(is_end & first_col)
        def _():
            incoming[rows, :] = jnp.where(pos > 0, before[1, rows, :], jnp.inf)
            share(c)
            box2_out[c] = line_total[1, rows, :]

        @pl.when(is_end & jnp.logical_not(first_col))
        def _():
            copy2(c).wait_recv()
            value = box2_in[c]
            incoming[rows, :] = jnp.where(
                pos > 0, jnp.minimum(value + before[0, rows, :], before[1, rows, :]), value)
            share(c)
            box2_out[c] = jnp.minimum(value + line_total[0, rows, :], line_total[1, rows, :])

            @pl.when(pos > 0)
            def _():
                copy3_from_end(c, 0, at(col, 0)).start()

            @pl.when(half < last)
            def _():
                copy3_from_end(c, 1, at(col, last - 1)).start()

        @pl.when(is_end & (col < lines - 1))
        def _():
            copy2(c).start()

        return carry

    def stages12(c, carry):
        stage1(c, carry)
        return stage2(c, carry)

    lax.fori_loop(0, chunks, stages12, 0)

    def stage3(c, carry):
        rows = rows_of(c)

        @pl.when(first_col & jnp.logical_not(is_end))
        def _():
            incoming[rows, :] = jnp.where(pos > 0, before[1, rows, :], jnp.inf)
            share(c)

        @pl.when(jnp.logical_not(first_col) & (in_up | in_down))
        def _():
            copy3_relay(c, at(col, 0)).wait_recv()
            value = box3_in[c]
            incoming[rows, :] = jnp.where(
                pos > 0, jnp.minimum(value + before[0, rows, :], before[1, rows, :]), value)
            share(c)

            @pl.when(in_up & up_next)
            def _():
                copy3_relay(c, at(col, pos + 1)).start()

            @pl.when(in_down & down_next)
            def _():
                copy3_relay(c, at(col, pos - 1)).start()

        return carry

    lax.fori_loop(0, chunks, stage3, 0)

    def gather(c, carry):
        rows = rows_of(c)
        least = incoming[rows, :]
        for k in range(len(masks)):
            copy4(c, k).wait_recv()
            least = jnp.minimum(least, box4[k, c])
        least_in[rows, :] = least
        return carry

    lax.fori_loop(0, chunks, gather, 0)

    for k in range(len(masks)):
        copy5(k).wait_recv()

    def gather_plane(c, carry):
        rows = rows_of(c)
        least = own[rows, :]
        for k in range(len(masks)):
            least = jnp.minimum(least, box5[k, rows, :])
        least_plane[rows, :] = least
        return carry

    lax.fori_loop(0, chunks, gather_plane, 0)

    def drain(c, carry):
        @pl.when(pos < last)
        def _():
            copy1(c).wait_send()

        @pl.when(is_end & (col < lines - 1))
        def _():
            copy2(c).wait_send()

        @pl.when(is_end & jnp.logical_not(first_col) & (pos > 0))
        def _():
            copy3_from_end(c, 0, at(col, 0)).wait_send()

        @pl.when(is_end & jnp.logical_not(first_col) & (half < last))
        def _():
            copy3_from_end(c, 1, at(col, last - 1)).wait_send()

        @pl.when(jnp.logical_not(first_col) & ((in_up & up_next) | (in_down & down_next)))
        def _():
            copy3_relay(c, at(col, 0)).wait_send()

        for k in range(len(masks)):
            copy4(c, k).wait_send()
        return carry

    lax.fori_loop(0, chunks, drain, 0)
    for k in range(len(masks)):
        copy5(k).wait_send()


def relay(totals, own, slabs, orders):
    cells_y, cells_z = own.shape
    chunks = cells_y // RELAY_ROWS
    sharers = len(range(2, orders, 2))
    plane = jax.ShapeDtypeStruct(own.shape, jnp.float32)
    line = LINE if slabs % LINE == 0 else slabs
    vmem = pl.BlockSpec(memory_space=pltpu.VMEM)
    box = pltpu.VMEM((chunks, RELAY_ROWS, cells_z), jnp.float32)
    pair_box = pltpu.VMEM((chunks, 2, RELAY_ROWS, cells_z), jnp.float32)
    return pl.pallas_call(
        functools.partial(relay_kernel, line=line),
        out_shape=(plane, plane, plane),
        in_specs=[vmem, vmem],
        out_specs=(vmem, vmem, vmem),
        scratch_shapes=[
            pltpu.VMEM((2, cells_y, cells_z), jnp.float32),
            pltpu.VMEM((2, cells_y, cells_z), jnp.float32),
            pair_box,
            pair_box,
            box,
            box,
            box,
            pltpu.VMEM((max(sharers, 1), chunks, RELAY_ROWS, cells_z), jnp.float32),
            pltpu.VMEM((max(sharers, 1), cells_y, cells_z), jnp.float32),
            pltpu.SemaphoreType.DMA((chunks,)),
            pltpu.SemaphoreType.DMA((chunks,)),
            pltpu.SemaphoreType.DMA((chunks,)),
            pltpu.SemaphoreType.DMA((chunks,)),
            pltpu.SemaphoreType.DMA((chunks, 2)),
            pltpu.SemaphoreType.DMA((chunks,)),
            pltpu.SemaphoreType.DMA((chunks, max(sharers, 1))),
            pltpu.SemaphoreType.DMA((chunks, max(sharers, 1))),
            pltpu.SemaphoreType.DMA((max(sharers, 1),)),
            pltpu.SemaphoreType.DMA((max(sharers, 1),)),
        ],
        compiler_params=pltpu.CompilerParams(collective_id=0, has_side_effects=True),
    )(totals, own)


def shards(previous, fibre_tensor, tissue, stim_sites, stim_times):
    planes, cells_y, cells_z = previous.shape
    slabs = lax.axis_size("slab")
    orders = lax.axis_size("order")
    slab_index = lax.axis_index("slab")
    group_index = lax.axis_index("order")
    grid_step = 2.0 / (planes * slabs)

    plane_index = stim_sites // (cells_y * cells_z) - slab_index * planes
    row_index = stim_sites // cells_z % cells_y
    column_index = stim_sites % cells_z
    stims = jnp.stack([plane_index, row_index, column_index]).astype(jnp.int32)

    bits = jnp.stack([group_index % 2, group_index // 2 % 2, group_index // 4 % 2]).astype(jnp.int32)
    cost_x, field, totals, own_plane = local_sweeps(
        bits, stims, stim_times, fibre_tensor, tissue, previous, grid_step)

    core = group_index % 2
    incoming, least_in, least_plane = relay(totals, own_plane, slabs, orders)
    other = lax.ppermute(jnp.stack([least_plane, least_in]), "order", [(g, g ^ 1) for g in range(orders)])

    least0 = jnp.where(core == 0, least_plane, other[0])
    least1 = jnp.where(core == 0, other[0], least_plane)
    up_in = jnp.where(core == 0, least_in, other[1])
    down_in = jnp.where(core == 0, other[1], least_in)

    up_add = jnp.stack([cost_x[0], cost_x[0] + cost_x[1]])
    up_min = jnp.stack([field[0], jnp.minimum(field[0] + cost_x[1], field[1])])
    down_add = jnp.stack([cost_x[1] + cost_x[0], cost_x[1]])
    down_min = jnp.stack([jnp.minimum(field[1] + cost_x[0], field[0]), field[1]])
    backward_x = core == 1
    line_add = jnp.where(backward_x, down_add, up_add)
    line_min = jnp.where(backward_x, down_min, up_min)
    sweep_field = jnp.minimum(incoming[None] + line_add, line_min)

    least_local = jnp.stack([
        jnp.minimum(least0, least1 + cost_x[0]),
        jnp.minimum(least1, least0 + cost_x[1]),
    ])
    merged = jnp.minimum(
        least_local,
        jnp.minimum(up_in[None] + up_add, down_in[None] + down_add),
    )
    return (merged, sweep_field[None])


def solution(mesh):
    placed = (P("slab", None, None), P(None, "slab", None, None), P("slab", None, None), P(), P())
    return jax.shard_map(
        shards,
        mesh=mesh,
        in_specs=placed,
        out_specs=(P("slab", None, None), P("order", "slab", None, None)),
        check_vma=False,
    )
```

```python
import functools

import jax
import jax.numpy as jnp
from jax import lax
from jax.experimental import pallas as pl
from jax.experimental.pallas import tpu as pltpu
from jax.sharding import PartitionSpec as P

ROWS = 8
CHUNK = 32


def scan_step(a, m, k, axis, reverse, last):
    n = a.shape[axis]
    index = lax.broadcasted_iota(jnp.int32, a.shape, axis)
    shift = n - k if reverse else k
    valid = index < n - k if reverse else index >= k
    a_src = pltpu.roll(a, shift, axis)
    m_src = pltpu.roll(m, shift, axis)
    m = jnp.where(valid, jnp.minimum(m_src + a, m), m)
    if not last:
        a = jnp.where(valid, a_src + a, a)
    return a, m


def block_scan(a, m, axis, reverse, need_sum):
    n = a.shape[axis]
    k = 1
    while k < n:
        a, m = scan_step(a, m, k, axis, reverse, last=(2 * k >= n) and not need_sum)
        k *= 2
    return a, m


def local_kernel(flags, stims, stim_times, fibre, tissue, previous, cost_x, field, totals, own,
                 cost_y, *, grid_step):
    planes, cells_y, cells_z = previous.shape
    chunks = cells_y // CHUNK
    inf = jnp.float32(jnp.inf)

    field[...] = previous[...]

    def seed(k, carry):
        p = stims[0, k]
        r = stims[1, k]
        c = stims[2, k]

        @pl.when((p >= 0) & (p < planes))
        def _():
            base = pl.multiple_of(r // ROWS * ROWS, ROWS)
            block = field[p, pl.ds(base, ROWS), :]
            row = lax.broadcasted_iota(jnp.int32, block.shape, 0)
            lane = lax.broadcasted_iota(jnp.int32, block.shape, 1)
            hit = (row == r - base) & (lane == c)
            field[p, pl.ds(base, ROWS), :] = jnp.where(hit, jnp.minimum(block, stim_times[k]), block)

        return carry

    lax.fori_loop(0, stims.shape[1], seed, 0)

    def costs_and_z(reverse):
        def body(i, carry):
            p = i // chunks
            rows = pl.ds(pl.multiple_of((i % chunks) * CHUNK, CHUNK), CHUNK)
            xx = fibre[0, p, rows, :]
            yy = fibre[1, p, rows, :]
            zz = fibre[2, p, rows, :]
            xy = fibre[3, p, rows, :]
            xz = fibre[4, p, rows, :]
            yz = fibre[5, p, rows, :]
            cx = yy * zz - yz * yz
            cy = xx * zz - xz * xz
            cz = xx * yy - xy * xy
            det = xx * cx - xy * (xy * zz - yz * xz) + xz * (xy * yz - yy * xz)
            factor = jnp.where(tissue[p, rows, :] == 1, 1.0, 4.0).astype(jnp.float32) * grid_step
            inverse = 1.0 / det
            cost_x[p, rows, :] = jnp.sqrt(cx * inverse) * factor
            cost_y[p, rows, :] = jnp.sqrt(cy * inverse) * factor
            step_z = jnp.sqrt(cz * inverse) * factor
            _, u = block_scan(step_z, field[p, rows, :], 1, reverse, False)
            field[p, rows, :] = u
            return carry

        lax.fori_loop(0, planes * chunks, body, 0, unroll=2)

    def sweep_y(reverse):
        def body(j, carry):
            i = chunks - 1 - j if reverse else j
            rows = pl.ds(pl.multiple_of(i * CHUNK, CHUNK), CHUNK)
            out = []
            for p in range(planes):
                a, m = block_scan(cost_y[p, rows, :], field[p, rows, :], 0, reverse, True)
                u = jnp.minimum(carry[p] + a, m)
                field[p, rows, :] = u
                edge = u[0:1, :] if reverse else u[CHUNK - 1:CHUNK, :]
                out.append(jnp.broadcast_to(edge, u.shape))
            return tuple(out)

        start = tuple(jnp.full((CHUNK, cells_z), inf, jnp.float32) for _ in range(planes))
        lax.fori_loop(0, chunks, body, start, unroll=2)

    for flag, fn in ((flags[2], costs_and_z), (flags[1], sweep_y)):
        pl.when(flag == 1)(functools.partial(fn, True))
        pl.when(flag != 1)(functools.partial(fn, False))

    def edge(i, carry):
        rows = pl.ds(pl.multiple_of(i * CHUNK, CHUNK), CHUNK)
        c0 = cost_x[0, rows, :]
        c1 = cost_x[1, rows, :]
        u0 = field[0, rows, :]
        u1 = field[1, rows, :]
        down = flags[0] == 1
        totals[0, rows, :] = jnp.where(down, c1 + c0, c0 + c1)
        totals[1, rows, :] = jnp.where(down, jnp.minimum(u1 + c0, u0), jnp.minimum(u0 + c1, u1))
        own[rows, :] = jnp.where(down, u1, u0)
        return carry

    lax.fori_loop(0, chunks, edge, 0)


def local_sweeps(flags, stims, stim_times, fibre, tissue, previous, grid_step):
    planes, cells_y, cells_z = previous.shape
    field = jax.ShapeDtypeStruct(previous.shape, jnp.float32)
    totals = jax.ShapeDtypeStruct((2, cells_y, cells_z), jnp.float32)
    own = jax.ShapeDtypeStruct((cells_y, cells_z), jnp.float32)
    vmem = pl.BlockSpec(memory_space=pltpu.VMEM)
    smem = pl.BlockSpec(memory_space=pltpu.SMEM)
    elements = planes * cells_y * cells_z
    return pl.pallas_call(
        functools.partial(local_kernel, grid_step=grid_step),
        out_shape=(field, field, totals, own),
        in_specs=[smem, smem, smem, vmem, vmem, vmem],
        out_specs=(vmem, vmem, vmem, vmem),
        scratch_shapes=[pltpu.VMEM(previous.shape, jnp.float32)],
        compiler_params=pltpu.CompilerParams(vmem_limit_bytes=48 * 1024 * 1024),
        cost_estimate=pl.CostEstimate(
            flops=300 * elements, transcendentals=6 * elements, bytes_accessed=40 * elements
        ),
    )(flags, stims, stim_times, fibre, tissue, previous)


RELAY_ROWS = 8
LINE = 8


def flip_bits(value, mask, bits):
    out = 0
    for j in range(bits):
        out = out + (2 ** j) * ((value // 2 ** j + (mask >> j) % 2) % 2)
    return out


def relay_kernel(totals, own, incoming, least_in, least_plane, before, line_total, box1_in,
                 box1_out, box2_in, box2_out, box3_in, box4, box5, send1, recv1, send2, recv2, send3,
                 recv3, send4, recv4, send5, recv5, *, line):
    total_add = totals.at[0]
    total_min = totals.at[1]
    cells_y, cells_z = incoming.shape
    chunks = cells_y // RELAY_ROWS
    slabs = lax.axis_size("slab")
    lines = slabs // line
    half = line // 2
    slab = lax.axis_index("slab")
    group = lax.axis_index("order")
    odd = group % 2
    rank = slab + odd * (slabs - 1 - 2 * slab)
    col = rank // line
    pos = rank % line
    last = line - 1
    mesh_id = pl.DeviceIdType.MESH

    def device(r):
        return (group, r + odd * (slabs - 1 - 2 * r))

    def at(c, p):
        return device(c * line + p)

    orders = lax.axis_size("order")
    masks = list(range(2, orders, 2))
    order_bits = max(orders - 1, 1).bit_length()
    first_col = col == 0
    is_end = pos == last
    in_up = pos < half
    in_down = (pos >= half) & (pos < last)
    up_next = pos + 1 < half
    down_next = pos > half

    barrier = pltpu.get_barrier_semaphore()
    neighbours = []
    neighbours.append((pos > 0, at(col, pos - 1)))
    neighbours.append((pos < last, at(col, pos + 1)))
    neighbours.append(((pos == 0) & (col > 0) & (last > 0), at(col, last)))
    neighbours.append((is_end & (col > 0) & (last > 0), at(col, 0)))
    neighbours.append((is_end & (col > 0), at(col - 1, last)))
    neighbours.append((is_end & (col < lines - 1), at(col + 1, last)))
    for m in masks:
        neighbours.append((slab >= 0, (flip_bits(group, m, order_bits), slab)))
    count = jnp.int32(0)
    for cond, dev in neighbours:
        @pl.when(cond)
        def _():
            pl.semaphore_signal(barrier, 1, device_id=dev, device_id_type=mesh_id)

        count = count + cond.astype(jnp.int32)
    pl.semaphore_wait(barrier, count)

    def copy1(c):
        return pltpu.make_async_remote_copy(box1_out.at[c], box1_in.at[c], send1.at[c], recv1.at[c],
                                            device_id=at(col, pos + 1), device_id_type=mesh_id)

    def copy2(c):
        return pltpu.make_async_remote_copy(box2_out.at[c], box2_in.at[c], send2.at[c], recv2.at[c],
                                            device_id=at(col + 1, last), device_id_type=mesh_id)

    def copy3_from_end(c, k, target):
        return pltpu.make_async_remote_copy(box2_in.at[c], box3_in.at[c], send3.at[c, k], recv3.at[c],
                                            device_id=target, device_id_type=mesh_id)

    def copy3_relay(c, target):
        return pltpu.make_async_remote_copy(box3_in.at[c], box3_in.at[c], send3.at[c, 0], recv3.at[c],
                                            device_id=target, device_id_type=mesh_id)

    def rows_of(c):
        return pl.ds(pl.multiple_of(c * RELAY_ROWS, RELAY_ROWS), RELAY_ROWS)

    def copy5(k):
        return pltpu.make_async_remote_copy(own, box5.at[k], send5.at[k], recv5.at[k],
                                            device_id=(flip_bits(group, masks[k], order_bits), slab),
                                            device_id_type=mesh_id)

    for k in range(len(masks)):
        copy5(k).start()

    def copy4(c, k):
        return pltpu.make_async_remote_copy(incoming.at[rows_of(c)], box4.at[k, c], send4.at[c, k],
                                            recv4.at[c, k], device_id=(flip_bits(group, masks[k], order_bits), slab),
                                            device_id_type=mesh_id)

    def share(c):
        for k in range(len(masks)):
            copy4(c, k).start()

    def stage1(c, carry):
        rows = rows_of(c)
        own_add = total_add[rows, :]
        own_min = total_min[rows, :]

        @pl.when(pos == 0)
        def _():
            box1_out[c, 0] = own_add
            box1_out[c, 1] = own_min

        @pl.when(pos > 0)
        def _():
            copy1(c).wait_recv()
            got_add = box1_in[c, 0]
            got_min = box1_in[c, 1]
            before[0, rows, :] = got_add
            before[1, rows, :] = got_min
            new_add = got_add + own_add
            new_min = jnp.minimum(got_min + own_add, own_min)

            @pl.when(pos < last)
            def _():
                box1_out[c, 0] = new_add
                box1_out[c, 1] = new_min

            @pl.when(is_end)
            def _():
                line_total[0, rows, :] = new_add
                line_total[1, rows, :] = new_min

        @pl.when((pos == 0) & is_end)
        def _():
            line_total[0, rows, :] = own_add
            line_total[1, rows, :] = own_min

        @pl.when(pos < last)
        def _():
            copy1(c).start()

        return carry

    def stage2(c, carry):
        rows = rows_of(c)

        @pl.when(is_end & first_col)
        def _():
            incoming[rows, :] = jnp.where(pos > 0, before[1, rows, :], jnp.inf)
            share(c)
            box2_out[c] = line_total[1, rows, :]

        @pl.when(is_end & jnp.logical_not(first_col))
        def _():
            copy2(c).wait_recv()
            value = box2_in[c]
            incoming[rows, :] = jnp.where(
                pos > 0, jnp.minimum(value + before[0, rows, :], before[1, rows, :]), value)
            share(c)
            box2_out[c] = jnp.minimum(value + line_total[0, rows, :], line_total[1, rows, :])

            @pl.when(pos > 0)
            def _():
                copy3_from_end(c, 0, at(col, 0)).start()

            @pl.when(half < last)
            def _():
                copy3_from_end(c, 1, at(col, last - 1)).start()

        @pl.when(is_end & (col < lines - 1))
        def _():
            copy2(c).start()

        return carry

    def stages12(c, carry):
        stage1(c, carry)
        return stage2(c, carry)

    lax.fori_loop(0, chunks, stages12, 0)

    def stage3(c, carry):
        rows = rows_of(c)

        @pl.when(first_col & jnp.logical_not(is_end))
        def _():
            incoming[rows, :] = jnp.where(pos > 0, before[1, rows, :], jnp.inf)
            share(c)

        @pl.when(jnp.logical_not(first_col) & (in_up | in_down))
        def _():
            copy3_relay(c, at(col, 0)).wait_recv()
            value = box3_in[c]
            incoming[rows, :] = jnp.where(
                pos > 0, jnp.minimum(value + before[0, rows, :], before[1, rows, :]), value)
            share(c)

            @pl.when(in_up & up_next)
            def _():
                copy3_relay(c, at(col, pos + 1)).start()

            @pl.when(in_down & down_next)
            def _():
                copy3_relay(c, at(col, pos - 1)).start()

        return carry

    lax.fori_loop(0, chunks, stage3, 0)

    def gather(c, carry):
        rows = rows_of(c)
        least = incoming[rows, :]
        for k in range(len(masks)):
            copy4(c, k).wait_recv()
            least = jnp.minimum(least, box4[k, c])
        least_in[rows, :] = least
        return carry

    lax.fori_loop(0, chunks, gather, 0)

    for k in range(len(masks)):
        copy5(k).wait_recv()

    def gather_plane(c, carry):
        rows = rows_of(c)
        least = own[rows, :]
        for k in range(len(masks)):
            least = jnp.minimum(least, box5[k, rows, :])
        least_plane[rows, :] = least
        return carry

    lax.fori_loop(0, chunks, gather_plane, 0)

    def drain(c, carry):
        @pl.when(pos < last)
        def _():
            copy1(c).wait_send()

        @pl.when(is_end & (col < lines - 1))
        def _():
            copy2(c).wait_send()

        @pl.when(is_end & jnp.logical_not(first_col) & (pos > 0))
        def _():
            copy3_from_end(c, 0, at(col, 0)).wait_send()

        @pl.when(is_end & jnp.logical_not(first_col) & (half < last))
        def _():
            copy3_from_end(c, 1, at(col, last - 1)).wait_send()

        @pl.when(jnp.logical_not(first_col) & ((in_up & up_next) | (in_down & down_next)))
        def _():
            copy3_relay(c, at(col, 0)).wait_send()

        for k in range(len(masks)):
            copy4(c, k).wait_send()
        return carry

    lax.fori_loop(0, chunks, drain, 0)
    for k in range(len(masks)):
        copy5(k).wait_send()


def relay(totals, own, slabs, orders):
    cells_y, cells_z = own.shape
    chunks = cells_y // RELAY_ROWS
    sharers = len(range(2, orders, 2))
    plane = jax.ShapeDtypeStruct(own.shape, jnp.float32)
    line = LINE if slabs % LINE == 0 else slabs
    vmem = pl.BlockSpec(memory_space=pltpu.VMEM)
    box = pltpu.VMEM((chunks, RELAY_ROWS, cells_z), jnp.float32)
    pair_box = pltpu.VMEM((chunks, 2, RELAY_ROWS, cells_z), jnp.float32)
    return pl.pallas_call(
        functools.partial(relay_kernel, line=line),
        out_shape=(plane, plane, plane),
        in_specs=[vmem, vmem],
        out_specs=(vmem, vmem, vmem),
        scratch_shapes=[
            pltpu.VMEM((2, cells_y, cells_z), jnp.float32),
            pltpu.VMEM((2, cells_y, cells_z), jnp.float32),
            pair_box,
            pair_box,
            box,
            box,
            box,
            pltpu.VMEM((max(sharers, 1), chunks, RELAY_ROWS, cells_z), jnp.float32),
            pltpu.VMEM((max(sharers, 1), cells_y, cells_z), jnp.float32),
            pltpu.SemaphoreType.DMA((chunks,)),
            pltpu.SemaphoreType.DMA((chunks,)),
            pltpu.SemaphoreType.DMA((chunks,)),
            pltpu.SemaphoreType.DMA((chunks,)),
            pltpu.SemaphoreType.DMA((chunks, 2)),
            pltpu.SemaphoreType.DMA((chunks,)),
            pltpu.SemaphoreType.DMA((chunks, max(sharers, 1))),
            pltpu.SemaphoreType.DMA((chunks, max(sharers, 1))),
            pltpu.SemaphoreType.DMA((max(sharers, 1),)),
            pltpu.SemaphoreType.DMA((max(sharers, 1),)),
        ],
        compiler_params=pltpu.CompilerParams(collective_id=0, has_side_effects=True),
    )(totals, own)


def shards(previous, fibre_tensor, tissue, stim_sites, stim_times):
    planes, cells_y, cells_z = previous.shape
    slabs = lax.axis_size("slab")
    orders = lax.axis_size("order")
    slab_index = lax.axis_index("slab")
    group_index = lax.axis_index("order")
    grid_step = 2.0 / (planes * slabs)

    plane_index = stim_sites // (cells_y * cells_z) - slab_index * planes
    row_index = stim_sites // cells_z % cells_y
    column_index = stim_sites % cells_z
    stims = jnp.stack([plane_index, row_index, column_index]).astype(jnp.int32)

    bits = jnp.stack([group_index % 2, group_index // 2 % 2, group_index // 4 % 2]).astype(jnp.int32)
    cost_x, field, totals, own_plane = local_sweeps(
        bits, stims, stim_times, fibre_tensor, tissue, previous, grid_step)

    core = group_index % 2
    incoming, least_in, least_plane = relay(totals, own_plane, slabs, orders)
    other = lax.ppermute(jnp.stack([least_plane, least_in]), "order", [(g, g ^ 1) for g in range(orders)])

    least0 = jnp.where(core == 0, least_plane, other[0])
    least1 = jnp.where(core == 0, other[0], least_plane)
    up_in = jnp.where(core == 0, least_in, other[1])
    down_in = jnp.where(core == 0, other[1], least_in)

    up_add = jnp.stack([cost_x[0], cost_x[0] + cost_x[1]])
    up_min = jnp.stack([field[0], jnp.minimum(field[0] + cost_x[1], field[1])])
    down_add = jnp.stack([cost_x[1] + cost_x[0], cost_x[1]])
    down_min = jnp.stack([jnp.minimum(field[1] + cost_x[0], field[0]), field[1]])
    backward_x = core == 1
    line_add = jnp.where(backward_x, down_add, up_add)
    line_min = jnp.where(backward_x, down_min, up_min)
    sweep_field = jnp.minimum(incoming[None] + line_add, line_min)

    least_local = jnp.stack([
        jnp.minimum(least0, least1 + cost_x[0]),
        jnp.minimum(least1, least0 + cost_x[1]),
    ])
    merged = jnp.minimum(
        least_local,
        jnp.minimum(up_in[None] + up_add, down_in[None] + down_add),
    )
    return (merged, sweep_field[None])


def solution(mesh):
    placed = (P("slab", None, None), P(None, "slab", None, None), P("slab", None, None), P(), P())
    return jax.shard_map(
        shards,
        mesh=mesh,
        in_specs=placed,
        out_specs=(P("slab", None, None), P("order", "slab", None, None)),
        check_vma=False,
    )
```

```python
import functools

import jax
import jax.numpy as jnp
from jax import lax
from jax.experimental import pallas as pl
from jax.experimental.pallas import tpu as pltpu
from jax.sharding import PartitionSpec as P

ROWS = 8
CHUNK = 32


def scan_step(a, m, k, axis, reverse, last):
    n = a.shape[axis]
    index = lax.broadcasted_iota(jnp.int32, a.shape, axis)
    shift = n - k if reverse else k
    valid = index < n - k if reverse else index >= k
    a_src = pltpu.roll(a, shift, axis)
    m_src = pltpu.roll(m, shift, axis)
    m = jnp.where(valid, jnp.minimum(m_src + a, m), m)
    if not last:
        a = jnp.where(valid, a_src + a, a)
    return a, m


def block_scan(a, m, axis, reverse, need_sum):
    n = a.shape[axis]
    k = 1
    while k < n:
        a, m = scan_step(a, m, k, axis, reverse, last=(2 * k >= n) and not need_sum)
        k *= 2
    return a, m


def local_kernel(flags, stims, stim_times, fibre, tissue, previous, cost_x, field, totals, own,
                 cost_y, *, grid_step):
    planes, cells_y, cells_z = previous.shape
    chunks = cells_y // CHUNK
    inf = jnp.float32(jnp.inf)

    field[...] = previous[...]

    def seed(k, carry):
        p = stims[0, k]
        r = stims[1, k]
        c = stims[2, k]

        @pl.when((p >= 0) & (p < planes))
        def _():
            base = pl.multiple_of(r // ROWS * ROWS, ROWS)
            block = field[p, pl.ds(base, ROWS), :]
            row = lax.broadcasted_iota(jnp.int32, block.shape, 0)
            lane = lax.broadcasted_iota(jnp.int32, block.shape, 1)
            hit = (row == r - base) & (lane == c)
            field[p, pl.ds(base, ROWS), :] = jnp.where(hit, jnp.minimum(block, stim_times[k]), block)

        return carry

    lax.fori_loop(0, stims.shape[1], seed, 0)

    def costs_and_z(reverse):
        def body(i, carry):
            p = i // chunks
            rows = pl.ds(pl.multiple_of((i % chunks) * CHUNK, CHUNK), CHUNK)
            xx = fibre[0, p, rows, :]
            yy = fibre[1, p, rows, :]
            zz = fibre[2, p, rows, :]
            xy = fibre[3, p, rows, :]
            xz = fibre[4, p, rows, :]
            yz = fibre[5, p, rows, :]
            cx = yy * zz - yz * yz
            cy = xx * zz - xz * xz
            cz = xx * yy - xy * xy
            det = xx * cx - xy * (xy * zz - yz * xz) + xz * (xy * yz - yy * xz)
            factor = jnp.where(tissue[p, rows, :] == 1, 1.0, 4.0).astype(jnp.float32) * grid_step
            inverse = 1.0 / det
            cost_x[p, rows, :] = jnp.sqrt(cx * inverse) * factor
            cost_y[p, rows, :] = jnp.sqrt(cy * inverse) * factor
            step_z = jnp.sqrt(cz * inverse) * factor
            _, u = block_scan(step_z, field[p, rows, :], 1, reverse, False)
            field[p, rows, :] = u
            return carry

        lax.fori_loop(0, planes * chunks, body, 0, unroll=2)

    def sweep_y(reverse):
        def body(j, carry):
            i = chunks - 1 - j if reverse else j
            rows = pl.ds(pl.multiple_of(i * CHUNK, CHUNK), CHUNK)
            out = []
            for p in range(planes):
                a, m = block_scan(cost_y[p, rows, :], field[p, rows, :], 0, reverse, True)
                u = jnp.minimum(carry[p] + a, m)
                field[p, rows, :] = u
                edge = u[0:1, :] if reverse else u[CHUNK - 1:CHUNK, :]
                out.append(jnp.broadcast_to(edge, u.shape))
            return tuple(out)

        start = tuple(jnp.full((CHUNK, cells_z), inf, jnp.float32) for _ in range(planes))
        lax.fori_loop(0, chunks, body, start, unroll=2)

    for flag, fn in ((flags[2], costs_and_z), (flags[1], sweep_y)):
        pl.when(flag == 1)(functools.partial(fn, True))
        pl.when(flag != 1)(functools.partial(fn, False))

    def edge(i, carry):
        rows = pl.ds(pl.multiple_of(i * CHUNK, CHUNK), CHUNK)
        c0 = cost_x[0, rows, :]
        c1 = cost_x[1, rows, :]
        u0 = field[0, rows, :]
        u1 = field[1, rows, :]
        down = flags[0] == 1
        totals[0, rows, :] = jnp.where(down, c1 + c0, c0 + c1)
        totals[1, rows, :] = jnp.where(down, jnp.minimum(u1 + c0, u0), jnp.minimum(u0 + c1, u1))
        own[rows, :] = jnp.where(down, u1, u0)
        return carry

    lax.fori_loop(0, chunks, edge, 0)


def local_sweeps(flags, stims, stim_times, fibre, tissue, previous, grid_step):
    planes, cells_y, cells_z = previous.shape
    field = jax.ShapeDtypeStruct(previous.shape, jnp.float32)
    totals = jax.ShapeDtypeStruct((2, cells_y, cells_z), jnp.float32)
    own = jax.ShapeDtypeStruct((cells_y, cells_z), jnp.float32)
    vmem = pl.BlockSpec(memory_space=pltpu.VMEM)
    smem = pl.BlockSpec(memory_space=pltpu.SMEM)
    elements = planes * cells_y * cells_z
    return pl.pallas_call(
        functools.partial(local_kernel, grid_step=grid_step),
        out_shape=(field, field, totals, own),
        in_specs=[smem, smem, smem, vmem, vmem, vmem],
        out_specs=(vmem, vmem, vmem, vmem),
        scratch_shapes=[pltpu.VMEM(previous.shape, jnp.float32)],
        compiler_params=pltpu.CompilerParams(vmem_limit_bytes=48 * 1024 * 1024),
        cost_estimate=pl.CostEstimate(
            flops=300 * elements, transcendentals=6 * elements, bytes_accessed=40 * elements
        ),
    )(flags, stims, stim_times, fibre, tissue, previous)


RELAY_ROWS = 32
LINE = 8


def flip_bits(value, mask, bits):
    out = 0
    for j in range(bits):
        out = out + (2 ** j) * ((value // 2 ** j + (mask >> j) % 2) % 2)
    return out


def relay_kernel(totals, own, incoming, least_in, least_plane, before, line_total, box1_in,
                 box1_out, box2_in, box2_out, box3_in, box4, box5, send1, recv1, send2, recv2, send3,
                 recv3, send4, recv4, send5, recv5, *, line):
    total_add = totals.at[0]
    total_min = totals.at[1]
    cells_y, cells_z = incoming.shape
    chunks = cells_y // RELAY_ROWS
    slabs = lax.axis_size("slab")
    lines = slabs // line
    half = line // 2
    slab = lax.axis_index("slab")
    group = lax.axis_index("order")
    odd = group % 2
    rank = slab + odd * (slabs - 1 - 2 * slab)
    col = rank // line
    pos = rank % line
    last = line - 1
    mesh_id = pl.DeviceIdType.MESH

    def device(r):
        return (group, r + odd * (slabs - 1 - 2 * r))

    def at(c, p):
        return device(c * line + p)

    orders = lax.axis_size("order")
    masks = list(range(2, orders, 2))
    order_bits = max(orders - 1, 1).bit_length()
    first_col = col == 0
    is_end = pos == last
    in_up = pos < half
    in_down = (pos >= half) & (pos < last)
    up_next = pos + 1 < half
    down_next = pos > half

    barrier = pltpu.get_barrier_semaphore()
    neighbours = []
    neighbours.append((pos > 0, at(col, pos - 1)))
    neighbours.append((pos < last, at(col, pos + 1)))
    neighbours.append(((pos == 0) & (col > 0) & (last > 0), at(col, last)))
    neighbours.append((is_end & (col > 0) & (last > 0), at(col, 0)))
    neighbours.append((is_end & (col > 0), at(col - 1, last)))
    neighbours.append((is_end & (col < lines - 1), at(col + 1, last)))
    for m in masks:
        neighbours.append((slab >= 0, (flip_bits(group, m, order_bits), slab)))
    count = jnp.int32(0)
    for cond, dev in neighbours:
        @pl.when(cond)
        def _():
            pl.semaphore_signal(barrier, 1, device_id=dev, device_id_type=mesh_id)

        count = count + cond.astype(jnp.int32)
    pl.semaphore_wait(barrier, count)

    def copy1(c):
        return pltpu.make_async_remote_copy(box1_out.at[c], box1_in.at[c], send1.at[c], recv1.at[c],
                                            device_id=at(col, pos + 1), device_id_type=mesh_id)

    def copy2(c):
        return pltpu.make_async_remote_copy(box2_out.at[c], box2_in.at[c], send2.at[c], recv2.at[c],
                                            device_id=at(col + 1, last), device_id_type=mesh_id)

    def copy3_from_end(c, k, target):
        return pltpu.make_async_remote_copy(box2_in.at[c], box3_in.at[c], send3.at[c, k], recv3.at[c],
                                            device_id=target, device_id_type=mesh_id)

    def copy3_relay(c, target):
        return pltpu.make_async_remote_copy(box3_in.at[c], box3_in.at[c], send3.at[c, 0], recv3.at[c],
                                            device_id=target, device_id_type=mesh_id)

    def rows_of(c):
        return pl.ds(pl.multiple_of(c * RELAY_ROWS, RELAY_ROWS), RELAY_ROWS)

    def copy5(k):
        return pltpu.make_async_remote_copy(own, box5.at[k], send5.at[k], recv5.at[k],
                                            device_id=(flip_bits(group, masks[k], order_bits), slab),
                                            device_id_type=mesh_id)

    for k in range(len(masks)):
        copy5(k).start()

    def copy4(c, k):
        return pltpu.make_async_remote_copy(incoming.at[rows_of(c)], box4.at[k, c], send4.at[c, k],
                                            recv4.at[c, k], device_id=(flip_bits(group, masks[k], order_bits), slab),
                                            device_id_type=mesh_id)

    def share(c):
        for k in range(len(masks)):
            copy4(c, k).start()

    def stage1(c, carry):
        rows = rows_of(c)
        own_add = total_add[rows, :]
        own_min = total_min[rows, :]

        @pl.when(pos == 0)
        def _():
            box1_out[c, 0] = own_add
            box1_out[c, 1] = own_min

        @pl.when(pos > 0)
        def _():
            copy1(c).wait_recv()
            got_add = box1_in[c, 0]
            got_min = box1_in[c, 1]
            before[0, rows, :] = got_add
            before[1, rows, :] = got_min
            new_add = got_add + own_add
            new_min = jnp.minimum(got_min + own_add, own_min)

            @pl.when(pos < last)
            def _():
                box1_out[c, 0] = new_add
                box1_out[c, 1] = new_min

            @pl.when(is_end)
            def _():
                line_total[0, rows, :] = new_add
                line_total[1, rows, :] = new_min

        @pl.when((pos == 0) & is_end)
        def _():
            line_total[0, rows, :] = own_add
            line_total[1, rows, :] = own_min

        @pl.when(pos < last)
        def _():
            copy1(c).start()

        return carry

    def stage2(c, carry):
        rows = rows_of(c)

        @pl.when(is_end & first_col)
        def _():
            incoming[rows, :] = jnp.where(pos > 0, before[1, rows, :], jnp.inf)
            share(c)
            box2_out[c] = line_total[1, rows, :]

        @pl.when(is_end & jnp.logical_not(first_col))
        def _():
            copy2(c).wait_recv()
            value = box2_in[c]
            incoming[rows, :] = jnp.where(
                pos > 0, jnp.minimum(value + before[0, rows, :], before[1, rows, :]), value)
            share(c)
            box2_out[c] = jnp.minimum(value + line_total[0, rows, :], line_total[1, rows, :])

            @pl.when(pos > 0)
            def _():
                copy3_from_end(c, 0, at(col, 0)).start()

            @pl.when(half < last)
            def _():
                copy3_from_end(c, 1, at(col, last - 1)).start()

        @pl.when(is_end & (col < lines - 1))
        def _():
            copy2(c).start()

        return carry

    def stages12(c, carry):
        stage1(c, carry)
        return stage2(c, carry)

    lax.fori_loop(0, chunks, stages12, 0)

    def stage3(c, carry):
        rows = rows_of(c)

        @pl.when(first_col & jnp.logical_not(is_end))
        def _():
            incoming[rows, :] = jnp.where(pos > 0, before[1, rows, :], jnp.inf)
            share(c)

        @pl.when(jnp.logical_not(first_col) & (in_up | in_down))
        def _():
            copy3_relay(c, at(col, 0)).wait_recv()
            value = box3_in[c]
            incoming[rows, :] = jnp.where(
                pos > 0, jnp.minimum(value + before[0, rows, :], before[1, rows, :]), value)
            share(c)

            @pl.when(in_up & up_next)
            def _():
                copy3_relay(c, at(col, pos + 1)).start()

            @pl.when(in_down & down_next)
            def _():
                copy3_relay(c, at(col, pos - 1)).start()

        return carry

    lax.fori_loop(0, chunks, stage3, 0)

    def gather(c, carry):
        rows = rows_of(c)
        least = incoming[rows, :]
        for k in range(len(masks)):
            copy4(c, k).wait_recv()
            least = jnp.minimum(least, box4[k, c])
        least_in[rows, :] = least
        return carry

    lax.fori_loop(0, chunks, gather, 0)

    for k in range(len(masks)):
        copy5(k).wait_recv()

    def gather_plane(c, carry):
        rows = rows_of(c)
        least = own[rows, :]
        for k in range(len(masks)):
            least = jnp.minimum(least, box5[k, rows, :])
        least_plane[rows, :] = least
        return carry

    lax.fori_loop(0, chunks, gather_plane, 0)

    def drain(c, carry):
        @pl.when(pos < last)
        def _():
            copy1(c).wait_send()

        @pl.when(is_end & (col < lines - 1))
        def _():
            copy2(c).wait_send()

        @pl.when(is_end & jnp.logical_not(first_col) & (pos > 0))
        def _():
            copy3_from_end(c, 0, at(col, 0)).wait_send()

        @pl.when(is_end & jnp.logical_not(first_col) & (half < last))
        def _():
            copy3_from_end(c, 1, at(col, last - 1)).wait_send()

        @pl.when(jnp.logical_not(first_col) & ((in_up & up_next) | (in_down & down_next)))
        def _():
            copy3_relay(c, at(col, 0)).wait_send()

        for k in range(len(masks)):
            copy4(c, k).wait_send()
        return carry

    lax.fori_loop(0, chunks, drain, 0)
    for k in range(len(masks)):
        copy5(k).wait_send()


def relay(totals, own, slabs, orders):
    cells_y, cells_z = own.shape
    chunks = cells_y // RELAY_ROWS
    sharers = len(range(2, orders, 2))
    plane = jax.ShapeDtypeStruct(own.shape, jnp.float32)
    line = LINE if slabs % LINE == 0 else slabs
    vmem = pl.BlockSpec(memory_space=pltpu.VMEM)
    box = pltpu.VMEM((chunks, RELAY_ROWS, cells_z), jnp.float32)
    pair_box = pltpu.VMEM((chunks, 2, RELAY_ROWS, cells_z), jnp.float32)
    return pl.pallas_call(
        functools.partial(relay_kernel, line=line),
        out_shape=(plane, plane, plane),
        in_specs=[vmem, vmem],
        out_specs=(vmem, vmem, vmem),
        scratch_shapes=[
            pltpu.VMEM((2, cells_y, cells_z), jnp.float32),
            pltpu.VMEM((2, cells_y, cells_z), jnp.float32),
            pair_box,
            pair_box,
            box,
            box,
            box,
            pltpu.VMEM((max(sharers, 1), chunks, RELAY_ROWS, cells_z), jnp.float32),
            pltpu.VMEM((max(sharers, 1), cells_y, cells_z), jnp.float32),
            pltpu.SemaphoreType.DMA((chunks,)),
            pltpu.SemaphoreType.DMA((chunks,)),
            pltpu.SemaphoreType.DMA((chunks,)),
            pltpu.SemaphoreType.DMA((chunks,)),
            pltpu.SemaphoreType.DMA((chunks, 2)),
            pltpu.SemaphoreType.DMA((chunks,)),
            pltpu.SemaphoreType.DMA((chunks, max(sharers, 1))),
            pltpu.SemaphoreType.DMA((chunks, max(sharers, 1))),
            pltpu.SemaphoreType.DMA((max(sharers, 1),)),
            pltpu.SemaphoreType.DMA((max(sharers, 1),)),
        ],
        compiler_params=pltpu.CompilerParams(collective_id=0, has_side_effects=True),
    )(totals, own)


def shards(previous, fibre_tensor, tissue, stim_sites, stim_times):
    planes, cells_y, cells_z = previous.shape
    slabs = lax.axis_size("slab")
    orders = lax.axis_size("order")
    slab_index = lax.axis_index("slab")
    group_index = lax.axis_index("order")
    grid_step = 2.0 / (planes * slabs)

    plane_index = stim_sites // (cells_y * cells_z) - slab_index * planes
    row_index = stim_sites // cells_z % cells_y
    column_index = stim_sites % cells_z
    stims = jnp.stack([plane_index, row_index, column_index]).astype(jnp.int32)

    bits = jnp.stack([group_index % 2, group_index // 2 % 2, group_index // 4 % 2]).astype(jnp.int32)
    cost_x, field, totals, own_plane = local_sweeps(
        bits, stims, stim_times, fibre_tensor, tissue, previous, grid_step)

    core = group_index % 2
    incoming, least_in, least_plane = relay(totals, own_plane, slabs, orders)
    other = lax.ppermute(jnp.stack([least_plane, least_in]), "order", [(g, g ^ 1) for g in range(orders)])

    least0 = jnp.where(core == 0, least_plane, other[0])
    least1 = jnp.where(core == 0, other[0], least_plane)
    up_in = jnp.where(core == 0, least_in, other[1])
    down_in = jnp.where(core == 0, other[1], least_in)

    up_add = jnp.stack([cost_x[0], cost_x[0] + cost_x[1]])
    up_min = jnp.stack([field[0], jnp.minimum(field[0] + cost_x[1], field[1])])
    down_add = jnp.stack([cost_x[1] + cost_x[0], cost_x[1]])
    down_min = jnp.stack([jnp.minimum(field[1] + cost_x[0], field[0]), field[1]])
    backward_x = core == 1
    line_add = jnp.where(backward_x, down_add, up_add)
    line_min = jnp.where(backward_x, down_min, up_min)
    sweep_field = jnp.minimum(incoming[None] + line_add, line_min)

    least_local = jnp.stack([
        jnp.minimum(least0, least1 + cost_x[0]),
        jnp.minimum(least1, least0 + cost_x[1]),
    ])
    merged = jnp.minimum(
        least_local,
        jnp.minimum(up_in[None] + up_add, down_in[None] + down_add),
    )
    return (merged, sweep_field[None])


def solution(mesh):
    placed = (P("slab", None, None), P(None, "slab", None, None), P("slab", None, None), P(), P())
    return jax.shard_map(
        shards,
        mesh=mesh,
        in_specs=placed,
        out_specs=(P("slab", None, None), P("order", "slab", None, None)),
        check_vma=False,
    )
```

```python
import functools

import jax
import jax.numpy as jnp
from jax import lax
from jax.experimental import pallas as pl
from jax.experimental.pallas import tpu as pltpu
from jax.sharding import PartitionSpec as P

ROWS = 8
CHUNK = 32


def scan_step(a, m, k, axis, reverse, last):
    n = a.shape[axis]
    index = lax.broadcasted_iota(jnp.int32, a.shape, axis)
    shift = n - k if reverse else k
    valid = index < n - k if reverse else index >= k
    a_src = pltpu.roll(a, shift, axis)
    m_src = pltpu.roll(m, shift, axis)
    m = jnp.where(valid, jnp.minimum(m_src + a, m), m)
    if not last:
        a = jnp.where(valid, a_src + a, a)
    return a, m


def block_scan(a, m, axis, reverse, need_sum):
    n = a.shape[axis]
    k = 1
    while k < n:
        a, m = scan_step(a, m, k, axis, reverse, last=(2 * k >= n) and not need_sum)
        k *= 2
    return a, m


def local_kernel(flags, stims, stim_times, fibre, tissue, previous, cost_x, field, totals, own,
                 cost_y, *, grid_step):
    planes, cells_y, cells_z = previous.shape
    chunks = cells_y // CHUNK
    inf = jnp.float32(jnp.inf)

    field[...] = previous[...]

    def seed(k, carry):
        p = stims[0, k]
        r = stims[1, k]
        c = stims[2, k]

        @pl.when((p >= 0) & (p < planes))
        def _():
            base = pl.multiple_of(r // ROWS * ROWS, ROWS)
            block = field[p, pl.ds(base, ROWS), :]
            row = lax.broadcasted_iota(jnp.int32, block.shape, 0)
            lane = lax.broadcasted_iota(jnp.int32, block.shape, 1)
            hit = (row == r - base) & (lane == c)
            field[p, pl.ds(base, ROWS), :] = jnp.where(hit, jnp.minimum(block, stim_times[k]), block)

        return carry

    lax.fori_loop(0, stims.shape[1], seed, 0)

    def costs_and_z(reverse):
        def body(i, carry):
            p = i // chunks
            rows = pl.ds(pl.multiple_of((i % chunks) * CHUNK, CHUNK), CHUNK)
            xx = fibre[0, p, rows, :]
            yy = fibre[1, p, rows, :]
            zz = fibre[2, p, rows, :]
            xy = fibre[3, p, rows, :]
            xz = fibre[4, p, rows, :]
            yz = fibre[5, p, rows, :]
            cx = yy * zz - yz * yz
            cy = xx * zz - xz * xz
            cz = xx * yy - xy * xy
            det = xx * cx - xy * (xy * zz - yz * xz) + xz * (xy * yz - yy * xz)
            factor = jnp.where(tissue[p, rows, :] == 1, 1.0, 4.0).astype(jnp.float32) * grid_step
            inverse = 1.0 / det
            cost_x[p, rows, :] = jnp.sqrt(cx * inverse) * factor
            cost_y[p, rows, :] = jnp.sqrt(cy * inverse) * factor
            step_z = jnp.sqrt(cz * inverse) * factor
            _, u = block_scan(step_z, field[p, rows, :], 1, reverse, False)
            field[p, rows, :] = u
            return carry

        lax.fori_loop(0, planes * chunks, body, 0, unroll=2)

    def sweep_y(reverse):
        def body(j, carry):
            i = chunks - 1 - j if reverse else j
            rows = pl.ds(pl.multiple_of(i * CHUNK, CHUNK), CHUNK)
            out = []
            for p in range(planes):
                a, m = block_scan(cost_y[p, rows, :], field[p, rows, :], 0, reverse, True)
                u = jnp.minimum(carry[p] + a, m)
                field[p, rows, :] = u
                edge = u[0:1, :] if reverse else u[CHUNK - 1:CHUNK, :]
                out.append(jnp.broadcast_to(edge, u.shape))
            return tuple(out)

        start = tuple(jnp.full((CHUNK, cells_z), inf, jnp.float32) for _ in range(planes))
        lax.fori_loop(0, chunks, body, start, unroll=2)

    for flag, fn in ((flags[2], costs_and_z), (flags[1], sweep_y)):
        pl.when(flag == 1)(functools.partial(fn, True))
        pl.when(flag != 1)(functools.partial(fn, False))

    def edge(i, carry):
        rows = pl.ds(pl.multiple_of(i * CHUNK, CHUNK), CHUNK)
        c0 = cost_x[0, rows, :]
        c1 = cost_x[1, rows, :]
        u0 = field[0, rows, :]
        u1 = field[1, rows, :]
        down = flags[0] == 1
        totals[0, rows, :] = jnp.where(down, c1 + c0, c0 + c1)
        totals[1, rows, :] = jnp.where(down, jnp.minimum(u1 + c0, u0), jnp.minimum(u0 + c1, u1))
        own[rows, :] = jnp.where(down, u1, u0)
        return carry

    lax.fori_loop(0, chunks, edge, 0)


def local_sweeps(flags, stims, stim_times, fibre, tissue, previous, grid_step):
    planes, cells_y, cells_z = previous.shape
    field = jax.ShapeDtypeStruct(previous.shape, jnp.float32)
    totals = jax.ShapeDtypeStruct((2, cells_y, cells_z), jnp.float32)
    own = jax.ShapeDtypeStruct((cells_y, cells_z), jnp.float32)
    vmem = pl.BlockSpec(memory_space=pltpu.VMEM)
    smem = pl.BlockSpec(memory_space=pltpu.SMEM)
    elements = planes * cells_y * cells_z
    return pl.pallas_call(
        functools.partial(local_kernel, grid_step=grid_step),
        out_shape=(field, field, totals, own),
        in_specs=[smem, smem, smem, vmem, vmem, vmem],
        out_specs=(vmem, vmem, vmem, vmem),
        scratch_shapes=[pltpu.VMEM(previous.shape, jnp.float32)],
        compiler_params=pltpu.CompilerParams(vmem_limit_bytes=48 * 1024 * 1024),
        cost_estimate=pl.CostEstimate(
            flops=300 * elements, transcendentals=6 * elements, bytes_accessed=40 * elements
        ),
    )(flags, stims, stim_times, fibre, tissue, previous)


RELAY_ROWS = 16
LINE = 8


def flip_bits(value, mask, bits):
    out = 0
    for j in range(bits):
        out = out + (2 ** j) * ((value // 2 ** j + (mask >> j) % 2) % 2)
    return out


def relay_kernel(totals, own, cost_x, field, sweep_field, merged, incoming, least_in, least_plane,
                 before, line_total, box1_in, box1_out, box2_in, box2_out, box3_in, box4, box5,
                 swap_in, send1, recv1, send2, recv2, send3, recv3, send4, recv4, send5, recv5,
                 send6, recv6, *, line):
    total_add = totals.at[0]
    total_min = totals.at[1]
    cells_y, cells_z = incoming.shape
    chunks = cells_y // RELAY_ROWS
    slabs = lax.axis_size("slab")
    lines = slabs // line
    half = line // 2
    slab = lax.axis_index("slab")
    group = lax.axis_index("order")
    odd = group % 2
    rank = slab + odd * (slabs - 1 - 2 * slab)
    col = rank // line
    pos = rank % line
    last = line - 1
    mesh_id = pl.DeviceIdType.MESH

    def device(r):
        return (group, r + odd * (slabs - 1 - 2 * r))

    def at(c, p):
        return device(c * line + p)

    orders = lax.axis_size("order")
    masks = list(range(2, orders, 2))
    order_bits = max(orders - 1, 1).bit_length()
    first_col = col == 0
    is_end = pos == last
    in_up = pos < half
    in_down = (pos >= half) & (pos < last)
    up_next = pos + 1 < half
    down_next = pos > half

    barrier = pltpu.get_barrier_semaphore()
    neighbours = []
    neighbours.append((pos > 0, at(col, pos - 1)))
    neighbours.append((pos < last, at(col, pos + 1)))
    neighbours.append(((pos == 0) & (col > 0) & (last > 0), at(col, last)))
    neighbours.append((is_end & (col > 0) & (last > 0), at(col, 0)))
    neighbours.append((is_end & (col > 0), at(col - 1, last)))
    neighbours.append((is_end & (col < lines - 1), at(col + 1, last)))
    for m in masks + [1]:
        neighbours.append((slab >= 0, (flip_bits(group, m, order_bits), slab)))
    count = jnp.int32(0)
    for cond, dev in neighbours:
        @pl.when(cond)
        def _():
            pl.semaphore_signal(barrier, 1, device_id=dev, device_id_type=mesh_id)

        count = count + cond.astype(jnp.int32)
    pl.semaphore_wait(barrier, count)

    def copy1(c):
        return pltpu.make_async_remote_copy(box1_out.at[c], box1_in.at[c], send1.at[c], recv1.at[c],
                                            device_id=at(col, pos + 1), device_id_type=mesh_id)

    def copy2(c):
        return pltpu.make_async_remote_copy(box2_out.at[c], box2_in.at[c], send2.at[c], recv2.at[c],
                                            device_id=at(col + 1, last), device_id_type=mesh_id)

    def copy3_from_end(c, k, target):
        return pltpu.make_async_remote_copy(box2_in.at[c], box3_in.at[c], send3.at[c, k], recv3.at[c],
                                            device_id=target, device_id_type=mesh_id)

    def copy3_relay(c, target):
        return pltpu.make_async_remote_copy(box3_in.at[c], box3_in.at[c], send3.at[c, 0], recv3.at[c],
                                            device_id=target, device_id_type=mesh_id)

    def rows_of(c):
        return pl.ds(pl.multiple_of(c * RELAY_ROWS, RELAY_ROWS), RELAY_ROWS)

    def copy5(k):
        return pltpu.make_async_remote_copy(own, box5.at[k], send5.at[k], recv5.at[k],
                                            device_id=(flip_bits(group, masks[k], order_bits), slab),
                                            device_id_type=mesh_id)

    for k in range(len(masks)):
        copy5(k).start()

    def copy4(c, k):
        return pltpu.make_async_remote_copy(incoming.at[rows_of(c)], box4.at[k, c], send4.at[c, k],
                                            recv4.at[c, k], device_id=(flip_bits(group, masks[k], order_bits), slab),
                                            device_id_type=mesh_id)

    def share(c):
        for k in range(len(masks)):
            copy4(c, k).start()

    def stage1(c, carry):
        rows = rows_of(c)
        own_add = total_add[rows, :]
        own_min = total_min[rows, :]

        @pl.when(pos == 0)
        def _():
            box1_out[c, 0] = own_add
            box1_out[c, 1] = own_min

        @pl.when(pos > 0)
        def _():
            copy1(c).wait_recv()
            got_add = box1_in[c, 0]
            got_min = box1_in[c, 1]
            before[0, rows, :] = got_add
            before[1, rows, :] = got_min
            new_add = got_add + own_add
            new_min = jnp.minimum(got_min + own_add, own_min)

            @pl.when(pos < last)
            def _():
                box1_out[c, 0] = new_add
                box1_out[c, 1] = new_min

            @pl.when(is_end)
            def _():
                line_total[0, rows, :] = new_add
                line_total[1, rows, :] = new_min

        @pl.when((pos == 0) & is_end)
        def _():
            line_total[0, rows, :] = own_add
            line_total[1, rows, :] = own_min

        @pl.when(pos < last)
        def _():
            copy1(c).start()

        return carry

    def stage2(c, carry):
        rows = rows_of(c)

        @pl.when(is_end & first_col)
        def _():
            incoming[rows, :] = jnp.where(pos > 0, before[1, rows, :], jnp.inf)
            share(c)
            box2_out[c] = line_total[1, rows, :]

        @pl.when(is_end & jnp.logical_not(first_col))
        def _():
            copy2(c).wait_recv()
            value = box2_in[c]
            incoming[rows, :] = jnp.where(
                pos > 0, jnp.minimum(value + before[0, rows, :], before[1, rows, :]), value)
            share(c)
            box2_out[c] = jnp.minimum(value + line_total[0, rows, :], line_total[1, rows, :])

            @pl.when(pos > 0)
            def _():
                copy3_from_end(c, 0, at(col, 0)).start()

            @pl.when(half < last)
            def _():
                copy3_from_end(c, 1, at(col, last - 1)).start()

        @pl.when(is_end & (col < lines - 1))
        def _():
            copy2(c).start()

        return carry

    def stages12(c, carry):
        stage1(c, carry)
        return stage2(c, carry)

    lax.fori_loop(0, chunks, stages12, 0)

    def stage3(c, carry):
        rows = rows_of(c)

        @pl.when(first_col & jnp.logical_not(is_end))
        def _():
            incoming[rows, :] = jnp.where(pos > 0, before[1, rows, :], jnp.inf)
            share(c)

        @pl.when(jnp.logical_not(first_col) & (in_up | in_down))
        def _():
            copy3_relay(c, at(col, 0)).wait_recv()
            value = box3_in[c]
            incoming[rows, :] = jnp.where(
                pos > 0, jnp.minimum(value + before[0, rows, :], before[1, rows, :]), value)
            share(c)

            @pl.when(in_up & up_next)
            def _():
                copy3_relay(c, at(col, pos + 1)).start()

            @pl.when(in_down & down_next)
            def _():
                copy3_relay(c, at(col, pos - 1)).start()

        return carry

    lax.fori_loop(0, chunks, stage3, 0)

    def gather(c, carry):
        rows = rows_of(c)
        least = incoming[rows, :]
        for k in range(len(masks)):
            copy4(c, k).wait_recv()
            least = jnp.minimum(least, box4[k, c])
        least_in[rows, :] = least
        return carry

    lax.fori_loop(0, chunks, gather, 0)

    for k in range(len(masks)):
        copy5(k).wait_recv()

    def gather_plane(c, carry):
        rows = rows_of(c)
        least = own[rows, :]
        for k in range(len(masks)):
            least = jnp.minimum(least, box5[k, rows, :])
        least_plane[rows, :] = least
        return carry

    lax.fori_loop(0, chunks, gather_plane, 0)

    swaps = []
    for k, source in enumerate((least_plane, least_in)):
        copy = pltpu.make_async_remote_copy(source, swap_in.at[k], send6.at[k], recv6.at[k],
                                            device_id=(flip_bits(group, 1, order_bits), slab),
                                            device_id_type=mesh_id)
        copy.start()
        swaps.append(copy)
    for copy in swaps:
        copy.wait_recv()

    down = odd == 1

    def finish(c, carry):
        rows = rows_of(c)
        c0 = cost_x[0, rows, :]
        c1 = cost_x[1, rows, :]
        u0 = field[0, rows, :]
        u1 = field[1, rows, :]
        up_add = (c0, c0 + c1)
        down_add = (c1 + c0, c1)
        up_min = (u0, jnp.minimum(u0 + c1, u1))
        down_min = (jnp.minimum(u1 + c0, u0), u1)
        value = incoming[rows, :]
        mine_plane = least_plane[rows, :]
        mine_in = least_in[rows, :]
        other_plane = swap_in[0, rows, :]
        other_in = swap_in[1, rows, :]
        least0 = jnp.where(down, other_plane, mine_plane)
        least1 = jnp.where(down, mine_plane, other_plane)
        up_in = jnp.where(down, other_in, mine_in)
        down_in = jnp.where(down, mine_in, other_in)
        least_local = (jnp.minimum(least0, least1 + c0), jnp.minimum(least1, least0 + c1))
        for p in range(2):
            line_add = jnp.where(down, down_add[p], up_add[p])
            line_min = jnp.where(down, down_min[p], up_min[p])
            sweep_field[0, p, rows, :] = jnp.minimum(value + line_add, line_min)
            merged[p, rows, :] = jnp.minimum(
                least_local[p], jnp.minimum(up_in + up_add[p], down_in + down_add[p]))
        return carry

    lax.fori_loop(0, chunks, finish, 0)

    def drain(c, carry):
        @pl.when(pos < last)
        def _():
            copy1(c).wait_send()

        @pl.when(is_end & (col < lines - 1))
        def _():
            copy2(c).wait_send()

        @pl.when(is_end & jnp.logical_not(first_col) & (pos > 0))
        def _():
            copy3_from_end(c, 0, at(col, 0)).wait_send()

        @pl.when(is_end & jnp.logical_not(first_col) & (half < last))
        def _():
            copy3_from_end(c, 1, at(col, last - 1)).wait_send()

        @pl.when(jnp.logical_not(first_col) & ((in_up & up_next) | (in_down & down_next)))
        def _():
            copy3_relay(c, at(col, 0)).wait_send()

        for k in range(len(masks)):
            copy4(c, k).wait_send()
        return carry

    lax.fori_loop(0, chunks, drain, 0)
    for k in range(len(masks)):
        copy5(k).wait_send()
    for copy in swaps:
        copy.wait_send()


def relay(totals, own, cost_x, field, slabs, orders):
    cells_y, cells_z = own.shape
    chunks = cells_y // RELAY_ROWS
    sharers = len(range(2, orders, 2))
    plane = jax.ShapeDtypeStruct(own.shape, jnp.float32)
    line = LINE if slabs % LINE == 0 else slabs
    vmem = pl.BlockSpec(memory_space=pltpu.VMEM)
    box = pltpu.VMEM((chunks, RELAY_ROWS, cells_z), jnp.float32)
    pair_box = pltpu.VMEM((chunks, 2, RELAY_ROWS, cells_z), jnp.float32)
    return pl.pallas_call(
        functools.partial(relay_kernel, line=line),
        out_shape=(
            jax.ShapeDtypeStruct((1,) + field.shape, jnp.float32),
            jax.ShapeDtypeStruct(field.shape, jnp.float32),
        ),
        in_specs=[vmem, vmem, vmem, vmem],
        out_specs=(vmem, vmem),
        scratch_shapes=[
            pltpu.VMEM((cells_y, cells_z), jnp.float32),
            pltpu.VMEM((cells_y, cells_z), jnp.float32),
            pltpu.VMEM((cells_y, cells_z), jnp.float32),
            pltpu.VMEM((2, cells_y, cells_z), jnp.float32),
            pltpu.VMEM((2, cells_y, cells_z), jnp.float32),
            pair_box,
            pair_box,
            box,
            box,
            box,
            pltpu.VMEM((max(sharers, 1), chunks, RELAY_ROWS, cells_z), jnp.float32),
            pltpu.VMEM((max(sharers, 1), cells_y, cells_z), jnp.float32),
            pltpu.VMEM((2, cells_y, cells_z), jnp.float32),
            pltpu.SemaphoreType.DMA((chunks,)),
            pltpu.SemaphoreType.DMA((chunks,)),
            pltpu.SemaphoreType.DMA((chunks,)),
            pltpu.SemaphoreType.DMA((chunks,)),
            pltpu.SemaphoreType.DMA((chunks, 2)),
            pltpu.SemaphoreType.DMA((chunks,)),
            pltpu.SemaphoreType.DMA((chunks, max(sharers, 1))),
            pltpu.SemaphoreType.DMA((chunks, max(sharers, 1))),
            pltpu.SemaphoreType.DMA((max(sharers, 1),)),
            pltpu.SemaphoreType.DMA((max(sharers, 1),)),
            pltpu.SemaphoreType.DMA((2,)),
            pltpu.SemaphoreType.DMA((2,)),
        ],
        compiler_params=pltpu.CompilerParams(collective_id=0, has_side_effects=True),
    )(totals, own, cost_x, field)


def shards(previous, fibre_tensor, tissue, stim_sites, stim_times):
    planes, cells_y, cells_z = previous.shape
    slabs = lax.axis_size("slab")
    orders = lax.axis_size("order")
    slab_index = lax.axis_index("slab")
    group_index = lax.axis_index("order")
    grid_step = 2.0 / (planes * slabs)

    plane_index = stim_sites // (cells_y * cells_z) - slab_index * planes
    row_index = stim_sites // cells_z % cells_y
    column_index = stim_sites % cells_z
    stims = jnp.stack([plane_index, row_index, column_index]).astype(jnp.int32)

    bits = jnp.stack([group_index % 2, group_index // 2 % 2, group_index // 4 % 2]).astype(jnp.int32)
    cost_x, field, totals, own_plane = local_sweeps(
        bits, stims, stim_times, fibre_tensor, tissue, previous, grid_step)

    sweep_field, merged = relay(totals, own_plane, cost_x, field, slabs, orders)
    return (merged, sweep_field)


def solution(mesh):
    placed = (P("slab", None, None), P(None, "slab", None, None), P("slab", None, None), P(), P())
    return jax.shard_map(
        shards,
        mesh=mesh,
        in_specs=placed,
        out_specs=(P("slab", None, None), P("order", "slab", None, None)),
        check_vma=False,
    )
```

```python
import functools

import jax
import jax.numpy as jnp
from jax import lax
from jax.experimental import pallas as pl
from jax.experimental.pallas import tpu as pltpu
from jax.sharding import PartitionSpec as P

ROWS = 8
CHUNK = 32


def scan_step(a, m, k, axis, reverse, last):
    n = a.shape[axis]
    index = lax.broadcasted_iota(jnp.int32, a.shape, axis)
    shift = n - k if reverse else k
    valid = index < n - k if reverse else index >= k
    a_src = pltpu.roll(a, shift, axis)
    m_src = pltpu.roll(m, shift, axis)
    m = jnp.where(valid, jnp.minimum(m_src + a, m), m)
    if not last:
        a = jnp.where(valid, a_src + a, a)
    return a, m


def block_scan(a, m, axis, reverse, need_sum):
    n = a.shape[axis]
    k = 1
    while k < n:
        a, m = scan_step(a, m, k, axis, reverse, last=(2 * k >= n) and not need_sum)
        k *= 2
    return a, m


def local_kernel(flags, stims, stim_times, fibre, tissue, previous, cost_x, field, totals, own,
                 cost_y, cost_z, *, grid_step):
    planes, cells_y, cells_z = previous.shape
    chunks = cells_y // CHUNK
    inf = jnp.float32(jnp.inf)

    field[...] = previous[...]

    def seed(k, carry):
        p = stims[0, k]
        r = stims[1, k]
        c = stims[2, k]

        @pl.when((p >= 0) & (p < planes))
        def _():
            base = pl.multiple_of(r // ROWS * ROWS, ROWS)
            block = field[p, pl.ds(base, ROWS), :]
            row = lax.broadcasted_iota(jnp.int32, block.shape, 0)
            lane = lax.broadcasted_iota(jnp.int32, block.shape, 1)
            hit = (row == r - base) & (lane == c)
            field[p, pl.ds(base, ROWS), :] = jnp.where(hit, jnp.minimum(block, stim_times[k]), block)

        return carry

    lax.fori_loop(0, stims.shape[1], seed, 0)

    blocks = cells_y // ROWS

    def costs(i, carry):
        p = i // blocks
        rows = pl.ds(pl.multiple_of((i % blocks) * ROWS, ROWS), ROWS)
        xx = fibre[0, p, rows, :]
        yy = fibre[1, p, rows, :]
        zz = fibre[2, p, rows, :]
        xy = fibre[3, p, rows, :]
        xz = fibre[4, p, rows, :]
        yz = fibre[5, p, rows, :]
        cx = yy * zz - yz * yz
        cy = xx * zz - xz * xz
        cz = xx * yy - xy * xy
        det = xx * cx - xy * (xy * zz - yz * xz) + xz * (xy * yz - yy * xz)
        factor = jnp.where(tissue[p, rows, :] == 1, 1.0, 4.0).astype(jnp.float32) * grid_step
        inverse = 1.0 / det
        cost_x[p, rows, :] = jnp.sqrt(cx * inverse) * factor
        cost_y[p, rows, :] = jnp.sqrt(cy * inverse) * factor
        cost_z[p, rows, :] = jnp.sqrt(cz * inverse) * factor
        return carry

    lax.fori_loop(0, planes * blocks, costs, 0, unroll=4)

    def costs_and_z(reverse):
        def body(i, carry):
            p = i // chunks
            rows = pl.ds(pl.multiple_of((i % chunks) * CHUNK, CHUNK), CHUNK)
            _, u = block_scan(cost_z[p, rows, :], field[p, rows, :], 1, reverse, False)
            field[p, rows, :] = u
            return carry

        lax.fori_loop(0, planes * chunks, body, 0)

    def sweep_y(reverse):
        def body(j, carry):
            i = chunks - 1 - j if reverse else j
            rows = pl.ds(pl.multiple_of(i * CHUNK, CHUNK), CHUNK)
            out = []
            for p in range(planes):
                a, m = block_scan(cost_y[p, rows, :], field[p, rows, :], 0, reverse, True)
                u = jnp.minimum(carry[p] + a, m)
                field[p, rows, :] = u
                edge = u[0:1, :] if reverse else u[CHUNK - 1:CHUNK, :]
                out.append(jnp.broadcast_to(edge, u.shape))
            return tuple(out)

        start = tuple(jnp.full((CHUNK, cells_z), inf, jnp.float32) for _ in range(planes))
        lax.fori_loop(0, chunks, body, start)

    for flag, fn in ((flags[2], costs_and_z), (flags[1], sweep_y)):
        pl.when(flag == 1)(functools.partial(fn, True))
        pl.when(flag != 1)(functools.partial(fn, False))

    def edge(i, carry):
        rows = pl.ds(pl.multiple_of(i * CHUNK, CHUNK), CHUNK)
        c0 = cost_x[0, rows, :]
        c1 = cost_x[1, rows, :]
        u0 = field[0, rows, :]
        u1 = field[1, rows, :]
        down = flags[0] == 1
        totals[0, rows, :] = jnp.where(down, c1 + c0, c0 + c1)
        totals[1, rows, :] = jnp.where(down, jnp.minimum(u1 + c0, u0), jnp.minimum(u0 + c1, u1))
        own[rows, :] = jnp.where(down, u1, u0)
        return carry

    lax.fori_loop(0, chunks, edge, 0)


def local_sweeps(flags, stims, stim_times, fibre, tissue, previous, grid_step):
    planes, cells_y, cells_z = previous.shape
    field = jax.ShapeDtypeStruct(previous.shape, jnp.float32)
    totals = jax.ShapeDtypeStruct((2, cells_y, cells_z), jnp.float32)
    own = jax.ShapeDtypeStruct((cells_y, cells_z), jnp.float32)
    vmem = pl.BlockSpec(memory_space=pltpu.VMEM)
    smem = pl.BlockSpec(memory_space=pltpu.SMEM)
    elements = planes * cells_y * cells_z
    return pl.pallas_call(
        functools.partial(local_kernel, grid_step=grid_step),
        out_shape=(field, field, totals, own),
        in_specs=[smem, smem, smem, vmem, vmem, vmem],
        out_specs=(vmem, vmem, vmem, vmem),
        scratch_shapes=[pltpu.VMEM(previous.shape, jnp.float32), pltpu.VMEM(previous.shape, jnp.float32)],
        compiler_params=pltpu.CompilerParams(vmem_limit_bytes=48 * 1024 * 1024),
        cost_estimate=pl.CostEstimate(
            flops=300 * elements, transcendentals=6 * elements, bytes_accessed=40 * elements
        ),
    )(flags, stims, stim_times, fibre, tissue, previous)


RELAY_ROWS = 16
LINE = 8


def flip_bits(value, mask, bits):
    out = 0
    for j in range(bits):
        out = out + (2 ** j) * ((value // 2 ** j + (mask >> j) % 2) % 2)
    return out


def relay_kernel(totals, own, incoming, least_in, least_plane, before, line_total, box1_in,
                 box1_out, box2_in, box2_out, box3_in, box4, box5, send1, recv1, send2, recv2, send3,
                 recv3, send4, recv4, send5, recv5, *, line):
    total_add = totals.at[0]
    total_min = totals.at[1]
    cells_y, cells_z = incoming.shape
    chunks = cells_y // RELAY_ROWS
    slabs = lax.axis_size("slab")
    lines = slabs // line
    half = line // 2
    slab = lax.axis_index("slab")
    group = lax.axis_index("order")
    odd = group % 2
    rank = slab + odd * (slabs - 1 - 2 * slab)
    col = rank // line
    pos = rank % line
    last = line - 1
    mesh_id = pl.DeviceIdType.MESH

    def device(r):
        return (group, r + odd * (slabs - 1 - 2 * r))

    def at(c, p):
        return device(c * line + p)

    orders = lax.axis_size("order")
    masks = list(range(2, orders, 2))
    order_bits = max(orders - 1, 1).bit_length()
    first_col = col == 0
    is_end = pos == last
    in_up = pos < half
    in_down = (pos >= half) & (pos < last)
    up_next = pos + 1 < half
    down_next = pos > half

    barrier = pltpu.get_barrier_semaphore()
    neighbours = []
    neighbours.append((pos > 0, at(col, pos - 1)))
    neighbours.append((pos < last, at(col, pos + 1)))
    neighbours.append(((pos == 0) & (col > 0) & (last > 0), at(col, last)))
    neighbours.append((is_end & (col > 0) & (last > 0), at(col, 0)))
    neighbours.append((is_end & (col > 0), at(col - 1, last)))
    neighbours.append((is_end & (col < lines - 1), at(col + 1, last)))
    for m in masks:
        neighbours.append((slab >= 0, (flip_bits(group, m, order_bits), slab)))
    count = jnp.int32(0)
    for cond, dev in neighbours:
        @pl.when(cond)
        def _():
            pl.semaphore_signal(barrier, 1, device_id=dev, device_id_type=mesh_id)

        count = count + cond.astype(jnp.int32)
    pl.semaphore_wait(barrier, count)

    def copy1(c):
        return pltpu.make_async_remote_copy(box1_out.at[c], box1_in.at[c], send1.at[c], recv1.at[c],
                                            device_id=at(col, pos + 1), device_id_type=mesh_id)

    def copy2(c):
        return pltpu.make_async_remote_copy(box2_out.at[c], box2_in.at[c], send2.at[c], recv2.at[c],
                                            device_id=at(col + 1, last), device_id_type=mesh_id)

    def copy3_from_end(c, k, target):
        return pltpu.make_async_remote_copy(box2_in.at[c], box3_in.at[c], send3.at[c, k], recv3.at[c],
                                            device_id=target, device_id_type=mesh_id)

    def copy3_relay(c, target):
        return pltpu.make_async_remote_copy(box3_in.at[c], box3_in.at[c], send3.at[c, 0], recv3.at[c],
                                            device_id=target, device_id_type=mesh_id)

    def rows_of(c):
        return pl.ds(pl.multiple_of(c * RELAY_ROWS, RELAY_ROWS), RELAY_ROWS)

    def copy5(k):
        return pltpu.make_async_remote_copy(own, box5.at[k], send5.at[k], recv5.at[k],
                                            device_id=(flip_bits(group, masks[k], order_bits), slab),
                                            device_id_type=mesh_id)

    for k in range(len(masks)):
        copy5(k).start()

    def copy4(c, k):
        return pltpu.make_async_remote_copy(incoming.at[rows_of(c)], box4.at[k, c], send4.at[c, k],
                                            recv4.at[c, k], device_id=(flip_bits(group, masks[k], order_bits), slab),
                                            device_id_type=mesh_id)

    def share(c):
        for k in range(len(masks)):
            copy4(c, k).start()

    def stage1(c, carry):
        rows = rows_of(c)
        own_add = total_add[rows, :]
        own_min = total_min[rows, :]

        @pl.when(pos == 0)
        def _():
            box1_out[c, 0] = own_add
            box1_out[c, 1] = own_min

        @pl.when(pos > 0)
        def _():
            copy1(c).wait_recv()
            got_add = box1_in[c, 0]
            got_min = box1_in[c, 1]
            before[0, rows, :] = got_add
            before[1, rows, :] = got_min
            new_add = got_add + own_add
            new_min = jnp.minimum(got_min + own_add, own_min)

            @pl.when(pos < last)
            def _():
                box1_out[c, 0] = new_add
                box1_out[c, 1] = new_min

            @pl.when(is_end)
            def _():
                line_total[0, rows, :] = new_add
                line_total[1, rows, :] = new_min

        @pl.when((pos == 0) & is_end)
        def _():
            line_total[0, rows, :] = own_add
            line_total[1, rows, :] = own_min

        @pl.when(pos < last)
        def _():
            copy1(c).start()

        return carry

    def stage2(c, carry):
        rows = rows_of(c)

        @pl.when(is_end & first_col)
        def _():
            incoming[rows, :] = jnp.where(pos > 0, before[1, rows, :], jnp.inf)
            share(c)
            box2_out[c] = line_total[1, rows, :]

        @pl.when(is_end & jnp.logical_not(first_col))
        def _():
            copy2(c).wait_recv()
            value = box2_in[c]
            incoming[rows, :] = jnp.where(
                pos > 0, jnp.minimum(value + before[0, rows, :], before[1, rows, :]), value)
            share(c)
            box2_out[c] = jnp.minimum(value + line_total[0, rows, :], line_total[1, rows, :])

            @pl.when(pos > 0)
            def _():
                copy3_from_end(c, 0, at(col, 0)).start()

            @pl.when(half < last)
            def _():
                copy3_from_end(c, 1, at(col, last - 1)).start()

        @pl.when(is_end & (col < lines - 1))
        def _():
            copy2(c).start()

        return carry

    def stages12(c, carry):
        stage1(c, carry)
        return stage2(c, carry)

    lax.fori_loop(0, chunks, stages12, 0)

    def stage3(c, carry):
        rows = rows_of(c)

        @pl.when(first_col & jnp.logical_not(is_end))
        def _():
            incoming[rows, :] = jnp.where(pos > 0, before[1, rows, :], jnp.inf)
            share(c)

        @pl.when(jnp.logical_not(first_col) & (in_up | in_down))
        def _():
            copy3_relay(c, at(col, 0)).wait_recv()
            value = box3_in[c]
            incoming[rows, :] = jnp.where(
                pos > 0, jnp.minimum(value + before[0, rows, :], before[1, rows, :]), value)
            share(c)

            @pl.when(in_up & up_next)
            def _():
                copy3_relay(c, at(col, pos + 1)).start()

            @pl.when(in_down & down_next)
            def _():
                copy3_relay(c, at(col, pos - 1)).start()

        return carry

    lax.fori_loop(0, chunks, stage3, 0)

    def gather(c, carry):
        rows = rows_of(c)
        least = incoming[rows, :]
        for k in range(len(masks)):
            copy4(c, k).wait_recv()
            least = jnp.minimum(least, box4[k, c])
        least_in[rows, :] = least
        return carry

    lax.fori_loop(0, chunks, gather, 0)

    for k in range(len(masks)):
        copy5(k).wait_recv()

    def gather_plane(c, carry):
        rows = rows_of(c)
        least = own[rows, :]
        for k in range(len(masks)):
            least = jnp.minimum(least, box5[k, rows, :])
        least_plane[rows, :] = least
        return carry

    lax.fori_loop(0, chunks, gather_plane, 0)

    def drain(c, carry):
        @pl.when(pos < last)
        def _():
            copy1(c).wait_send()

        @pl.when(is_end & (col < lines - 1))
        def _():
            copy2(c).wait_send()

        @pl.when(is_end & jnp.logical_not(first_col) & (pos > 0))
        def _():
            copy3_from_end(c, 0, at(col, 0)).wait_send()

        @pl.when(is_end & jnp.logical_not(first_col) & (half < last))
        def _():
            copy3_from_end(c, 1, at(col, last - 1)).wait_send()

        @pl.when(jnp.logical_not(first_col) & ((in_up & up_next) | (in_down & down_next)))
        def _():
            copy3_relay(c, at(col, 0)).wait_send()

        for k in range(len(masks)):
            copy4(c, k).wait_send()
        return carry

    lax.fori_loop(0, chunks, drain, 0)
    for k in range(len(masks)):
        copy5(k).wait_send()


def relay(totals, own, slabs, orders):
    cells_y, cells_z = own.shape
    chunks = cells_y // RELAY_ROWS
    sharers = len(range(2, orders, 2))
    plane = jax.ShapeDtypeStruct(own.shape, jnp.float32)
    line = LINE if slabs % LINE == 0 else slabs
    vmem = pl.BlockSpec(memory_space=pltpu.VMEM)
    box = pltpu.VMEM((chunks, RELAY_ROWS, cells_z), jnp.float32)
    pair_box = pltpu.VMEM((chunks, 2, RELAY_ROWS, cells_z), jnp.float32)
    return pl.pallas_call(
        functools.partial(relay_kernel, line=line),
        out_shape=(plane, plane, plane),
        in_specs=[vmem, vmem],
        out_specs=(vmem, vmem, vmem),
        scratch_shapes=[
            pltpu.VMEM((2, cells_y, cells_z), jnp.float32),
            pltpu.VMEM((2, cells_y, cells_z), jnp.float32),
            pair_box,
            pair_box,
            box,
            box,
            box,
            pltpu.VMEM((max(sharers, 1), chunks, RELAY_ROWS, cells_z), jnp.float32),
            pltpu.VMEM((max(sharers, 1), cells_y, cells_z), jnp.float32),
            pltpu.SemaphoreType.DMA((chunks,)),
            pltpu.SemaphoreType.DMA((chunks,)),
            pltpu.SemaphoreType.DMA((chunks,)),
            pltpu.SemaphoreType.DMA((chunks,)),
            pltpu.SemaphoreType.DMA((chunks, 2)),
            pltpu.SemaphoreType.DMA((chunks,)),
            pltpu.SemaphoreType.DMA((chunks, max(sharers, 1))),
            pltpu.SemaphoreType.DMA((chunks, max(sharers, 1))),
            pltpu.SemaphoreType.DMA((max(sharers, 1),)),
            pltpu.SemaphoreType.DMA((max(sharers, 1),)),
        ],
        compiler_params=pltpu.CompilerParams(collective_id=0, has_side_effects=True),
    )(totals, own)


def shards(previous, fibre_tensor, tissue, stim_sites, stim_times):
    planes, cells_y, cells_z = previous.shape
    slabs = lax.axis_size("slab")
    orders = lax.axis_size("order")
    slab_index = lax.axis_index("slab")
    group_index = lax.axis_index("order")
    grid_step = 2.0 / (planes * slabs)

    plane_index = stim_sites // (cells_y * cells_z) - slab_index * planes
    row_index = stim_sites // cells_z % cells_y
    column_index = stim_sites % cells_z
    stims = jnp.stack([plane_index, row_index, column_index]).astype(jnp.int32)

    bits = jnp.stack([group_index % 2, group_index // 2 % 2, group_index // 4 % 2]).astype(jnp.int32)
    cost_x, field, totals, own_plane = local_sweeps(
        bits, stims, stim_times, fibre_tensor, tissue, previous, grid_step)

    core = group_index % 2
    incoming, least_in, least_plane = relay(totals, own_plane, slabs, orders)
    other = lax.ppermute(jnp.stack([least_plane, least_in]), "order", [(g, g ^ 1) for g in range(orders)])

    least0 = jnp.where(core == 0, least_plane, other[0])
    least1 = jnp.where(core == 0, other[0], least_plane)
    up_in = jnp.where(core == 0, least_in, other[1])
    down_in = jnp.where(core == 0, other[1], least_in)

    up_add = jnp.stack([cost_x[0], cost_x[0] + cost_x[1]])
    up_min = jnp.stack([field[0], jnp.minimum(field[0] + cost_x[1], field[1])])
    down_add = jnp.stack([cost_x[1] + cost_x[0], cost_x[1]])
    down_min = jnp.stack([jnp.minimum(field[1] + cost_x[0], field[0]), field[1]])
    backward_x = core == 1
    line_add = jnp.where(backward_x, down_add, up_add)
    line_min = jnp.where(backward_x, down_min, up_min)
    sweep_field = jnp.minimum(incoming[None] + line_add, line_min)

    least_local = jnp.stack([
        jnp.minimum(least0, least1 + cost_x[0]),
        jnp.minimum(least1, least0 + cost_x[1]),
    ])
    merged = jnp.minimum(
        least_local,
        jnp.minimum(up_in[None] + up_add, down_in[None] + down_add),
    )
    return (merged, sweep_field[None])


def solution(mesh):
    placed = (P("slab", None, None), P(None, "slab", None, None), P("slab", None, None), P(), P())
    return jax.shard_map(
        shards,
        mesh=mesh,
        in_specs=placed,
        out_specs=(P("slab", None, None), P("order", "slab", None, None)),
        check_vma=False,
    )
```

```python
import functools

import jax
import jax.numpy as jnp
from jax import lax
from jax.experimental import pallas as pl
from jax.experimental.pallas import tpu as pltpu
from jax.sharding import PartitionSpec as P

ROWS = 8
CHUNK = 32


def scan_step(a, m, k, axis, reverse, last):
    n = a.shape[axis]
    index = lax.broadcasted_iota(jnp.int32, a.shape, axis)
    shift = n - k if reverse else k
    valid = index < n - k if reverse else index >= k
    a_src = pltpu.roll(a, shift, axis)
    m_src = pltpu.roll(m, shift, axis)
    m = jnp.where(valid, jnp.minimum(m_src + a, m), m)
    if not last:
        a = jnp.where(valid, a_src + a, a)
    return a, m


def block_scan(a, m, axis, reverse, need_sum):
    n = a.shape[axis]
    k = 1
    while k < n:
        a, m = scan_step(a, m, k, axis, reverse, last=(2 * k >= n) and not need_sum)
        k *= 2
    return a, m


def lane_scan(step, seeded, reverse):
    width = step.shape[1]
    if width % 128 or width == 128:
        return block_scan(step, seeded, 1, reverse, False)[1]
    parts = []
    for i in range(width // 128):
        lanes = slice(i * 128, (i + 1) * 128)
        parts.append(block_scan(step[:, lanes], seeded[:, lanes], 1, reverse, True))
    order = range(len(parts) - 1, -1, -1) if reverse else range(len(parts))
    carry = None
    out = [None] * len(parts)
    for i in order:
        a, m = parts[i]
        if carry is not None:
            m = jnp.minimum(carry + a, m)
        edge = m[:, 0:1] if reverse else m[:, 127:128]
        carry = jnp.broadcast_to(edge, m.shape)
        out[i] = m
    return jnp.concatenate(out, axis=1)


def local_kernel(flags, stims, stim_times, fibre, tissue, previous, cost_x, field, totals, own,
                 cost_y, *, grid_step):
    planes, cells_y, cells_z = previous.shape
    chunks = cells_y // CHUNK
    inf = jnp.float32(jnp.inf)

    field[...] = previous[...]

    def seed(k, carry):
        p = stims[0, k]
        r = stims[1, k]
        c = stims[2, k]

        @pl.when((p >= 0) & (p < planes))
        def _():
            base = pl.multiple_of(r // ROWS * ROWS, ROWS)
            block = field[p, pl.ds(base, ROWS), :]
            row = lax.broadcasted_iota(jnp.int32, block.shape, 0)
            lane = lax.broadcasted_iota(jnp.int32, block.shape, 1)
            hit = (row == r - base) & (lane == c)
            field[p, pl.ds(base, ROWS), :] = jnp.where(hit, jnp.minimum(block, stim_times[k]), block)

        return carry

    lax.fori_loop(0, stims.shape[1], seed, 0)

    def costs_and_z(reverse):
        def body(i, carry):
            p = i // chunks
            rows = pl.ds(pl.multiple_of((i % chunks) * CHUNK, CHUNK), CHUNK)
            xx = fibre[0, p, rows, :]
            yy = fibre[1, p, rows, :]
            zz = fibre[2, p, rows, :]
            xy = fibre[3, p, rows, :]
            xz = fibre[4, p, rows, :]
            yz = fibre[5, p, rows, :]
            cx = yy * zz - yz * yz
            cy = xx * zz - xz * xz
            cz = xx * yy - xy * xy
            det = xx * cx - xy * (xy * zz - yz * xz) + xz * (xy * yz - yy * xz)
            factor = jnp.where(tissue[p, rows, :] == 1, 1.0, 4.0).astype(jnp.float32) * grid_step
            inverse = 1.0 / det
            cost_x[p, rows, :] = jnp.sqrt(cx * inverse) * factor
            cost_y[p, rows, :] = jnp.sqrt(cy * inverse) * factor
            step_z = jnp.sqrt(cz * inverse) * factor
            u = lane_scan(step_z, field[p, rows, :], reverse)
            field[p, rows, :] = u
            return carry

        lax.fori_loop(0, planes * chunks, body, 0, unroll=2)

    def sweep_y(reverse):
        def body(j, carry):
            i = chunks - 1 - j if reverse else j
            rows = pl.ds(pl.multiple_of(i * CHUNK, CHUNK), CHUNK)
            out = []
            for p in range(planes):
                a, m = block_scan(cost_y[p, rows, :], field[p, rows, :], 0, reverse, True)
                u = jnp.minimum(carry[p] + a, m)
                field[p, rows, :] = u
                edge = u[0:1, :] if reverse else u[CHUNK - 1:CHUNK, :]
                out.append(jnp.broadcast_to(edge, u.shape))
            return tuple(out)

        start = tuple(jnp.full((CHUNK, cells_z), inf, jnp.float32) for _ in range(planes))
        lax.fori_loop(0, chunks, body, start, unroll=2)

    for flag, fn in ((flags[2], costs_and_z), (flags[1], sweep_y)):
        pl.when(flag == 1)(functools.partial(fn, True))
        pl.when(flag != 1)(functools.partial(fn, False))

    def edge(i, carry):
        rows = pl.ds(pl.multiple_of(i * CHUNK, CHUNK), CHUNK)
        c0 = cost_x[0, rows, :]
        c1 = cost_x[1, rows, :]
        u0 = field[0, rows, :]
        u1 = field[1, rows, :]
        down = flags[0] == 1
        totals[0, rows, :] = jnp.where(down, c1 + c0, c0 + c1)
        totals[1, rows, :] = jnp.where(down, jnp.minimum(u1 + c0, u0), jnp.minimum(u0 + c1, u1))
        own[rows, :] = jnp.where(down, u1, u0)
        return carry

    lax.fori_loop(0, chunks, edge, 0)


def local_sweeps(flags, stims, stim_times, fibre, tissue, previous, grid_step):
    planes, cells_y, cells_z = previous.shape
    field = jax.ShapeDtypeStruct(previous.shape, jnp.float32)
    totals = jax.ShapeDtypeStruct((2, cells_y, cells_z), jnp.float32)
    own = jax.ShapeDtypeStruct((cells_y, cells_z), jnp.float32)
    vmem = pl.BlockSpec(memory_space=pltpu.VMEM)
    smem = pl.BlockSpec(memory_space=pltpu.SMEM)
    elements = planes * cells_y * cells_z
    return pl.pallas_call(
        functools.partial(local_kernel, grid_step=grid_step),
        out_shape=(field, field, totals, own),
        in_specs=[smem, smem, smem, vmem, vmem, vmem],
        out_specs=(vmem, vmem, vmem, vmem),
        scratch_shapes=[pltpu.VMEM(previous.shape, jnp.float32)],
        compiler_params=pltpu.CompilerParams(vmem_limit_bytes=48 * 1024 * 1024),
        cost_estimate=pl.CostEstimate(
            flops=300 * elements, transcendentals=6 * elements, bytes_accessed=40 * elements
        ),
    )(flags, stims, stim_times, fibre, tissue, previous)


RELAY_ROWS = 16
LINE = 8


def flip_bits(value, mask, bits):
    out = 0
    for j in range(bits):
        out = out + (2 ** j) * ((value // 2 ** j + (mask >> j) % 2) % 2)
    return out


def relay_kernel(totals, own, incoming, least_in, least_plane, before, line_total, box1_in,
                 box1_out, box2_in, box2_out, box3_in, box4, box5, send1, recv1, send2, recv2, send3,
                 recv3, send4, recv4, send5, recv5, *, line):
    total_add = totals.at[0]
    total_min = totals.at[1]
    cells_y, cells_z = incoming.shape
    chunks = cells_y // RELAY_ROWS
    slabs = lax.axis_size("slab")
    lines = slabs // line
    half = line // 2
    slab = lax.axis_index("slab")
    group = lax.axis_index("order")
    odd = group % 2
    rank = slab + odd * (slabs - 1 - 2 * slab)
    col = rank // line
    pos = rank % line
    last = line - 1
    mesh_id = pl.DeviceIdType.MESH

    def device(r):
        return (group, r + odd * (slabs - 1 - 2 * r))

    def at(c, p):
        return device(c * line + p)

    orders = lax.axis_size("order")
    masks = list(range(2, orders, 2))
    order_bits = max(orders - 1, 1).bit_length()
    first_col = col == 0
    is_end = pos == last
    in_up = pos < half
    in_down = (pos >= half) & (pos < last)
    up_next = pos + 1 < half
    down_next = pos > half

    barrier = pltpu.get_barrier_semaphore()
    neighbours = []
    neighbours.append((pos > 0, at(col, pos - 1)))
    neighbours.append((pos < last, at(col, pos + 1)))
    neighbours.append(((pos == 0) & (col > 0) & (last > 0), at(col, last)))
    neighbours.append((is_end & (col > 0) & (last > 0), at(col, 0)))
    neighbours.append((is_end & (col > 0), at(col - 1, last)))
    neighbours.append((is_end & (col < lines - 1), at(col + 1, last)))
    for m in masks:
        neighbours.append((slab >= 0, (flip_bits(group, m, order_bits), slab)))
    count = jnp.int32(0)
    for cond, dev in neighbours:
        @pl.when(cond)
        def _():
            pl.semaphore_signal(barrier, 1, device_id=dev, device_id_type=mesh_id)

        count = count + cond.astype(jnp.int32)
    pl.semaphore_wait(barrier, count)

    def copy1(c):
        return pltpu.make_async_remote_copy(box1_out.at[c], box1_in.at[c], send1.at[c], recv1.at[c],
                                            device_id=at(col, pos + 1), device_id_type=mesh_id)

    def copy2(c):
        return pltpu.make_async_remote_copy(box2_out.at[c], box2_in.at[c], send2.at[c], recv2.at[c],
                                            device_id=at(col + 1, last), device_id_type=mesh_id)

    def copy3_from_end(c, k, target):
        return pltpu.make_async_remote_copy(box2_in.at[c], box3_in.at[c], send3.at[c, k], recv3.at[c],
                                            device_id=target, device_id_type=mesh_id)

    def copy3_relay(c, target):
        return pltpu.make_async_remote_copy(box3_in.at[c], box3_in.at[c], send3.at[c, 0], recv3.at[c],
                                            device_id=target, device_id_type=mesh_id)

    def rows_of(c):
        return pl.ds(pl.multiple_of(c * RELAY_ROWS, RELAY_ROWS), RELAY_ROWS)

    def copy5(k):
        return pltpu.make_async_remote_copy(own, box5.at[k], send5.at[k], recv5.at[k],
                                            device_id=(flip_bits(group, masks[k], order_bits), slab),
                                            device_id_type=mesh_id)

    for k in range(len(masks)):
        copy5(k).start()

    def copy4(c, k):
        return pltpu.make_async_remote_copy(incoming.at[rows_of(c)], box4.at[k, c], send4.at[c, k],
                                            recv4.at[c, k], device_id=(flip_bits(group, masks[k], order_bits), slab),
                                            device_id_type=mesh_id)

    def share(c):
        for k in range(len(masks)):
            copy4(c, k).start()

    def stage1(c, carry):
        rows = rows_of(c)
        own_add = total_add[rows, :]
        own_min = total_min[rows, :]

        @pl.when(pos == 0)
        def _():
            box1_out[c, 0] = own_add
            box1_out[c, 1] = own_min

        @pl.when(pos > 0)
        def _():
            copy1(c).wait_recv()
            got_add = box1_in[c, 0]
            got_min = box1_in[c, 1]
            before[0, rows, :] = got_add
            before[1, rows, :] = got_min
            new_add = got_add + own_add
            new_min = jnp.minimum(got_min + own_add, own_min)

            @pl.when(pos < last)
            def _():
                box1_out[c, 0] = new_add
                box1_out[c, 1] = new_min

            @pl.when(is_end)
            def _():
                line_total[0, rows, :] = new_add
                line_total[1, rows, :] = new_min

        @pl.when((pos == 0) & is_end)
        def _():
            line_total[0, rows, :] = own_add
            line_total[1, rows, :] = own_min

        @pl.when(pos < last)
        def _():
            copy1(c).start()

        return carry

    def stage2(c, carry):
        rows = rows_of(c)

        @pl.when(is_end & first_col)
        def _():
            incoming[rows, :] = jnp.where(pos > 0, before[1, rows, :], jnp.inf)
            share(c)
            box2_out[c] = line_total[1, rows, :]

        @pl.when(is_end & jnp.logical_not(first_col))
        def _():
            copy2(c).wait_recv()
            value = box2_in[c]
            incoming[rows, :] = jnp.where(
                pos > 0, jnp.minimum(value + before[0, rows, :], before[1, rows, :]), value)
            share(c)
            box2_out[c] = jnp.minimum(value + line_total[0, rows, :], line_total[1, rows, :])

            @pl.when(pos > 0)
            def _():
                copy3_from_end(c, 0, at(col, 0)).start()

            @pl.when(half < last)
            def _():
                copy3_from_end(c, 1, at(col, last - 1)).start()

        @pl.when(is_end & (col < lines - 1))
        def _():
            copy2(c).start()

        return carry

    def stages12(c, carry):
        stage1(c, carry)
        return stage2(c, carry)

    lax.fori_loop(0, chunks, stages12, 0)

    def stage3(c, carry):
        rows = rows_of(c)

        @pl.when(first_col & jnp.logical_not(is_end))
        def _():
            incoming[rows, :] = jnp.where(pos > 0, before[1, rows, :], jnp.inf)
            share(c)

        @pl.when(jnp.logical_not(first_col) & (in_up | in_down))
        def _():
            copy3_relay(c, at(col, 0)).wait_recv()
            value = box3_in[c]
            incoming[rows, :] = jnp.where(
                pos > 0, jnp.minimum(value + before[0, rows, :], before[1, rows, :]), value)
            share(c)

            @pl.when(in_up & up_next)
            def _():
                copy3_relay(c, at(col, pos + 1)).start()

            @pl.when(in_down & down_next)
            def _():
                copy3_relay(c, at(col, pos - 1)).start()

        return carry

    lax.fori_loop(0, chunks, stage3, 0)

    def gather(c, carry):
        rows = rows_of(c)
        least = incoming[rows, :]
        for k in range(len(masks)):
            copy4(c, k).wait_recv()
            least = jnp.minimum(least, box4[k, c])
        least_in[rows, :] = least
        return carry

    lax.fori_loop(0, chunks, gather, 0)

    for k in range(len(masks)):
        copy5(k).wait_recv()

    def gather_plane(c, carry):
        rows = rows_of(c)
        least = own[rows, :]
        for k in range(len(masks)):
            least = jnp.minimum(least, box5[k, rows, :])
        least_plane[rows, :] = least
        return carry

    lax.fori_loop(0, chunks, gather_plane, 0)

    def drain(c, carry):
        @pl.when(pos < last)
        def _():
            copy1(c).wait_send()

        @pl.when(is_end & (col < lines - 1))
        def _():
            copy2(c).wait_send()

        @pl.when(is_end & jnp.logical_not(first_col) & (pos > 0))
        def _():
            copy3_from_end(c, 0, at(col, 0)).wait_send()

        @pl.when(is_end & jnp.logical_not(first_col) & (half < last))
        def _():
            copy3_from_end(c, 1, at(col, last - 1)).wait_send()

        @pl.when(jnp.logical_not(first_col) & ((in_up & up_next) | (in_down & down_next)))
        def _():
            copy3_relay(c, at(col, 0)).wait_send()

        for k in range(len(masks)):
            copy4(c, k).wait_send()
        return carry

    lax.fori_loop(0, chunks, drain, 0)
    for k in range(len(masks)):
        copy5(k).wait_send()


def relay(totals, own, slabs, orders):
    cells_y, cells_z = own.shape
    chunks = cells_y // RELAY_ROWS
    sharers = len(range(2, orders, 2))
    plane = jax.ShapeDtypeStruct(own.shape, jnp.float32)
    line = LINE if slabs % LINE == 0 else slabs
    vmem = pl.BlockSpec(memory_space=pltpu.VMEM)
    box = pltpu.VMEM((chunks, RELAY_ROWS, cells_z), jnp.float32)
    pair_box = pltpu.VMEM((chunks, 2, RELAY_ROWS, cells_z), jnp.float32)
    return pl.pallas_call(
        functools.partial(relay_kernel, line=line),
        out_shape=(plane, plane, plane),
        in_specs=[vmem, vmem],
        out_specs=(vmem, vmem, vmem),
        scratch_shapes=[
            pltpu.VMEM((2, cells_y, cells_z), jnp.float32),
            pltpu.VMEM((2, cells_y, cells_z), jnp.float32),
            pair_box,
            pair_box,
            box,
            box,
            box,
            pltpu.VMEM((max(sharers, 1), chunks, RELAY_ROWS, cells_z), jnp.float32),
            pltpu.VMEM((max(sharers, 1), cells_y, cells_z), jnp.float32),
            pltpu.SemaphoreType.DMA((chunks,)),
            pltpu.SemaphoreType.DMA((chunks,)),
            pltpu.SemaphoreType.DMA((chunks,)),
            pltpu.SemaphoreType.DMA((chunks,)),
            pltpu.SemaphoreType.DMA((chunks, 2)),
            pltpu.SemaphoreType.DMA((chunks,)),
            pltpu.SemaphoreType.DMA((chunks, max(sharers, 1))),
            pltpu.SemaphoreType.DMA((chunks, max(sharers, 1))),
            pltpu.SemaphoreType.DMA((max(sharers, 1),)),
            pltpu.SemaphoreType.DMA((max(sharers, 1),)),
        ],
        compiler_params=pltpu.CompilerParams(collective_id=0, has_side_effects=True),
    )(totals, own)


def shards(previous, fibre_tensor, tissue, stim_sites, stim_times):
    planes, cells_y, cells_z = previous.shape
    slabs = lax.axis_size("slab")
    orders = lax.axis_size("order")
    slab_index = lax.axis_index("slab")
    group_index = lax.axis_index("order")
    grid_step = 2.0 / (planes * slabs)

    plane_index = stim_sites // (cells_y * cells_z) - slab_index * planes
    row_index = stim_sites // cells_z % cells_y
    column_index = stim_sites % cells_z
    stims = jnp.stack([plane_index, row_index, column_index]).astype(jnp.int32)

    bits = jnp.stack([group_index % 2, group_index // 2 % 2, group_index // 4 % 2]).astype(jnp.int32)
    cost_x, field, totals, own_plane = local_sweeps(
        bits, stims, stim_times, fibre_tensor, tissue, previous, grid_step)

    core = group_index % 2
    incoming, least_in, least_plane = relay(totals, own_plane, slabs, orders)
    other = lax.ppermute(jnp.stack([least_plane, least_in]), "order", [(g, g ^ 1) for g in range(orders)])

    least0 = jnp.where(core == 0, least_plane, other[0])
    least1 = jnp.where(core == 0, other[0], least_plane)
    up_in = jnp.where(core == 0, least_in, other[1])
    down_in = jnp.where(core == 0, other[1], least_in)

    up_add = jnp.stack([cost_x[0], cost_x[0] + cost_x[1]])
    up_min = jnp.stack([field[0], jnp.minimum(field[0] + cost_x[1], field[1])])
    down_add = jnp.stack([cost_x[1] + cost_x[0], cost_x[1]])
    down_min = jnp.stack([jnp.minimum(field[1] + cost_x[0], field[0]), field[1]])
    backward_x = core == 1
    line_add = jnp.where(backward_x, down_add, up_add)
    line_min = jnp.where(backward_x, down_min, up_min)
    sweep_field = jnp.minimum(incoming[None] + line_add, line_min)

    least_local = jnp.stack([
        jnp.minimum(least0, least1 + cost_x[0]),
        jnp.minimum(least1, least0 + cost_x[1]),
    ])
    merged = jnp.minimum(
        least_local,
        jnp.minimum(up_in[None] + up_add, down_in[None] + down_add),
    )
    return (merged, sweep_field[None])


def solution(mesh):
    placed = (P("slab", None, None), P(None, "slab", None, None), P("slab", None, None), P(), P())
    return jax.shard_map(
        shards,
        mesh=mesh,
        in_specs=placed,
        out_specs=(P("slab", None, None), P("order", "slab", None, None)),
        check_vma=False,
    )
```

```python
import functools

import jax
import jax.numpy as jnp
from jax import lax
from jax.experimental import pallas as pl
from jax.experimental.pallas import tpu as pltpu
from jax.sharding import PartitionSpec as P

ROWS = 8
CHUNK = 32


def scan_step(a, m, k, axis, reverse, last):
    n = a.shape[axis]
    index = lax.broadcasted_iota(jnp.int32, a.shape, axis)
    shift = n - k if reverse else k
    valid = index < n - k if reverse else index >= k
    a_src = pltpu.roll(a, shift, axis)
    m_src = pltpu.roll(m, shift, axis)
    m = jnp.where(valid, jnp.minimum(m_src + a, m), m)
    if not last:
        a = jnp.where(valid, a_src + a, a)
    return a, m


def block_scan(a, m, axis, reverse, need_sum):
    n = a.shape[axis]
    k = 1
    while k < n:
        a, m = scan_step(a, m, k, axis, reverse, last=(2 * k >= n) and not need_sum)
        k *= 2
    return a, m


def lane_scan(step, seeded, reverse):
    width = step.shape[1]
    if width % 128 or width == 128:
        return block_scan(step, seeded, 1, reverse, False)[1]
    parts = []
    for i in range(width // 128):
        lanes = slice(i * 128, (i + 1) * 128)
        parts.append(block_scan(step[:, lanes], seeded[:, lanes], 1, reverse, True))
    order = range(len(parts) - 1, -1, -1) if reverse else range(len(parts))
    carry = None
    out = [None] * len(parts)
    for i in order:
        a, m = parts[i]
        if carry is not None:
            m = jnp.minimum(carry + a, m)
        edge = m[:, 0:1] if reverse else m[:, 127:128]
        carry = jnp.broadcast_to(edge, m.shape)
        out[i] = m
    return jnp.concatenate(out, axis=1)


def local_kernel(flags, stims, stim_times, fibre, tissue, previous, cost_x, field, totals, own,
                 cost_y, *, grid_step):
    planes, cells_y, cells_z = previous.shape
    chunks = cells_y // CHUNK
    inf = jnp.float32(jnp.inf)

    field[...] = previous[...]

    def seed(k, carry):
        p = stims[0, k]
        r = stims[1, k]
        c = stims[2, k]

        @pl.when((p >= 0) & (p < planes))
        def _():
            base = pl.multiple_of(r // ROWS * ROWS, ROWS)
            block = field[p, pl.ds(base, ROWS), :]
            row = lax.broadcasted_iota(jnp.int32, block.shape, 0)
            lane = lax.broadcasted_iota(jnp.int32, block.shape, 1)
            hit = (row == r - base) & (lane == c)
            field[p, pl.ds(base, ROWS), :] = jnp.where(hit, jnp.minimum(block, stim_times[k]), block)

        return carry

    lax.fori_loop(0, stims.shape[1], seed, 0)

    def costs_and_z(reverse):
        def body(i, carry):
            p = i // chunks
            rows = pl.ds(pl.multiple_of((i % chunks) * CHUNK, CHUNK), CHUNK)
            xx = fibre[0, p, rows, :]
            yy = fibre[1, p, rows, :]
            zz = fibre[2, p, rows, :]
            xy = fibre[3, p, rows, :]
            xz = fibre[4, p, rows, :]
            yz = fibre[5, p, rows, :]
            cx = yy * zz - yz * yz
            cy = xx * zz - xz * xz
            cz = xx * yy - xy * xy
            det = xx * cx - xy * (xy * zz - yz * xz) + xz * (xy * yz - yy * xz)
            factor = jnp.where(tissue[p, rows, :] == 1, 1.0, 4.0).astype(jnp.float32) * grid_step
            inverse = 1.0 / det
            cost_x[p, rows, :] = jnp.sqrt(cx * inverse) * factor
            cost_y[p, rows, :] = jnp.sqrt(cy * inverse) * factor
            step_z = jnp.sqrt(cz * inverse) * factor
            u = lane_scan(step_z, field[p, rows, :], reverse)
            field[p, rows, :] = u
            return carry

        lax.fori_loop(0, planes * chunks, body, 0, unroll=2)

    def sweep_y(reverse):
        def body(j, carry):
            i = chunks - 1 - j if reverse else j
            rows = pl.ds(pl.multiple_of(i * CHUNK, CHUNK), CHUNK)
            out = []
            for p in range(planes):
                a, m = block_scan(cost_y[p, rows, :], field[p, rows, :], 0, reverse, True)
                u = jnp.minimum(carry[p] + a, m)
                field[p, rows, :] = u
                edge = u[0:1, :] if reverse else u[CHUNK - 1:CHUNK, :]
                out.append(jnp.broadcast_to(edge, u.shape))
            return tuple(out)

        start = tuple(jnp.full((CHUNK, cells_z), inf, jnp.float32) for _ in range(planes))
        lax.fori_loop(0, chunks, body, start, unroll=2)

    for flag, fn in ((flags[2], costs_and_z), (flags[1], sweep_y)):
        pl.when(flag == 1)(functools.partial(fn, True))
        pl.when(flag != 1)(functools.partial(fn, False))

    def edge(i, carry):
        rows = pl.ds(pl.multiple_of(i * CHUNK, CHUNK), CHUNK)
        c0 = cost_x[0, rows, :]
        c1 = cost_x[1, rows, :]
        u0 = field[0, rows, :]
        u1 = field[1, rows, :]
        down = flags[0] == 1
        totals[0, rows, :] = jnp.where(down, c1 + c0, c0 + c1)
        totals[1, rows, :] = jnp.where(down, jnp.minimum(u1 + c0, u0), jnp.minimum(u0 + c1, u1))
        own[rows, :] = jnp.where(down, u1, u0)
        return carry

    lax.fori_loop(0, chunks, edge, 0)


def local_sweeps(flags, stims, stim_times, fibre, tissue, previous, grid_step):
    planes, cells_y, cells_z = previous.shape
    field = jax.ShapeDtypeStruct(previous.shape, jnp.float32)
    totals = jax.ShapeDtypeStruct((2, cells_y, cells_z), jnp.float32)
    own = jax.ShapeDtypeStruct((cells_y, cells_z), jnp.float32)
    vmem = pl.BlockSpec(memory_space=pltpu.VMEM)
    smem = pl.BlockSpec(memory_space=pltpu.SMEM)
    elements = planes * cells_y * cells_z
    return pl.pallas_call(
        functools.partial(local_kernel, grid_step=grid_step),
        out_shape=(field, field, totals, own),
        in_specs=[smem, smem, smem, vmem, vmem, vmem],
        out_specs=(vmem, vmem, vmem, vmem),
        scratch_shapes=[pltpu.VMEM(previous.shape, jnp.float32)],
        compiler_params=pltpu.CompilerParams(vmem_limit_bytes=48 * 1024 * 1024),
        cost_estimate=pl.CostEstimate(
            flops=300 * elements, transcendentals=6 * elements, bytes_accessed=40 * elements
        ),
    )(flags, stims, stim_times, fibre, tissue, previous)


RELAY_ROWS = 16
LINE = 8


def flip_bits(value, mask, bits):
    out = 0
    for j in range(bits):
        out = out + (2 ** j) * ((value // 2 ** j + (mask >> j) % 2) % 2)
    return out


def relay_kernel(totals, own, incoming, least_in, least_plane, before, line_total, box1_in,
                 box1_out, box2_in, box2_out, box3_in, box4, box5, send1, recv1, send2, recv2, send3,
                 recv3, send4, recv4, send5, recv5, *, line):
    total_add = totals.at[0]
    total_min = totals.at[1]
    cells_y, cells_z = incoming.shape
    chunks = cells_y // RELAY_ROWS
    slabs = lax.axis_size("slab")
    lines = slabs // line
    half = line // 2
    slab = lax.axis_index("slab")
    group = lax.axis_index("order")
    odd = group % 2
    rank = slab + odd * (slabs - 1 - 2 * slab)
    col = rank // line
    pos = rank % line
    last = line - 1
    mesh_id = pl.DeviceIdType.MESH

    def device(r):
        return (group, r + odd * (slabs - 1 - 2 * r))

    def at(c, p):
        return device(c * line + p)

    orders = lax.axis_size("order")
    masks = list(range(2, orders, 2))
    order_bits = max(orders - 1, 1).bit_length()
    first_col = col == 0
    is_end = pos == last
    in_up = pos < half
    in_down = (pos >= half) & (pos < last)
    up_next = (pos >= 1) & (pos + 1 < half)
    down_next = (pos <= last - 2) & (pos > half)
    ends_to = [p for p in (0, 1) if p < half] + [p for p in (last - 1, last - 2) if half <= p < last]

    barrier = pltpu.get_barrier_semaphore()
    neighbours = []
    neighbours.append((pos > 0, at(col, pos - 1)))
    neighbours.append((pos < last, at(col, pos + 1)))
    for p in ends_to:
        if p not in (last - 1,):
            neighbours.append(((pos == p) & (col > 0), at(col, last)))
            neighbours.append((is_end & (col > 0), at(col, p)))
    neighbours.append((is_end & (col > 0), at(col - 1, last)))
    neighbours.append((is_end & (col < lines - 1), at(col + 1, last)))
    for m in masks:
        neighbours.append((slab >= 0, (flip_bits(group, m, order_bits), slab)))
    count = jnp.int32(0)
    for cond, dev in neighbours:
        @pl.when(cond)
        def _():
            pl.semaphore_signal(barrier, 1, device_id=dev, device_id_type=mesh_id)

        count = count + cond.astype(jnp.int32)
    pl.semaphore_wait(barrier, count)

    def copy1(c):
        return pltpu.make_async_remote_copy(box1_out.at[c], box1_in.at[c], send1.at[c], recv1.at[c],
                                            device_id=at(col, pos + 1), device_id_type=mesh_id)

    def copy2(c):
        return pltpu.make_async_remote_copy(box2_out.at[c], box2_in.at[c], send2.at[c], recv2.at[c],
                                            device_id=at(col + 1, last), device_id_type=mesh_id)

    def copy3_from_end(c, k, target):
        return pltpu.make_async_remote_copy(box2_in.at[c], box3_in.at[c], send3.at[c, k], recv3.at[c],
                                            device_id=target, device_id_type=mesh_id)

    def copy3_relay(c, target):
        return pltpu.make_async_remote_copy(box3_in.at[c], box3_in.at[c], send3.at[c, 0], recv3.at[c],
                                            device_id=target, device_id_type=mesh_id)

    def rows_of(c):
        return pl.ds(pl.multiple_of(c * RELAY_ROWS, RELAY_ROWS), RELAY_ROWS)

    def copy5(k):
        return pltpu.make_async_remote_copy(own, box5.at[k], send5.at[k], recv5.at[k],
                                            device_id=(flip_bits(group, masks[k], order_bits), slab),
                                            device_id_type=mesh_id)

    for k in range(len(masks)):
        copy5(k).start()

    def copy4(c, k):
        return pltpu.make_async_remote_copy(incoming.at[rows_of(c)], box4.at[k, c], send4.at[c, k],
                                            recv4.at[c, k], device_id=(flip_bits(group, masks[k], order_bits), slab),
                                            device_id_type=mesh_id)

    def share(c):
        for k in range(len(masks)):
            copy4(c, k).start()

    def stage1(c, carry):
        rows = rows_of(c)
        own_add = total_add[rows, :]
        own_min = total_min[rows, :]

        @pl.when(pos == 0)
        def _():
            box1_out[c, 0] = own_add
            box1_out[c, 1] = own_min

        @pl.when(pos > 0)
        def _():
            copy1(c).wait_recv()
            got_add = box1_in[c, 0]
            got_min = box1_in[c, 1]
            before[0, rows, :] = got_add
            before[1, rows, :] = got_min
            new_add = got_add + own_add
            new_min = jnp.minimum(got_min + own_add, own_min)

            @pl.when(pos < last)
            def _():
                box1_out[c, 0] = new_add
                box1_out[c, 1] = new_min

            @pl.when(is_end)
            def _():
                line_total[0, rows, :] = new_add
                line_total[1, rows, :] = new_min

        @pl.when((pos == 0) & is_end)
        def _():
            line_total[0, rows, :] = own_add
            line_total[1, rows, :] = own_min

        @pl.when(pos < last)
        def _():
            copy1(c).start()

        return carry

    def stage2(c, carry):
        rows = rows_of(c)

        @pl.when(is_end & first_col)
        def _():
            incoming[rows, :] = jnp.where(pos > 0, before[1, rows, :], jnp.inf)
            share(c)
            box2_out[c] = line_total[1, rows, :]

        @pl.when(is_end & jnp.logical_not(first_col))
        def _():
            copy2(c).wait_recv()
            value = box2_in[c]
            incoming[rows, :] = jnp.where(
                pos > 0, jnp.minimum(value + before[0, rows, :], before[1, rows, :]), value)
            share(c)
            box2_out[c] = jnp.minimum(value + line_total[0, rows, :], line_total[1, rows, :])

            for k, p in enumerate(ends_to):
                copy3_from_end(c, k, at(col, p)).start()

        @pl.when(is_end & (col < lines - 1))
        def _():
            copy2(c).start()

        return carry

    def stages12(c, carry):
        stage1(c, carry)
        return stage2(c, carry)

    lax.fori_loop(0, chunks, stages12, 0)

    def stage3(c, carry):
        rows = rows_of(c)

        @pl.when(first_col & jnp.logical_not(is_end))
        def _():
            incoming[rows, :] = jnp.where(pos > 0, before[1, rows, :], jnp.inf)
            share(c)

        @pl.when(jnp.logical_not(first_col) & (in_up | in_down))
        def _():
            copy3_relay(c, at(col, 0)).wait_recv()
            value = box3_in[c]
            incoming[rows, :] = jnp.where(
                pos > 0, jnp.minimum(value + before[0, rows, :], before[1, rows, :]), value)
            share(c)

            @pl.when(in_up & up_next)
            def _():
                copy3_relay(c, at(col, pos + 1)).start()

            @pl.when(in_down & down_next)
            def _():
                copy3_relay(c, at(col, pos - 1)).start()

        return carry

    lax.fori_loop(0, chunks, stage3, 0)

    def gather(c, carry):
        rows = rows_of(c)
        least = incoming[rows, :]
        for k in range(len(masks)):
            copy4(c, k).wait_recv()
            least = jnp.minimum(least, box4[k, c])
        least_in[rows, :] = least
        return carry

    lax.fori_loop(0, chunks, gather, 0)

    for k in range(len(masks)):
        copy5(k).wait_recv()

    def gather_plane(c, carry):
        rows = rows_of(c)
        least = own[rows, :]
        for k in range(len(masks)):
            least = jnp.minimum(least, box5[k, rows, :])
        least_plane[rows, :] = least
        return carry

    lax.fori_loop(0, chunks, gather_plane, 0)

    def drain(c, carry):
        @pl.when(pos < last)
        def _():
            copy1(c).wait_send()

        @pl.when(is_end & (col < lines - 1))
        def _():
            copy2(c).wait_send()

        @pl.when(is_end & jnp.logical_not(first_col))
        def _():
            for k, p in enumerate(ends_to):
                copy3_from_end(c, k, at(col, p)).wait_send()

        @pl.when(jnp.logical_not(first_col) & ((in_up & up_next) | (in_down & down_next)))
        def _():
            copy3_relay(c, at(col, 0)).wait_send()

        for k in range(len(masks)):
            copy4(c, k).wait_send()
        return carry

    lax.fori_loop(0, chunks, drain, 0)
    for k in range(len(masks)):
        copy5(k).wait_send()


def relay(totals, own, slabs, orders):
    cells_y, cells_z = own.shape
    chunks = cells_y // RELAY_ROWS
    sharers = len(range(2, orders, 2))
    plane = jax.ShapeDtypeStruct(own.shape, jnp.float32)
    line = LINE if slabs % LINE == 0 else slabs
    vmem = pl.BlockSpec(memory_space=pltpu.VMEM)
    box = pltpu.VMEM((chunks, RELAY_ROWS, cells_z), jnp.float32)
    pair_box = pltpu.VMEM((chunks, 2, RELAY_ROWS, cells_z), jnp.float32)
    return pl.pallas_call(
        functools.partial(relay_kernel, line=line),
        out_shape=(plane, plane, plane),
        in_specs=[vmem, vmem],
        out_specs=(vmem, vmem, vmem),
        scratch_shapes=[
            pltpu.VMEM((2, cells_y, cells_z), jnp.float32),
            pltpu.VMEM((2, cells_y, cells_z), jnp.float32),
            pair_box,
            pair_box,
            box,
            box,
            box,
            pltpu.VMEM((max(sharers, 1), chunks, RELAY_ROWS, cells_z), jnp.float32),
            pltpu.VMEM((max(sharers, 1), cells_y, cells_z), jnp.float32),
            pltpu.SemaphoreType.DMA((chunks,)),
            pltpu.SemaphoreType.DMA((chunks,)),
            pltpu.SemaphoreType.DMA((chunks,)),
            pltpu.SemaphoreType.DMA((chunks,)),
            pltpu.SemaphoreType.DMA((chunks, 4)),
            pltpu.SemaphoreType.DMA((chunks,)),
            pltpu.SemaphoreType.DMA((chunks, max(sharers, 1))),
            pltpu.SemaphoreType.DMA((chunks, max(sharers, 1))),
            pltpu.SemaphoreType.DMA((max(sharers, 1),)),
            pltpu.SemaphoreType.DMA((max(sharers, 1),)),
        ],
        compiler_params=pltpu.CompilerParams(collective_id=0, has_side_effects=True),
    )(totals, own)


def shards(previous, fibre_tensor, tissue, stim_sites, stim_times):
    planes, cells_y, cells_z = previous.shape
    slabs = lax.axis_size("slab")
    orders = lax.axis_size("order")
    slab_index = lax.axis_index("slab")
    group_index = lax.axis_index("order")
    grid_step = 2.0 / (planes * slabs)

    plane_index = stim_sites // (cells_y * cells_z) - slab_index * planes
    row_index = stim_sites // cells_z % cells_y
    column_index = stim_sites % cells_z
    stims = jnp.stack([plane_index, row_index, column_index]).astype(jnp.int32)

    bits = jnp.stack([group_index % 2, group_index // 2 % 2, group_index // 4 % 2]).astype(jnp.int32)
    cost_x, field, totals, own_plane = local_sweeps(
        bits, stims, stim_times, fibre_tensor, tissue, previous, grid_step)

    core = group_index % 2
    incoming, least_in, least_plane = relay(totals, own_plane, slabs, orders)
    other = lax.ppermute(jnp.stack([least_plane, least_in]), "order", [(g, g ^ 1) for g in range(orders)])

    least0 = jnp.where(core == 0, least_plane, other[0])
    least1 = jnp.where(core == 0, other[0], least_plane)
    up_in = jnp.where(core == 0, least_in, other[1])
    down_in = jnp.where(core == 0, other[1], least_in)

    up_add = jnp.stack([cost_x[0], cost_x[0] + cost_x[1]])
    up_min = jnp.stack([field[0], jnp.minimum(field[0] + cost_x[1], field[1])])
    down_add = jnp.stack([cost_x[1] + cost_x[0], cost_x[1]])
    down_min = jnp.stack([jnp.minimum(field[1] + cost_x[0], field[0]), field[1]])
    backward_x = core == 1
    line_add = jnp.where(backward_x, down_add, up_add)
    line_min = jnp.where(backward_x, down_min, up_min)
    sweep_field = jnp.minimum(incoming[None] + line_add, line_min)

    least_local = jnp.stack([
        jnp.minimum(least0, least1 + cost_x[0]),
        jnp.minimum(least1, least0 + cost_x[1]),
    ])
    merged = jnp.minimum(
        least_local,
        jnp.minimum(up_in[None] + up_add, down_in[None] + down_add),
    )
    return (merged, sweep_field[None])


def solution(mesh):
    placed = (P("slab", None, None), P(None, "slab", None, None), P("slab", None, None), P(), P())
    return jax.shard_map(
        shards,
        mesh=mesh,
        in_specs=placed,
        out_specs=(P("slab", None, None), P("order", "slab", None, None)),
        check_vma=False,
    )
```

```python
import functools

import jax
import jax.numpy as jnp
from jax import lax
from jax.experimental import pallas as pl
from jax.experimental.pallas import tpu as pltpu
from jax.sharding import PartitionSpec as P

ROWS = 8
CHUNK = 32


def scan_step(a, m, k, axis, reverse, last):
    n = a.shape[axis]
    index = lax.broadcasted_iota(jnp.int32, a.shape, axis)
    shift = n - k if reverse else k
    valid = index < n - k if reverse else index >= k
    a_src = pltpu.roll(a, shift, axis)
    m_src = pltpu.roll(m, shift, axis)
    m = jnp.where(valid, jnp.minimum(m_src + a, m), m)
    if not last:
        a = jnp.where(valid, a_src + a, a)
    return a, m


def block_scan(a, m, axis, reverse, need_sum):
    n = a.shape[axis]
    k = 1
    while k < n:
        a, m = scan_step(a, m, k, axis, reverse, last=(2 * k >= n) and not need_sum)
        k *= 2
    return a, m


def lane_scan(step, seeded, reverse):
    width = step.shape[1]
    if width % 128 or width == 128:
        return block_scan(step, seeded, 1, reverse, False)[1]
    parts = []
    for i in range(width // 128):
        lanes = slice(i * 128, (i + 1) * 128)
        parts.append(block_scan(step[:, lanes], seeded[:, lanes], 1, reverse, True))
    order = range(len(parts) - 1, -1, -1) if reverse else range(len(parts))
    carry = None
    out = [None] * len(parts)
    for i in order:
        a, m = parts[i]
        if carry is not None:
            m = jnp.minimum(carry + a, m)
        edge = m[:, 0:1] if reverse else m[:, 127:128]
        carry = jnp.broadcast_to(edge, m.shape)
        out[i] = m
    return jnp.concatenate(out, axis=1)


def local_kernel(flags, stims, stim_times, fibre, tissue, previous, cost_x, field, totals, own,
                 cost_y, *, grid_step):
    planes, cells_y, cells_z = previous.shape
    chunks = cells_y // CHUNK
    inf = jnp.float32(jnp.inf)

    field[...] = previous[...]

    def seed(k, carry):
        p = stims[0, k]
        r = stims[1, k]
        c = stims[2, k]

        @pl.when((p >= 0) & (p < planes))
        def _():
            base = pl.multiple_of(r // ROWS * ROWS, ROWS)
            block = field[p, pl.ds(base, ROWS), :]
            row = lax.broadcasted_iota(jnp.int32, block.shape, 0)
            lane = lax.broadcasted_iota(jnp.int32, block.shape, 1)
            hit = (row == r - base) & (lane == c)
            field[p, pl.ds(base, ROWS), :] = jnp.where(hit, jnp.minimum(block, stim_times[k]), block)

        return carry

    lax.fori_loop(0, stims.shape[1], seed, 0)

    def costs_and_z(reverse):
        def body(i, carry):
            p = i // chunks
            rows = pl.ds(pl.multiple_of((i % chunks) * CHUNK, CHUNK), CHUNK)
            xx = fibre[0, p, rows, :]
            yy = fibre[1, p, rows, :]
            zz = fibre[2, p, rows, :]
            xy = fibre[3, p, rows, :]
            xz = fibre[4, p, rows, :]
            yz = fibre[5, p, rows, :]
            cx = yy * zz - yz * yz
            cy = xx * zz - xz * xz
            cz = xx * yy - xy * xy
            det = xx * cx - xy * (xy * zz - yz * xz) + xz * (xy * yz - yy * xz)
            factor = jnp.where(tissue[p, rows, :] == 1, 1.0, 4.0).astype(jnp.float32) * grid_step
            inverse = 1.0 / det
            cost_x[p, rows, :] = jnp.sqrt(cx * inverse) * factor
            cost_y[p, rows, :] = jnp.sqrt(cy * inverse) * factor
            step_z = jnp.sqrt(cz * inverse) * factor
            u = lane_scan(step_z, field[p, rows, :], reverse)
            field[p, rows, :] = u
            return carry

        lax.fori_loop(0, planes * chunks, body, 0, unroll=2)

    def sweep_y(reverse):
        def body(j, carry):
            i = chunks - 1 - j if reverse else j
            rows = pl.ds(pl.multiple_of(i * CHUNK, CHUNK), CHUNK)
            out = []
            for p in range(planes):
                a, m = block_scan(cost_y[p, rows, :], field[p, rows, :], 0, reverse, True)
                u = jnp.minimum(carry[p] + a, m)
                field[p, rows, :] = u
                edge = u[0:1, :] if reverse else u[CHUNK - 1:CHUNK, :]
                out.append(jnp.broadcast_to(edge, u.shape))
            return tuple(out)

        start = tuple(jnp.full((CHUNK, cells_z), inf, jnp.float32) for _ in range(planes))
        lax.fori_loop(0, chunks, body, start, unroll=2)

    for flag, fn in ((flags[2], costs_and_z), (flags[1], sweep_y)):
        pl.when(flag == 1)(functools.partial(fn, True))
        pl.when(flag != 1)(functools.partial(fn, False))

    def edge(i, carry):
        rows = pl.ds(pl.multiple_of(i * CHUNK, CHUNK), CHUNK)
        c0 = cost_x[0, rows, :]
        c1 = cost_x[1, rows, :]
        u0 = field[0, rows, :]
        u1 = field[1, rows, :]
        down = flags[0] == 1
        totals[0, rows, :] = jnp.where(down, c1 + c0, c0 + c1)
        totals[1, rows, :] = jnp.where(down, jnp.minimum(u1 + c0, u0), jnp.minimum(u0 + c1, u1))
        own[rows, :] = jnp.where(down, u1, u0)
        return carry

    lax.fori_loop(0, chunks, edge, 0)


def local_sweeps(flags, stims, stim_times, fibre, tissue, previous, grid_step):
    planes, cells_y, cells_z = previous.shape
    field = jax.ShapeDtypeStruct(previous.shape, jnp.float32)
    totals = jax.ShapeDtypeStruct((2, cells_y, cells_z), jnp.float32)
    own = jax.ShapeDtypeStruct((cells_y, cells_z), jnp.float32)
    vmem = pl.BlockSpec(memory_space=pltpu.VMEM)
    smem = pl.BlockSpec(memory_space=pltpu.SMEM)
    elements = planes * cells_y * cells_z
    return pl.pallas_call(
        functools.partial(local_kernel, grid_step=grid_step),
        out_shape=(field, field, totals, own),
        in_specs=[smem, smem, smem, vmem, vmem, vmem],
        out_specs=(vmem, vmem, vmem, vmem),
        scratch_shapes=[pltpu.VMEM(previous.shape, jnp.float32)],
        compiler_params=pltpu.CompilerParams(vmem_limit_bytes=48 * 1024 * 1024),
        cost_estimate=pl.CostEstimate(
            flops=300 * elements, transcendentals=6 * elements, bytes_accessed=40 * elements
        ),
    )(flags, stims, stim_times, fibre, tissue, previous)


RELAY_ROWS = 16
LINE = 8
UP_DIRECT = 3
DOWN_DIRECT = 2


def flip_bits(value, mask, bits):
    out = 0
    for j in range(bits):
        out = out + (2 ** j) * ((value // 2 ** j + (mask >> j) % 2) % 2)
    return out


def relay_kernel(totals, own, incoming, least_in, least_plane, before, line_total, box1_in,
                 box1_out, box2_in, box2_out, box3_in, box4, box5, send1, recv1, send2, recv2, send3,
                 recv3, send4, recv4, send5, recv5, *, line):
    total_add = totals.at[0]
    total_min = totals.at[1]
    cells_y, cells_z = incoming.shape
    chunks = cells_y // RELAY_ROWS
    slabs = lax.axis_size("slab")
    lines = slabs // line
    half = line // 2
    slab = lax.axis_index("slab")
    group = lax.axis_index("order")
    odd = group % 2
    rank = slab + odd * (slabs - 1 - 2 * slab)
    col = rank // line
    pos = rank % line
    last = line - 1
    mesh_id = pl.DeviceIdType.MESH

    def device(r):
        return (group, r + odd * (slabs - 1 - 2 * r))

    def at(c, p):
        return device(c * line + p)

    orders = lax.axis_size("order")
    masks = list(range(2, orders, 2))
    order_bits = max(orders - 1, 1).bit_length()
    first_col = col == 0
    is_end = pos == last
    in_up = pos < half
    in_down = (pos >= half) & (pos < last)
    up_next = (pos >= UP_DIRECT - 1) & (pos + 1 < half)
    down_next = (pos <= last - DOWN_DIRECT) & (pos > half)
    ends_to = [p for p in range(UP_DIRECT) if p < half]
    ends_to += [last - 1 - j for j in range(DOWN_DIRECT) if half <= last - 1 - j < last]

    barrier = pltpu.get_barrier_semaphore()
    neighbours = []
    neighbours.append((pos > 0, at(col, pos - 1)))
    neighbours.append((pos < last, at(col, pos + 1)))
    for p in ends_to:
        if p not in (last - 1,):
            neighbours.append(((pos == p) & (col > 0), at(col, last)))
            neighbours.append((is_end & (col > 0), at(col, p)))
    neighbours.append((is_end & (col > 0), at(col - 1, last)))
    neighbours.append((is_end & (col < lines - 1), at(col + 1, last)))
    for m in masks:
        neighbours.append((slab >= 0, (flip_bits(group, m, order_bits), slab)))
    count = jnp.int32(0)
    for cond, dev in neighbours:
        @pl.when(cond)
        def _():
            pl.semaphore_signal(barrier, 1, device_id=dev, device_id_type=mesh_id)

        count = count + cond.astype(jnp.int32)
    pl.semaphore_wait(barrier, count)

    def copy1(c):
        return pltpu.make_async_remote_copy(box1_out.at[c], box1_in.at[c], send1.at[c], recv1.at[c],
                                            device_id=at(col, pos + 1), device_id_type=mesh_id)

    def copy2(c):
        return pltpu.make_async_remote_copy(box2_out.at[c], box2_in.at[c], send2.at[c], recv2.at[c],
                                            device_id=at(col + 1, last), device_id_type=mesh_id)

    def copy3_from_end(c, k, target):
        return pltpu.make_async_remote_copy(box2_in.at[c], box3_in.at[c], send3.at[c, k], recv3.at[c],
                                            device_id=target, device_id_type=mesh_id)

    def copy3_relay(c, target):
        return pltpu.make_async_remote_copy(box3_in.at[c], box3_in.at[c], send3.at[c, 0], recv3.at[c],
                                            device_id=target, device_id_type=mesh_id)

    def rows_of(c):
        return pl.ds(pl.multiple_of(c * RELAY_ROWS, RELAY_ROWS), RELAY_ROWS)

    def copy5(k):
        return pltpu.make_async_remote_copy(own, box5.at[k], send5.at[k], recv5.at[k],
                                            device_id=(flip_bits(group, masks[k], order_bits), slab),
                                            device_id_type=mesh_id)

    for k in range(len(masks)):
        copy5(k).start()

    def copy4(c, k):
        return pltpu.make_async_remote_copy(incoming.at[rows_of(c)], box4.at[k, c], send4.at[c, k],
                                            recv4.at[c, k], device_id=(flip_bits(group, masks[k], order_bits), slab),
                                            device_id_type=mesh_id)

    def share(c):
        for k in range(len(masks)):
            copy4(c, k).start()

    def stage1(c, carry):
        rows = rows_of(c)
        own_add = total_add[rows, :]
        own_min = total_min[rows, :]

        @pl.when(pos == 0)
        def _():
            box1_out[c, 0] = own_add
            box1_out[c, 1] = own_min

        @pl.when(pos > 0)
        def _():
            copy1(c).wait_recv()
            got_add = box1_in[c, 0]
            got_min = box1_in[c, 1]
            before[0, rows, :] = got_add
            before[1, rows, :] = got_min
            new_add = got_add + own_add
            new_min = jnp.minimum(got_min + own_add, own_min)

            @pl.when(pos < last)
            def _():
                box1_out[c, 0] = new_add
                box1_out[c, 1] = new_min

            @pl.when(is_end)
            def _():
                line_total[0, rows, :] = new_add
                line_total[1, rows, :] = new_min

        @pl.when((pos == 0) & is_end)
        def _():
            line_total[0, rows, :] = own_add
            line_total[1, rows, :] = own_min

        @pl.when(pos < last)
        def _():
            copy1(c).start()

        return carry

    def stage2(c, carry):
        rows = rows_of(c)

        @pl.when(is_end & first_col)
        def _():
            incoming[rows, :] = jnp.where(pos > 0, before[1, rows, :], jnp.inf)
            share(c)
            box2_out[c] = line_total[1, rows, :]

        @pl.when(is_end & jnp.logical_not(first_col))
        def _():
            copy2(c).wait_recv()
            value = box2_in[c]
            incoming[rows, :] = jnp.where(
                pos > 0, jnp.minimum(value + before[0, rows, :], before[1, rows, :]), value)
            share(c)
            box2_out[c] = jnp.minimum(value + line_total[0, rows, :], line_total[1, rows, :])

            for k, p in enumerate(ends_to):
                copy3_from_end(c, k, at(col, p)).start()

        @pl.when(is_end & (col < lines - 1))
        def _():
            copy2(c).start()

        return carry

    def stages12(c, carry):
        stage1(c, carry)
        return stage2(c, carry)

    lax.fori_loop(0, chunks, stages12, 0)

    def stage3(c, carry):
        rows = rows_of(c)

        @pl.when(first_col & jnp.logical_not(is_end))
        def _():
            incoming[rows, :] = jnp.where(pos > 0, before[1, rows, :], jnp.inf)
            share(c)

        @pl.when(jnp.logical_not(first_col) & (in_up | in_down))
        def _():
            copy3_relay(c, at(col, 0)).wait_recv()
            value = box3_in[c]
            incoming[rows, :] = jnp.where(
                pos > 0, jnp.minimum(value + before[0, rows, :], before[1, rows, :]), value)
            share(c)

            @pl.when(in_up & up_next)
            def _():
                copy3_relay(c, at(col, pos + 1)).start()

            @pl.when(in_down & down_next)
            def _():
                copy3_relay(c, at(col, pos - 1)).start()

        return carry

    lax.fori_loop(0, chunks, stage3, 0)

    def gather(c, carry):
        rows = rows_of(c)
        least = incoming[rows, :]
        for k in range(len(masks)):
            copy4(c, k).wait_recv()
            least = jnp.minimum(least, box4[k, c])
        least_in[rows, :] = least
        return carry

    lax.fori_loop(0, chunks, gather, 0)

    for k in range(len(masks)):
        copy5(k).wait_recv()

    def gather_plane(c, carry):
        rows = rows_of(c)
        least = own[rows, :]
        for k in range(len(masks)):
            least = jnp.minimum(least, box5[k, rows, :])
        least_plane[rows, :] = least
        return carry

    lax.fori_loop(0, chunks, gather_plane, 0)

    def drain(c, carry):
        @pl.when(pos < last)
        def _():
            copy1(c).wait_send()

        @pl.when(is_end & (col < lines - 1))
        def _():
            copy2(c).wait_send()

        @pl.when(is_end & jnp.logical_not(first_col))
        def _():
            for k, p in enumerate(ends_to):
                copy3_from_end(c, k, at(col, p)).wait_send()

        @pl.when(jnp.logical_not(first_col) & ((in_up & up_next) | (in_down & down_next)))
        def _():
            copy3_relay(c, at(col, 0)).wait_send()

        for k in range(len(masks)):
            copy4(c, k).wait_send()
        return carry

    lax.fori_loop(0, chunks, drain, 0)
    for k in range(len(masks)):
        copy5(k).wait_send()


def relay(totals, own, slabs, orders):
    cells_y, cells_z = own.shape
    chunks = cells_y // RELAY_ROWS
    sharers = len(range(2, orders, 2))
    plane = jax.ShapeDtypeStruct(own.shape, jnp.float32)
    line = LINE if slabs % LINE == 0 else slabs
    vmem = pl.BlockSpec(memory_space=pltpu.VMEM)
    box = pltpu.VMEM((chunks, RELAY_ROWS, cells_z), jnp.float32)
    pair_box = pltpu.VMEM((chunks, 2, RELAY_ROWS, cells_z), jnp.float32)
    return pl.pallas_call(
        functools.partial(relay_kernel, line=line),
        out_shape=(plane, plane, plane),
        in_specs=[vmem, vmem],
        out_specs=(vmem, vmem, vmem),
        scratch_shapes=[
            pltpu.VMEM((2, cells_y, cells_z), jnp.float32),
            pltpu.VMEM((2, cells_y, cells_z), jnp.float32),
            pair_box,
            pair_box,
            box,
            box,
            box,
            pltpu.VMEM((max(sharers, 1), chunks, RELAY_ROWS, cells_z), jnp.float32),
            pltpu.VMEM((max(sharers, 1), cells_y, cells_z), jnp.float32),
            pltpu.SemaphoreType.DMA((chunks,)),
            pltpu.SemaphoreType.DMA((chunks,)),
            pltpu.SemaphoreType.DMA((chunks,)),
            pltpu.SemaphoreType.DMA((chunks,)),
            pltpu.SemaphoreType.DMA((chunks, UP_DIRECT + DOWN_DIRECT)),
            pltpu.SemaphoreType.DMA((chunks,)),
            pltpu.SemaphoreType.DMA((chunks, max(sharers, 1))),
            pltpu.SemaphoreType.DMA((chunks, max(sharers, 1))),
            pltpu.SemaphoreType.DMA((max(sharers, 1),)),
            pltpu.SemaphoreType.DMA((max(sharers, 1),)),
        ],
        compiler_params=pltpu.CompilerParams(collective_id=0, has_side_effects=True),
    )(totals, own)


def shards(previous, fibre_tensor, tissue, stim_sites, stim_times):
    planes, cells_y, cells_z = previous.shape
    slabs = lax.axis_size("slab")
    orders = lax.axis_size("order")
    slab_index = lax.axis_index("slab")
    group_index = lax.axis_index("order")
    grid_step = 2.0 / (planes * slabs)

    plane_index = stim_sites // (cells_y * cells_z) - slab_index * planes
    row_index = stim_sites // cells_z % cells_y
    column_index = stim_sites % cells_z
    stims = jnp.stack([plane_index, row_index, column_index]).astype(jnp.int32)

    bits = jnp.stack([group_index % 2, group_index // 2 % 2, group_index // 4 % 2]).astype(jnp.int32)
    cost_x, field, totals, own_plane = local_sweeps(
        bits, stims, stim_times, fibre_tensor, tissue, previous, grid_step)

    core = group_index % 2
    incoming, least_in, least_plane = relay(totals, own_plane, slabs, orders)
    other = lax.ppermute(jnp.stack([least_plane, least_in]), "order", [(g, g ^ 1) for g in range(orders)])

    least0 = jnp.where(core == 0, least_plane, other[0])
    least1 = jnp.where(core == 0, other[0], least_plane)
    up_in = jnp.where(core == 0, least_in, other[1])
    down_in = jnp.where(core == 0, other[1], least_in)

    up_add = jnp.stack([cost_x[0], cost_x[0] + cost_x[1]])
    up_min = jnp.stack([field[0], jnp.minimum(field[0] + cost_x[1], field[1])])
    down_add = jnp.stack([cost_x[1] + cost_x[0], cost_x[1]])
    down_min = jnp.stack([jnp.minimum(field[1] + cost_x[0], field[0]), field[1]])
    backward_x = core == 1
    line_add = jnp.where(backward_x, down_add, up_add)
    line_min = jnp.where(backward_x, down_min, up_min)
    sweep_field = jnp.minimum(incoming[None] + line_add, line_min)

    least_local = jnp.stack([
        jnp.minimum(least0, least1 + cost_x[0]),
        jnp.minimum(least1, least0 + cost_x[1]),
    ])
    merged = jnp.minimum(
        least_local,
        jnp.minimum(up_in[None] + up_add, down_in[None] + down_add),
    )
    return (merged, sweep_field[None])


def solution(mesh):
    placed = (P("slab", None, None), P(None, "slab", None, None), P("slab", None, None), P(), P())
    return jax.shard_map(
        shards,
        mesh=mesh,
        in_specs=placed,
        out_specs=(P("slab", None, None), P("order", "slab", None, None)),
        check_vma=False,
    )
```

```python
import functools

import jax
import jax.numpy as jnp
from jax import lax
from jax.experimental import pallas as pl
from jax.experimental.pallas import tpu as pltpu
from jax.sharding import PartitionSpec as P

ROWS = 8
CHUNK = 32


def scan_step(a, m, k, axis, reverse, last):
    n = a.shape[axis]
    index = lax.broadcasted_iota(jnp.int32, a.shape, axis)
    shift = n - k if reverse else k
    valid = index < n - k if reverse else index >= k
    a_src = pltpu.roll(a, shift, axis)
    m_src = pltpu.roll(m, shift, axis)
    m = jnp.where(valid, jnp.minimum(m_src + a, m), m)
    if not last:
        a = jnp.where(valid, a_src + a, a)
    return a, m


def block_scan(a, m, axis, reverse, need_sum):
    n = a.shape[axis]
    k = 1
    while k < n:
        a, m = scan_step(a, m, k, axis, reverse, last=(2 * k >= n) and not need_sum)
        k *= 2
    return a, m


def lane_scan(step, seeded, reverse):
    width = step.shape[1]
    if width % 128 or width == 128:
        return block_scan(step, seeded, 1, reverse, False)[1]
    parts = []
    for i in range(width // 128):
        lanes = slice(i * 128, (i + 1) * 128)
        parts.append(block_scan(step[:, lanes], seeded[:, lanes], 1, reverse, True))
    order = range(len(parts) - 1, -1, -1) if reverse else range(len(parts))
    carry = None
    out = [None] * len(parts)
    for i in order:
        a, m = parts[i]
        if carry is not None:
            m = jnp.minimum(carry + a, m)
        edge = m[:, 0:1] if reverse else m[:, 127:128]
        carry = jnp.broadcast_to(edge, m.shape)
        out[i] = m
    return jnp.concatenate(out, axis=1)


def local_kernel(flags, stims, stim_times, fibre, tissue, previous, cost_x, field, totals, own,
                 cost_y, *, grid_step):
    planes, cells_y, cells_z = previous.shape
    chunks = cells_y // CHUNK
    inf = jnp.float32(jnp.inf)

    field[...] = previous[...]

    def seed(k, carry):
        p = stims[0, k]
        r = stims[1, k]
        c = stims[2, k]

        @pl.when((p >= 0) & (p < planes))
        def _():
            base = pl.multiple_of(r // ROWS * ROWS, ROWS)
            block = field[p, pl.ds(base, ROWS), :]
            row = lax.broadcasted_iota(jnp.int32, block.shape, 0)
            lane = lax.broadcasted_iota(jnp.int32, block.shape, 1)
            hit = (row == r - base) & (lane == c)
            field[p, pl.ds(base, ROWS), :] = jnp.where(hit, jnp.minimum(block, stim_times[k]), block)

        return carry

    lax.fori_loop(0, stims.shape[1], seed, 0)

    def costs_and_z(reverse):
        def body(i, carry):
            p = i // chunks
            rows = pl.ds(pl.multiple_of((i % chunks) * CHUNK, CHUNK), CHUNK)
            xx = fibre[0, p, rows, :]
            yy = fibre[1, p, rows, :]
            zz = fibre[2, p, rows, :]
            xy = fibre[3, p, rows, :]
            xz = fibre[4, p, rows, :]
            yz = fibre[5, p, rows, :]
            cx = yy * zz - yz * yz
            cy = xx * zz - xz * xz
            cz = xx * yy - xy * xy
            det = xx * cx - xy * (xy * zz - yz * xz) + xz * (xy * yz - yy * xz)
            factor = jnp.where(tissue[p, rows, :] == 1, 1.0, 4.0).astype(jnp.float32) * grid_step
            inverse = 1.0 / det
            cost_x[p, rows, :] = jnp.sqrt(cx * inverse) * factor
            cost_y[p, rows, :] = jnp.sqrt(cy * inverse) * factor
            step_z = jnp.sqrt(cz * inverse) * factor
            u = lane_scan(step_z, field[p, rows, :], reverse)
            field[p, rows, :] = u
            return carry

        lax.fori_loop(0, planes * chunks, body, 0, unroll=2)

    def sweep_y(reverse):
        def body(j, carry):
            i = chunks - 1 - j if reverse else j
            rows = pl.ds(pl.multiple_of(i * CHUNK, CHUNK), CHUNK)
            out = []
            for p in range(planes):
                a, m = block_scan(cost_y[p, rows, :], field[p, rows, :], 0, reverse, True)
                u = jnp.minimum(carry[p] + a, m)
                field[p, rows, :] = u
                edge = u[0:1, :] if reverse else u[CHUNK - 1:CHUNK, :]
                out.append(jnp.broadcast_to(edge, u.shape))
            return tuple(out)

        start = tuple(jnp.full((CHUNK, cells_z), inf, jnp.float32) for _ in range(planes))
        lax.fori_loop(0, chunks, body, start, unroll=2)

    for flag, fn in ((flags[2], costs_and_z), (flags[1], sweep_y)):
        pl.when(flag == 1)(functools.partial(fn, True))
        pl.when(flag != 1)(functools.partial(fn, False))

    def edge(i, carry):
        rows = pl.ds(pl.multiple_of(i * CHUNK, CHUNK), CHUNK)
        c0 = cost_x[0, rows, :]
        c1 = cost_x[1, rows, :]
        u0 = field[0, rows, :]
        u1 = field[1, rows, :]
        down = flags[0] == 1
        totals[0, rows, :] = jnp.where(down, c1 + c0, c0 + c1)
        totals[1, rows, :] = jnp.where(down, jnp.minimum(u1 + c0, u0), jnp.minimum(u0 + c1, u1))
        own[rows, :] = jnp.where(down, u1, u0)
        return carry

    lax.fori_loop(0, chunks, edge, 0)


def local_sweeps(flags, stims, stim_times, fibre, tissue, previous, grid_step):
    planes, cells_y, cells_z = previous.shape
    field = jax.ShapeDtypeStruct(previous.shape, jnp.float32)
    totals = jax.ShapeDtypeStruct((2, cells_y, cells_z), jnp.float32)
    own = jax.ShapeDtypeStruct((cells_y, cells_z), jnp.float32)
    vmem = pl.BlockSpec(memory_space=pltpu.VMEM)
    smem = pl.BlockSpec(memory_space=pltpu.SMEM)
    elements = planes * cells_y * cells_z
    return pl.pallas_call(
        functools.partial(local_kernel, grid_step=grid_step),
        out_shape=(field, field, totals, own),
        in_specs=[smem, smem, smem, vmem, vmem, vmem],
        out_specs=(vmem, vmem, vmem, vmem),
        scratch_shapes=[pltpu.VMEM(previous.shape, jnp.float32)],
        compiler_params=pltpu.CompilerParams(vmem_limit_bytes=48 * 1024 * 1024),
        cost_estimate=pl.CostEstimate(
            flops=300 * elements, transcendentals=6 * elements, bytes_accessed=40 * elements
        ),
    )(flags, stims, stim_times, fibre, tissue, previous)


RELAY_ROWS = 16
LINE = 8


def flip_bits(value, mask, bits):
    out = 0
    for j in range(bits):
        out = out + (2 ** j) * ((value // 2 ** j + (mask >> j) % 2) % 2)
    return out


def relay_kernel(totals, own, incoming, least_both, before, line_total, box1_in, box1_out,
                 box2_in, box2_out, box3_in, box4, box5, send1, recv1, send2, recv2, send3, recv3,
                 send4, recv4, send5, recv5, *, line):
    total_add = totals.at[0]
    total_min = totals.at[1]
    least_plane = least_both.at[0]
    least_in = least_both.at[1]
    cells_y, cells_z = incoming.shape
    chunks = cells_y // RELAY_ROWS
    slabs = lax.axis_size("slab")
    lines = slabs // line
    half = line // 2
    slab = lax.axis_index("slab")
    group = lax.axis_index("order")
    odd = group % 2
    rank = slab + odd * (slabs - 1 - 2 * slab)
    col = rank // line
    pos = rank % line
    last = line - 1
    mesh_id = pl.DeviceIdType.MESH

    def device(r):
        return (group, r + odd * (slabs - 1 - 2 * r))

    def at(c, p):
        return device(c * line + p)

    orders = lax.axis_size("order")
    masks = list(range(2, orders, 2))
    order_bits = max(orders - 1, 1).bit_length()
    first_col = col == 0
    is_end = pos == last
    in_up = pos < half
    in_down = (pos >= half) & (pos < last)
    up_next = (pos >= 1) & (pos + 1 < half)
    down_next = (pos <= last - 2) & (pos > half)
    ends_to = [p for p in (0, 1) if p < half] + [p for p in (last - 1, last - 2) if half <= p < last]

    barrier = pltpu.get_barrier_semaphore()
    neighbours = []
    neighbours.append((pos > 0, at(col, pos - 1)))
    neighbours.append((pos < last, at(col, pos + 1)))
    for p in ends_to:
        if p not in (last - 1,):
            neighbours.append(((pos == p) & (col > 0), at(col, last)))
            neighbours.append((is_end & (col > 0), at(col, p)))
    neighbours.append((is_end & (col > 0), at(col - 1, last)))
    neighbours.append((is_end & (col < lines - 1), at(col + 1, last)))
    for m in masks:
        neighbours.append((slab >= 0, (flip_bits(group, m, order_bits), slab)))
    count = jnp.int32(0)
    for cond, dev in neighbours:
        @pl.when(cond)
        def _():
            pl.semaphore_signal(barrier, 1, device_id=dev, device_id_type=mesh_id)

        count = count + cond.astype(jnp.int32)
    pl.semaphore_wait(barrier, count)

    def copy1(c):
        return pltpu.make_async_remote_copy(box1_out.at[c], box1_in.at[c], send1.at[c], recv1.at[c],
                                            device_id=at(col, pos + 1), device_id_type=mesh_id)

    def copy2(c):
        return pltpu.make_async_remote_copy(box2_out.at[c], box2_in.at[c], send2.at[c], recv2.at[c],
                                            device_id=at(col + 1, last), device_id_type=mesh_id)

    def copy3_from_end(c, k, target):
        return pltpu.make_async_remote_copy(box2_in.at[c], box3_in.at[c], send3.at[c, k], recv3.at[c],
                                            device_id=target, device_id_type=mesh_id)

    def copy3_relay(c, target):
        return pltpu.make_async_remote_copy(box3_in.at[c], box3_in.at[c], send3.at[c, 0], recv3.at[c],
                                            device_id=target, device_id_type=mesh_id)

    def rows_of(c):
        return pl.ds(pl.multiple_of(c * RELAY_ROWS, RELAY_ROWS), RELAY_ROWS)

    def copy5(k):
        return pltpu.make_async_remote_copy(own, box5.at[k], send5.at[k], recv5.at[k],
                                            device_id=(flip_bits(group, masks[k], order_bits), slab),
                                            device_id_type=mesh_id)

    for k in range(len(masks)):
        copy5(k).start()

    def copy4(c, k):
        return pltpu.make_async_remote_copy(incoming.at[rows_of(c)], box4.at[k, c], send4.at[c, k],
                                            recv4.at[c, k], device_id=(flip_bits(group, masks[k], order_bits), slab),
                                            device_id_type=mesh_id)

    def share(c):
        for k in range(len(masks)):
            copy4(c, k).start()

    def stage1(c, carry):
        rows = rows_of(c)
        own_add = total_add[rows, :]
        own_min = total_min[rows, :]

        @pl.when(pos == 0)
        def _():
            box1_out[c, 0] = own_add
            box1_out[c, 1] = own_min

        @pl.when(pos > 0)
        def _():
            copy1(c).wait_recv()
            got_add = box1_in[c, 0]
            got_min = box1_in[c, 1]
            before[0, rows, :] = got_add
            before[1, rows, :] = got_min
            new_add = got_add + own_add
            new_min = jnp.minimum(got_min + own_add, own_min)

            @pl.when(pos < last)
            def _():
                box1_out[c, 0] = new_add
                box1_out[c, 1] = new_min

            @pl.when(is_end)
            def _():
                line_total[0, rows, :] = new_add
                line_total[1, rows, :] = new_min

        @pl.when((pos == 0) & is_end)
        def _():
            line_total[0, rows, :] = own_add
            line_total[1, rows, :] = own_min

        @pl.when(pos < last)
        def _():
            copy1(c).start()

        return carry

    def stage2(c, carry):
        rows = rows_of(c)

        @pl.when(is_end & first_col)
        def _():
            incoming[rows, :] = jnp.where(pos > 0, before[1, rows, :], jnp.inf)
            share(c)
            box2_out[c] = line_total[1, rows, :]

        @pl.when(is_end & jnp.logical_not(first_col))
        def _():
            copy2(c).wait_recv()
            value = box2_in[c]
            incoming[rows, :] = jnp.where(
                pos > 0, jnp.minimum(value + before[0, rows, :], before[1, rows, :]), value)
            share(c)
            box2_out[c] = jnp.minimum(value + line_total[0, rows, :], line_total[1, rows, :])

            for k, p in enumerate(ends_to):
                copy3_from_end(c, k, at(col, p)).start()

        @pl.when(is_end & (col < lines - 1))
        def _():
            copy2(c).start()

        return carry

    def stages12(c, carry):
        stage1(c, carry)
        return stage2(c, carry)

    lax.fori_loop(0, chunks, stages12, 0)

    def stage3(c, carry):
        rows = rows_of(c)

        @pl.when(first_col & jnp.logical_not(is_end))
        def _():
            incoming[rows, :] = jnp.where(pos > 0, before[1, rows, :], jnp.inf)
            share(c)

        @pl.when(jnp.logical_not(first_col) & (in_up | in_down))
        def _():
            copy3_relay(c, at(col, 0)).wait_recv()
            value = box3_in[c]
            incoming[rows, :] = jnp.where(
                pos > 0, jnp.minimum(value + before[0, rows, :], before[1, rows, :]), value)
            share(c)

            @pl.when(in_up & up_next)
            def _():
                copy3_relay(c, at(col, pos + 1)).start()

            @pl.when(in_down & down_next)
            def _():
                copy3_relay(c, at(col, pos - 1)).start()

        return carry

    lax.fori_loop(0, chunks, stage3, 0)

    def gather(c, carry):
        rows = rows_of(c)
        least = incoming[rows, :]
        for k in range(len(masks)):
            copy4(c, k).wait_recv()
            least = jnp.minimum(least, box4[k, c])
        least_in[rows, :] = least
        return carry

    lax.fori_loop(0, chunks, gather, 0)

    for k in range(len(masks)):
        copy5(k).wait_recv()

    def gather_plane(c, carry):
        rows = rows_of(c)
        least = own[rows, :]
        for k in range(len(masks)):
            least = jnp.minimum(least, box5[k, rows, :])
        least_plane[rows, :] = least
        return carry

    lax.fori_loop(0, chunks, gather_plane, 0)

    def drain(c, carry):
        @pl.when(pos < last)
        def _():
            copy1(c).wait_send()

        @pl.when(is_end & (col < lines - 1))
        def _():
            copy2(c).wait_send()

        @pl.when(is_end & jnp.logical_not(first_col))
        def _():
            for k, p in enumerate(ends_to):
                copy3_from_end(c, k, at(col, p)).wait_send()

        @pl.when(jnp.logical_not(first_col) & ((in_up & up_next) | (in_down & down_next)))
        def _():
            copy3_relay(c, at(col, 0)).wait_send()

        for k in range(len(masks)):
            copy4(c, k).wait_send()
        return carry

    lax.fori_loop(0, chunks, drain, 0)
    for k in range(len(masks)):
        copy5(k).wait_send()


def relay(totals, own, slabs, orders):
    cells_y, cells_z = own.shape
    chunks = cells_y // RELAY_ROWS
    sharers = len(range(2, orders, 2))
    plane = jax.ShapeDtypeStruct(own.shape, jnp.float32)
    line = LINE if slabs % LINE == 0 else slabs
    vmem = pl.BlockSpec(memory_space=pltpu.VMEM)
    box = pltpu.VMEM((chunks, RELAY_ROWS, cells_z), jnp.float32)
    pair_box = pltpu.VMEM((chunks, 2, RELAY_ROWS, cells_z), jnp.float32)
    return pl.pallas_call(
        functools.partial(relay_kernel, line=line),
        out_shape=(plane, jax.ShapeDtypeStruct((2,) + own.shape, jnp.float32)),
        in_specs=[vmem, vmem],
        out_specs=(vmem, vmem),
        scratch_shapes=[
            pltpu.VMEM((2, cells_y, cells_z), jnp.float32),
            pltpu.VMEM((2, cells_y, cells_z), jnp.float32),
            pair_box,
            pair_box,
            box,
            box,
            box,
            pltpu.VMEM((max(sharers, 1), chunks, RELAY_ROWS, cells_z), jnp.float32),
            pltpu.VMEM((max(sharers, 1), cells_y, cells_z), jnp.float32),
            pltpu.SemaphoreType.DMA((chunks,)),
            pltpu.SemaphoreType.DMA((chunks,)),
            pltpu.SemaphoreType.DMA((chunks,)),
            pltpu.SemaphoreType.DMA((chunks,)),
            pltpu.SemaphoreType.DMA((chunks, 4)),
            pltpu.SemaphoreType.DMA((chunks,)),
            pltpu.SemaphoreType.DMA((chunks, max(sharers, 1))),
            pltpu.SemaphoreType.DMA((chunks, max(sharers, 1))),
            pltpu.SemaphoreType.DMA((max(sharers, 1),)),
            pltpu.SemaphoreType.DMA((max(sharers, 1),)),
        ],
        compiler_params=pltpu.CompilerParams(collective_id=0, has_side_effects=True),
    )(totals, own)


def shards(previous, fibre_tensor, tissue, stim_sites, stim_times):
    planes, cells_y, cells_z = previous.shape
    slabs = lax.axis_size("slab")
    orders = lax.axis_size("order")
    slab_index = lax.axis_index("slab")
    group_index = lax.axis_index("order")
    grid_step = 2.0 / (planes * slabs)

    plane_index = stim_sites // (cells_y * cells_z) - slab_index * planes
    row_index = stim_sites // cells_z % cells_y
    column_index = stim_sites % cells_z
    stims = jnp.stack([plane_index, row_index, column_index]).astype(jnp.int32)

    bits = jnp.stack([group_index % 2, group_index // 2 % 2, group_index // 4 % 2]).astype(jnp.int32)
    cost_x, field, totals, own_plane = local_sweeps(
        bits, stims, stim_times, fibre_tensor, tissue, previous, grid_step)

    core = group_index % 2
    incoming, least_both = relay(totals, own_plane, slabs, orders)
    least_plane = least_both[0]
    least_in = least_both[1]
    other = lax.ppermute(least_both, "order", [(g, g ^ 1) for g in range(orders)])

    least0 = jnp.where(core == 0, least_plane, other[0])
    least1 = jnp.where(core == 0, other[0], least_plane)
    up_in = jnp.where(core == 0, least_in, other[1])
    down_in = jnp.where(core == 0, other[1], least_in)

    up_add = jnp.stack([cost_x[0], cost_x[0] + cost_x[1]])
    up_min = jnp.stack([field[0], jnp.minimum(field[0] + cost_x[1], field[1])])
    down_add = jnp.stack([cost_x[1] + cost_x[0], cost_x[1]])
    down_min = jnp.stack([jnp.minimum(field[1] + cost_x[0], field[0]), field[1]])
    backward_x = core == 1
    line_add = jnp.where(backward_x, down_add, up_add)
    line_min = jnp.where(backward_x, down_min, up_min)
    sweep_field = jnp.minimum(incoming[None] + line_add, line_min)

    least_local = jnp.stack([
        jnp.minimum(least0, least1 + cost_x[0]),
        jnp.minimum(least1, least0 + cost_x[1]),
    ])
    merged = jnp.minimum(
        least_local,
        jnp.minimum(up_in[None] + up_add, down_in[None] + down_add),
    )
    return (merged, sweep_field[None])


def solution(mesh):
    placed = (P("slab", None, None), P(None, "slab", None, None), P("slab", None, None), P(), P())
    return jax.shard_map(
        shards,
        mesh=mesh,
        in_specs=placed,
        out_specs=(P("slab", None, None), P("order", "slab", None, None)),
        check_vma=False,
    )
```

```python
import functools

import jax
import jax.numpy as jnp
from jax import lax
from jax.experimental import pallas as pl
from jax.experimental.pallas import tpu as pltpu
from jax.sharding import PartitionSpec as P

ROWS = 8
CHUNK = 32


def scan_step(a, m, k, axis, reverse, last):
    n = a.shape[axis]
    index = lax.broadcasted_iota(jnp.int32, a.shape, axis)
    shift = n - k if reverse else k
    valid = index < n - k if reverse else index >= k
    a_src = pltpu.roll(a, shift, axis)
    m_src = pltpu.roll(m, shift, axis)
    m = jnp.where(valid, jnp.minimum(m_src + a, m), m)
    if not last:
        a = jnp.where(valid, a_src + a, a)
    return a, m


def block_scan(a, m, axis, reverse, need_sum):
    n = a.shape[axis]
    k = 1
    while k < n:
        a, m = scan_step(a, m, k, axis, reverse, last=(2 * k >= n) and not need_sum)
        k *= 2
    return a, m


def lane_scan(step, seeded, reverse):
    width = step.shape[1]
    if width % 128 or width == 128:
        return block_scan(step, seeded, 1, reverse, False)[1]
    parts = []
    for i in range(width // 128):
        lanes = slice(i * 128, (i + 1) * 128)
        parts.append(block_scan(step[:, lanes], seeded[:, lanes], 1, reverse, True))
    order = range(len(parts) - 1, -1, -1) if reverse else range(len(parts))
    carry = None
    out = [None] * len(parts)
    for i in order:
        a, m = parts[i]
        if carry is not None:
            m = jnp.minimum(carry + a, m)
        edge = m[:, 0:1] if reverse else m[:, 127:128]
        carry = jnp.broadcast_to(edge, m.shape)
        out[i] = m
    return jnp.concatenate(out, axis=1)


def local_kernel(flags, stims, stim_times, fibre, tissue, previous, cost_x, field, totals, own,
                 cost_y, dma, *, grid_step):
    planes, cells_y, cells_z = previous.shape
    chunks = cells_y // CHUNK
    inf = jnp.float32(jnp.inf)

    seed_copy = pltpu.make_async_copy(previous, field, dma)
    seed_copy.start()
    seed_copy.wait()

    def seed(k, carry):
        p = stims[0, k]
        r = stims[1, k]
        c = stims[2, k]

        @pl.when((p >= 0) & (p < planes))
        def _():
            base = pl.multiple_of(r // ROWS * ROWS, ROWS)
            block = field[p, pl.ds(base, ROWS), :]
            row = lax.broadcasted_iota(jnp.int32, block.shape, 0)
            lane = lax.broadcasted_iota(jnp.int32, block.shape, 1)
            hit = (row == r - base) & (lane == c)
            field[p, pl.ds(base, ROWS), :] = jnp.where(hit, jnp.minimum(block, stim_times[k]), block)

        return carry

    lax.fori_loop(0, stims.shape[1], seed, 0)

    def costs_and_z(reverse):
        def body(i, carry):
            p = i // chunks
            rows = pl.ds(pl.multiple_of((i % chunks) * CHUNK, CHUNK), CHUNK)
            xx = fibre[0, p, rows, :]
            yy = fibre[1, p, rows, :]
            zz = fibre[2, p, rows, :]
            xy = fibre[3, p, rows, :]
            xz = fibre[4, p, rows, :]
            yz = fibre[5, p, rows, :]
            cx = yy * zz - yz * yz
            cy = xx * zz - xz * xz
            cz = xx * yy - xy * xy
            det = xx * cx - xy * (xy * zz - yz * xz) + xz * (xy * yz - yy * xz)
            factor = jnp.where(tissue[p, rows, :] == 1, 1.0, 4.0).astype(jnp.float32) * grid_step
            inverse = 1.0 / det
            cost_x[p, rows, :] = jnp.sqrt(cx * inverse) * factor
            cost_y[p, rows, :] = jnp.sqrt(cy * inverse) * factor
            step_z = jnp.sqrt(cz * inverse) * factor
            u = lane_scan(step_z, field[p, rows, :], reverse)
            field[p, rows, :] = u
            return carry

        lax.fori_loop(0, planes * chunks, body, 0, unroll=2)

    def sweep_y(reverse):
        def body(j, carry):
            i = chunks - 1 - j if reverse else j
            rows = pl.ds(pl.multiple_of(i * CHUNK, CHUNK), CHUNK)
            out = []
            for p in range(planes):
                a, m = block_scan(cost_y[p, rows, :], field[p, rows, :], 0, reverse, True)
                u = jnp.minimum(carry[p] + a, m)
                field[p, rows, :] = u
                edge = u[0:1, :] if reverse else u[CHUNK - 1:CHUNK, :]
                out.append(jnp.broadcast_to(edge, u.shape))
            return tuple(out)

        start = tuple(jnp.full((CHUNK, cells_z), inf, jnp.float32) for _ in range(planes))
        lax.fori_loop(0, chunks, body, start, unroll=2)

    for flag, fn in ((flags[2], costs_and_z), (flags[1], sweep_y)):
        pl.when(flag == 1)(functools.partial(fn, True))
        pl.when(flag != 1)(functools.partial(fn, False))

    def edge(i, carry):
        rows = pl.ds(pl.multiple_of(i * CHUNK, CHUNK), CHUNK)
        c0 = cost_x[0, rows, :]
        c1 = cost_x[1, rows, :]
        u0 = field[0, rows, :]
        u1 = field[1, rows, :]
        down = flags[0] == 1
        totals[0, rows, :] = jnp.where(down, c1 + c0, c0 + c1)
        totals[1, rows, :] = jnp.where(down, jnp.minimum(u1 + c0, u0), jnp.minimum(u0 + c1, u1))
        own[rows, :] = jnp.where(down, u1, u0)
        return carry

    lax.fori_loop(0, chunks, edge, 0)


def local_sweeps(flags, stims, stim_times, fibre, tissue, previous, grid_step):
    planes, cells_y, cells_z = previous.shape
    field = jax.ShapeDtypeStruct(previous.shape, jnp.float32)
    totals = jax.ShapeDtypeStruct((2, cells_y, cells_z), jnp.float32)
    own = jax.ShapeDtypeStruct((cells_y, cells_z), jnp.float32)
    vmem = pl.BlockSpec(memory_space=pltpu.VMEM)
    smem = pl.BlockSpec(memory_space=pltpu.SMEM)
    elements = planes * cells_y * cells_z
    return pl.pallas_call(
        functools.partial(local_kernel, grid_step=grid_step),
        out_shape=(field, field, totals, own),
        in_specs=[smem, smem, smem, vmem, vmem, vmem],
        out_specs=(vmem, vmem, vmem, vmem),
        scratch_shapes=[pltpu.VMEM(previous.shape, jnp.float32), pltpu.SemaphoreType.DMA(())],
        compiler_params=pltpu.CompilerParams(vmem_limit_bytes=48 * 1024 * 1024),
        cost_estimate=pl.CostEstimate(
            flops=300 * elements, transcendentals=6 * elements, bytes_accessed=40 * elements
        ),
    )(flags, stims, stim_times, fibre, tissue, previous)


RELAY_ROWS = 16
LINE = 8


def flip_bits(value, mask, bits):
    out = 0
    for j in range(bits):
        out = out + (2 ** j) * ((value // 2 ** j + (mask >> j) % 2) % 2)
    return out


def relay_kernel(totals, own, incoming, least_in, least_plane, before, line_total, box1_in,
                 box1_out, box2_in, box2_out, box3_in, box4, box5, send1, recv1, send2, recv2, send3,
                 recv3, send4, recv4, send5, recv5, *, line):
    total_add = totals.at[0]
    total_min = totals.at[1]
    cells_y, cells_z = incoming.shape
    chunks = cells_y // RELAY_ROWS
    slabs = lax.axis_size("slab")
    lines = slabs // line
    half = line // 2
    slab = lax.axis_index("slab")
    group = lax.axis_index("order")
    odd = group % 2
    rank = slab + odd * (slabs - 1 - 2 * slab)
    col = rank // line
    pos = rank % line
    last = line - 1
    mesh_id = pl.DeviceIdType.MESH

    def device(r):
        return (group, r + odd * (slabs - 1 - 2 * r))

    def at(c, p):
        return device(c * line + p)

    orders = lax.axis_size("order")
    masks = list(range(2, orders, 2))
    order_bits = max(orders - 1, 1).bit_length()
    first_col = col == 0
    is_end = pos == last
    in_up = pos < half
    in_down = (pos >= half) & (pos < last)
    up_next = (pos >= 1) & (pos + 1 < half)
    down_next = (pos <= last - 2) & (pos > half)
    ends_to = [p for p in (0, 1) if p < half] + [p for p in (last - 1, last - 2) if half <= p < last]

    barrier = pltpu.get_barrier_semaphore()
    neighbours = []
    neighbours.append((pos > 0, at(col, pos - 1)))
    neighbours.append((pos < last, at(col, pos + 1)))
    for p in ends_to:
        if p not in (last - 1,):
            neighbours.append(((pos == p) & (col > 0), at(col, last)))
            neighbours.append((is_end & (col > 0), at(col, p)))
    neighbours.append((is_end & (col > 0), at(col - 1, last)))
    neighbours.append((is_end & (col < lines - 1), at(col + 1, last)))
    for m in masks:
        neighbours.append((slab >= 0, (flip_bits(group, m, order_bits), slab)))
    count = jnp.int32(0)
    for cond, dev in neighbours:
        @pl.when(cond)
        def _():
            pl.semaphore_signal(barrier, 1, device_id=dev, device_id_type=mesh_id)

        count = count + cond.astype(jnp.int32)
    pl.semaphore_wait(barrier, count)

    def copy1(c):
        return pltpu.make_async_remote_copy(box1_out.at[c], box1_in.at[c], send1.at[c], recv1.at[c],
                                            device_id=at(col, pos + 1), device_id_type=mesh_id)

    def copy2(c):
        return pltpu.make_async_remote_copy(box2_out.at[c], box2_in.at[c], send2.at[c], recv2.at[c],
                                            device_id=at(col + 1, last), device_id_type=mesh_id)

    def copy3_from_end(c, k, target):
        return pltpu.make_async_remote_copy(box2_in.at[c], box3_in.at[c], send3.at[c, k], recv3.at[c],
                                            device_id=target, device_id_type=mesh_id)

    def copy3_relay(c, target):
        return pltpu.make_async_remote_copy(box3_in.at[c], box3_in.at[c], send3.at[c, 0], recv3.at[c],
                                            device_id=target, device_id_type=mesh_id)

    def rows_of(c):
        return pl.ds(pl.multiple_of(c * RELAY_ROWS, RELAY_ROWS), RELAY_ROWS)

    def copy5(k):
        return pltpu.make_async_remote_copy(own, box5.at[k], send5.at[k], recv5.at[k],
                                            device_id=(flip_bits(group, masks[k], order_bits), slab),
                                            device_id_type=mesh_id)

    for k in range(len(masks)):
        copy5(k).start()

    def copy4(c, k):
        return pltpu.make_async_remote_copy(incoming.at[rows_of(c)], box4.at[k, c], send4.at[c, k],
                                            recv4.at[c, k], device_id=(flip_bits(group, masks[k], order_bits), slab),
                                            device_id_type=mesh_id)

    def share(c):
        for k in range(len(masks)):
            copy4(c, k).start()

    def stage1(c, carry):
        rows = rows_of(c)
        own_add = total_add[rows, :]
        own_min = total_min[rows, :]

        @pl.when(pos == 0)
        def _():
            box1_out[c, 0] = own_add
            box1_out[c, 1] = own_min

        @pl.when(pos > 0)
        def _():
            copy1(c).wait_recv()
            got_add = box1_in[c, 0]
            got_min = box1_in[c, 1]
            before[0, rows, :] = got_add
            before[1, rows, :] = got_min
            new_add = got_add + own_add
            new_min = jnp.minimum(got_min + own_add, own_min)

            @pl.when(pos < last)
            def _():
                box1_out[c, 0] = new_add
                box1_out[c, 1] = new_min

            @pl.when(is_end)
            def _():
                line_total[0, rows, :] = new_add
                line_total[1, rows, :] = new_min

        @pl.when((pos == 0) & is_end)
        def _():
            line_total[0, rows, :] = own_add
            line_total[1, rows, :] = own_min

        @pl.when(pos < last)
        def _():
            copy1(c).start()

        return carry

    def stage2(c, carry):
        rows = rows_of(c)

        @pl.when(is_end & first_col)
        def _():
            incoming[rows, :] = jnp.where(pos > 0, before[1, rows, :], jnp.inf)
            share(c)
            box2_out[c] = line_total[1, rows, :]

        @pl.when(is_end & jnp.logical_not(first_col))
        def _():
            copy2(c).wait_recv()
            value = box2_in[c]
            incoming[rows, :] = jnp.where(
                pos > 0, jnp.minimum(value + before[0, rows, :], before[1, rows, :]), value)
            share(c)
            box2_out[c] = jnp.minimum(value + line_total[0, rows, :], line_total[1, rows, :])

            for k, p in enumerate(ends_to):
                copy3_from_end(c, k, at(col, p)).start()

        @pl.when(is_end & (col < lines - 1))
        def _():
            copy2(c).start()

        return carry

    def stages12(c, carry):
        stage1(c, carry)
        return stage2(c, carry)

    lax.fori_loop(0, chunks, stages12, 0)

    def stage3(c, carry):
        rows = rows_of(c)

        @pl.when(first_col & jnp.logical_not(is_end))
        def _():
            incoming[rows, :] = jnp.where(pos > 0, before[1, rows, :], jnp.inf)
            share(c)

        @pl.when(jnp.logical_not(first_col) & (in_up | in_down))
        def _():
            copy3_relay(c, at(col, 0)).wait_recv()
            value = box3_in[c]
            incoming[rows, :] = jnp.where(
                pos > 0, jnp.minimum(value + before[0, rows, :], before[1, rows, :]), value)
            share(c)

            @pl.when(in_up & up_next)
            def _():
                copy3_relay(c, at(col, pos + 1)).start()

            @pl.when(in_down & down_next)
            def _():
                copy3_relay(c, at(col, pos - 1)).start()

        return carry

    lax.fori_loop(0, chunks, stage3, 0)

    def gather(c, carry):
        rows = rows_of(c)
        least = incoming[rows, :]
        for k in range(len(masks)):
            copy4(c, k).wait_recv()
            least = jnp.minimum(least, box4[k, c])
        least_in[rows, :] = least
        return carry

    lax.fori_loop(0, chunks, gather, 0)

    for k in range(len(masks)):
        copy5(k).wait_recv()

    def gather_plane(c, carry):
        rows = rows_of(c)
        least = own[rows, :]
        for k in range(len(masks)):
            least = jnp.minimum(least, box5[k, rows, :])
        least_plane[rows, :] = least
        return carry

    lax.fori_loop(0, chunks, gather_plane, 0)

    def drain(c, carry):
        @pl.when(pos < last)
        def _():
            copy1(c).wait_send()

        @pl.when(is_end & (col < lines - 1))
        def _():
            copy2(c).wait_send()

        @pl.when(is_end & jnp.logical_not(first_col))
        def _():
            for k, p in enumerate(ends_to):
                copy3_from_end(c, k, at(col, p)).wait_send()

        @pl.when(jnp.logical_not(first_col) & ((in_up & up_next) | (in_down & down_next)))
        def _():
            copy3_relay(c, at(col, 0)).wait_send()

        for k in range(len(masks)):
            copy4(c, k).wait_send()
        return carry

    lax.fori_loop(0, chunks, drain, 0)
    for k in range(len(masks)):
        copy5(k).wait_send()


def relay(totals, own, slabs, orders):
    cells_y, cells_z = own.shape
    chunks = cells_y // RELAY_ROWS
    sharers = len(range(2, orders, 2))
    plane = jax.ShapeDtypeStruct(own.shape, jnp.float32)
    line = LINE if slabs % LINE == 0 else slabs
    vmem = pl.BlockSpec(memory_space=pltpu.VMEM)
    box = pltpu.VMEM((chunks, RELAY_ROWS, cells_z), jnp.float32)
    pair_box = pltpu.VMEM((chunks, 2, RELAY_ROWS, cells_z), jnp.float32)
    return pl.pallas_call(
        functools.partial(relay_kernel, line=line),
        out_shape=(plane, plane, plane),
        in_specs=[vmem, vmem],
        out_specs=(vmem, vmem, vmem),
        scratch_shapes=[
            pltpu.VMEM((2, cells_y, cells_z), jnp.float32),
            pltpu.VMEM((2, cells_y, cells_z), jnp.float32),
            pair_box,
            pair_box,
            box,
            box,
            box,
            pltpu.VMEM((max(sharers, 1), chunks, RELAY_ROWS, cells_z), jnp.float32),
            pltpu.VMEM((max(sharers, 1), cells_y, cells_z), jnp.float32),
            pltpu.SemaphoreType.DMA((chunks,)),
            pltpu.SemaphoreType.DMA((chunks,)),
            pltpu.SemaphoreType.DMA((chunks,)),
            pltpu.SemaphoreType.DMA((chunks,)),
            pltpu.SemaphoreType.DMA((chunks, 4)),
            pltpu.SemaphoreType.DMA((chunks,)),
            pltpu.SemaphoreType.DMA((chunks, max(sharers, 1))),
            pltpu.SemaphoreType.DMA((chunks, max(sharers, 1))),
            pltpu.SemaphoreType.DMA((max(sharers, 1),)),
            pltpu.SemaphoreType.DMA((max(sharers, 1),)),
        ],
        compiler_params=pltpu.CompilerParams(collective_id=0, has_side_effects=True),
    )(totals, own)


def shards(previous, fibre_tensor, tissue, stim_sites, stim_times):
    planes, cells_y, cells_z = previous.shape
    slabs = lax.axis_size("slab")
    orders = lax.axis_size("order")
    slab_index = lax.axis_index("slab")
    group_index = lax.axis_index("order")
    grid_step = 2.0 / (planes * slabs)

    plane_index = stim_sites // (cells_y * cells_z) - slab_index * planes
    row_index = stim_sites // cells_z % cells_y
    column_index = stim_sites % cells_z
    stims = jnp.stack([plane_index, row_index, column_index]).astype(jnp.int32)

    bits = jnp.stack([group_index % 2, group_index // 2 % 2, group_index // 4 % 2]).astype(jnp.int32)
    cost_x, field, totals, own_plane = local_sweeps(
        bits, stims, stim_times, fibre_tensor, tissue, previous, grid_step)

    core = group_index % 2
    incoming, least_in, least_plane = relay(totals, own_plane, slabs, orders)
    other = lax.ppermute(jnp.stack([least_plane, least_in]), "order", [(g, g ^ 1) for g in range(orders)])

    least0 = jnp.where(core == 0, least_plane, other[0])
    least1 = jnp.where(core == 0, other[0], least_plane)
    up_in = jnp.where(core == 0, least_in, other[1])
    down_in = jnp.where(core == 0, other[1], least_in)

    up_add = jnp.stack([cost_x[0], cost_x[0] + cost_x[1]])
    up_min = jnp.stack([field[0], jnp.minimum(field[0] + cost_x[1], field[1])])
    down_add = jnp.stack([cost_x[1] + cost_x[0], cost_x[1]])
    down_min = jnp.stack([jnp.minimum(field[1] + cost_x[0], field[0]), field[1]])
    backward_x = core == 1
    line_add = jnp.where(backward_x, down_add, up_add)
    line_min = jnp.where(backward_x, down_min, up_min)
    sweep_field = jnp.minimum(incoming[None] + line_add, line_min)

    least_local = jnp.stack([
        jnp.minimum(least0, least1 + cost_x[0]),
        jnp.minimum(least1, least0 + cost_x[1]),
    ])
    merged = jnp.minimum(
        least_local,
        jnp.minimum(up_in[None] + up_add, down_in[None] + down_add),
    )
    return (merged, sweep_field[None])


def solution(mesh):
    placed = (P("slab", None, None), P(None, "slab", None, None), P("slab", None, None), P(), P())
    return jax.shard_map(
        shards,
        mesh=mesh,
        in_specs=placed,
        out_specs=(P("slab", None, None), P("order", "slab", None, None)),
        check_vma=False,
    )
```

```python
import functools

import jax
import jax.numpy as jnp
from jax import lax
from jax.experimental import pallas as pl
from jax.experimental.pallas import tpu as pltpu
from jax.sharding import PartitionSpec as P

ROWS = 8
CHUNK = 32


def scan_step(a, m, k, axis, reverse, last):
    n = a.shape[axis]
    index = lax.broadcasted_iota(jnp.int32, a.shape, axis)
    shift = n - k if reverse else k
    valid = index < n - k if reverse else index >= k
    a_src = pltpu.roll(a, shift, axis)
    m_src = pltpu.roll(m, shift, axis)
    m = jnp.where(valid, jnp.minimum(m_src + a, m), m)
    if not last:
        a = jnp.where(valid, a_src + a, a)
    return a, m


def block_scan(a, m, axis, reverse, need_sum):
    n = a.shape[axis]
    k = 1
    while k < n:
        a, m = scan_step(a, m, k, axis, reverse, last=(2 * k >= n) and not need_sum)
        k *= 2
    return a, m


def lane_scan(step, seeded, reverse):
    width = step.shape[1]
    if width % 128 or width == 128:
        return block_scan(step, seeded, 1, reverse, False)[1]
    parts = []
    for i in range(width // 128):
        lanes = slice(i * 128, (i + 1) * 128)
        parts.append(block_scan(step[:, lanes], seeded[:, lanes], 1, reverse, True))
    order = range(len(parts) - 1, -1, -1) if reverse else range(len(parts))
    carry = None
    out = [None] * len(parts)
    for i in order:
        a, m = parts[i]
        if carry is not None:
            m = jnp.minimum(carry + a, m)
        edge = m[:, 0:1] if reverse else m[:, 127:128]
        carry = jnp.broadcast_to(edge, m.shape)
        out[i] = m
    return jnp.concatenate(out, axis=1)


def local_kernel(flags, stims, stim_times, fibre, tissue, previous, cost_x, field, totals, own,
                 cost_y, *, grid_step):
    planes, cells_y, cells_z = previous.shape
    chunks = cells_y // CHUNK
    inf = jnp.float32(jnp.inf)

    field[...] = previous[...]

    def seed(k, carry):
        p = stims[0, k]
        r = stims[1, k]
        c = stims[2, k]

        @pl.when((p >= 0) & (p < planes))
        def _():
            base = pl.multiple_of(r // ROWS * ROWS, ROWS)
            block = field[p, pl.ds(base, ROWS), :]
            row = lax.broadcasted_iota(jnp.int32, block.shape, 0)
            lane = lax.broadcasted_iota(jnp.int32, block.shape, 1)
            hit = (row == r - base) & (lane == c)
            field[p, pl.ds(base, ROWS), :] = jnp.where(hit, jnp.minimum(block, stim_times[k]), block)

        return carry

    lax.fori_loop(0, stims.shape[1], seed, 0)

    def costs_and_z(reverse):
        def body(i, carry):
            p = i // chunks
            rows = pl.ds(pl.multiple_of((i % chunks) * CHUNK, CHUNK), CHUNK)
            xx = fibre[0, p, rows, :]
            yy = fibre[1, p, rows, :]
            zz = fibre[2, p, rows, :]
            xy = fibre[3, p, rows, :]
            xz = fibre[4, p, rows, :]
            yz = fibre[5, p, rows, :]
            cx = yy * zz - yz * yz
            cy = xx * zz - xz * xz
            cz = xx * yy - xy * xy
            det = xx * cx - xy * (xy * zz - yz * xz) + xz * (xy * yz - yy * xz)
            factor = jnp.where(tissue[p, rows, :] == 1, 1.0, 4.0).astype(jnp.float32) * grid_step
            inverse = 1.0 / det
            cost_x[p, rows, :] = jnp.sqrt(cx * inverse) * factor
            cost_y[p, rows, :] = jnp.sqrt(cy * inverse) * factor
            step_z = jnp.sqrt(cz * inverse) * factor
            u = lane_scan(step_z, field[p, rows, :], reverse)
            field[p, rows, :] = u
            return carry

        lax.fori_loop(0, planes * chunks, body, 0, unroll=2)

    def sweep_y(reverse):
        def body(j, carry):
            i = chunks - 1 - j if reverse else j
            rows = pl.ds(pl.multiple_of(i * CHUNK, CHUNK), CHUNK)
            out = []
            for p in range(planes):
                a, m = block_scan(cost_y[p, rows, :], field[p, rows, :], 0, reverse, True)
                u = jnp.minimum(carry[p] + a, m)
                field[p, rows, :] = u
                edge = u[0:1, :] if reverse else u[CHUNK - 1:CHUNK, :]
                out.append(jnp.broadcast_to(edge, u.shape))
            return tuple(out)

        start = tuple(jnp.full((CHUNK, cells_z), inf, jnp.float32) for _ in range(planes))
        lax.fori_loop(0, chunks, body, start, unroll=2)

    for flag, fn in ((flags[2], costs_and_z), (flags[1], sweep_y)):
        pl.when(flag == 1)(functools.partial(fn, True))
        pl.when(flag != 1)(functools.partial(fn, False))

    def edge(i, carry):
        rows = pl.ds(pl.multiple_of(i * CHUNK, CHUNK), CHUNK)
        c0 = cost_x[0, rows, :]
        c1 = cost_x[1, rows, :]
        u0 = field[0, rows, :]
        u1 = field[1, rows, :]
        down = flags[0] == 1
        totals[0, rows, :] = jnp.where(down, c1 + c0, c0 + c1)
        totals[1, rows, :] = jnp.where(down, jnp.minimum(u1 + c0, u0), jnp.minimum(u0 + c1, u1))
        own[rows, :] = jnp.where(down, u1, u0)
        return carry

    lax.fori_loop(0, chunks, edge, 0)


def local_sweeps(flags, stims, stim_times, fibre, tissue, previous, grid_step):
    planes, cells_y, cells_z = previous.shape
    field = jax.ShapeDtypeStruct(previous.shape, jnp.float32)
    totals = jax.ShapeDtypeStruct((2, cells_y, cells_z), jnp.float32)
    own = jax.ShapeDtypeStruct((cells_y, cells_z), jnp.float32)
    vmem = pl.BlockSpec(memory_space=pltpu.VMEM)
    smem = pl.BlockSpec(memory_space=pltpu.SMEM)
    elements = planes * cells_y * cells_z
    return pl.pallas_call(
        functools.partial(local_kernel, grid_step=grid_step),
        out_shape=(field, field, totals, own),
        in_specs=[smem, smem, smem, vmem, vmem, vmem],
        out_specs=(vmem, vmem, vmem, vmem),
        scratch_shapes=[pltpu.VMEM(previous.shape, jnp.float32)],
        compiler_params=pltpu.CompilerParams(vmem_limit_bytes=48 * 1024 * 1024),
        cost_estimate=pl.CostEstimate(
            flops=300 * elements, transcendentals=6 * elements, bytes_accessed=40 * elements
        ),
    )(flags, stims, stim_times, fibre, tissue, previous)


RELAY_ROWS = 24
LINE = 8


def flip_bits(value, mask, bits):
    out = 0
    for j in range(bits):
        out = out + (2 ** j) * ((value // 2 ** j + (mask >> j) % 2) % 2)
    return out


def relay_kernel(totals, own, incoming, least_in, least_plane, before, line_total, box1_in,
                 box1_out, box2_in, box2_out, box3_in, box4, box5, send1, recv1, send2, recv2, send3,
                 recv3, send4, recv4, send5, recv5, *, line):
    total_add = totals.at[0]
    total_min = totals.at[1]
    cells_y, cells_z = incoming.shape
    chunks = cells_y // RELAY_ROWS
    slabs = lax.axis_size("slab")
    lines = slabs // line
    half = line // 2
    slab = lax.axis_index("slab")
    group = lax.axis_index("order")
    odd = group % 2
    rank = slab + odd * (slabs - 1 - 2 * slab)
    col = rank // line
    pos = rank % line
    last = line - 1
    mesh_id = pl.DeviceIdType.MESH

    def device(r):
        return (group, r + odd * (slabs - 1 - 2 * r))

    def at(c, p):
        return device(c * line + p)

    orders = lax.axis_size("order")
    masks = list(range(2, orders, 2))
    order_bits = max(orders - 1, 1).bit_length()
    first_col = col == 0
    is_end = pos == last
    in_up = pos < half
    in_down = (pos >= half) & (pos < last)
    up_next = (pos >= 1) & (pos + 1 < half)
    down_next = (pos <= last - 2) & (pos > half)
    ends_to = [p for p in (0, 1) if p < half] + [p for p in (last - 1, last - 2) if half <= p < last]

    barrier = pltpu.get_barrier_semaphore()
    neighbours = []
    neighbours.append((pos > 0, at(col, pos - 1)))
    neighbours.append((pos < last, at(col, pos + 1)))
    for p in ends_to:
        if p not in (last - 1,):
            neighbours.append(((pos == p) & (col > 0), at(col, last)))
            neighbours.append((is_end & (col > 0), at(col, p)))
    neighbours.append((is_end & (col > 0), at(col - 1, last)))
    neighbours.append((is_end & (col < lines - 1), at(col + 1, last)))
    for m in masks:
        neighbours.append((slab >= 0, (flip_bits(group, m, order_bits), slab)))
    count = jnp.int32(0)
    for cond, dev in neighbours:
        @pl.when(cond)
        def _():
            pl.semaphore_signal(barrier, 1, device_id=dev, device_id_type=mesh_id)

        count = count + cond.astype(jnp.int32)
    pl.semaphore_wait(barrier, count)

    def copy1(c):
        return pltpu.make_async_remote_copy(box1_out.at[c], box1_in.at[c], send1.at[c], recv1.at[c],
                                            device_id=at(col, pos + 1), device_id_type=mesh_id)

    def copy2(c):
        return pltpu.make_async_remote_copy(box2_out.at[c], box2_in.at[c], send2.at[c], recv2.at[c],
                                            device_id=at(col + 1, last), device_id_type=mesh_id)

    def copy3_from_end(c, k, target):
        return pltpu.make_async_remote_copy(box2_in.at[c], box3_in.at[c], send3.at[c, k], recv3.at[c],
                                            device_id=target, device_id_type=mesh_id)

    def copy3_relay(c, target):
        return pltpu.make_async_remote_copy(box3_in.at[c], box3_in.at[c], send3.at[c, 0], recv3.at[c],
                                            device_id=target, device_id_type=mesh_id)

    def rows_of(c):
        return pl.ds(pl.multiple_of(c * RELAY_ROWS, RELAY_ROWS), RELAY_ROWS)

    def copy5(k):
        return pltpu.make_async_remote_copy(own, box5.at[k], send5.at[k], recv5.at[k],
                                            device_id=(flip_bits(group, masks[k], order_bits), slab),
                                            device_id_type=mesh_id)

    for k in range(len(masks)):
        copy5(k).start()

    def copy4(c, k):
        return pltpu.make_async_remote_copy(incoming.at[rows_of(c)], box4.at[k, c], send4.at[c, k],
                                            recv4.at[c, k], device_id=(flip_bits(group, masks[k], order_bits), slab),
                                            device_id_type=mesh_id)

    def share(c):
        for k in range(len(masks)):
            copy4(c, k).start()

    def stage1(c, carry):
        rows = rows_of(c)
        own_add = total_add[rows, :]
        own_min = total_min[rows, :]

        @pl.when(pos == 0)
        def _():
            box1_out[c, 0] = own_add
            box1_out[c, 1] = own_min

        @pl.when(pos > 0)
        def _():
            copy1(c).wait_recv()
            got_add = box1_in[c, 0]
            got_min = box1_in[c, 1]
            before[0, rows, :] = got_add
            before[1, rows, :] = got_min
            new_add = got_add + own_add
            new_min = jnp.minimum(got_min + own_add, own_min)

            @pl.when(pos < last)
            def _():
                box1_out[c, 0] = new_add
                box1_out[c, 1] = new_min

            @pl.when(is_end)
            def _():
                line_total[0, rows, :] = new_add
                line_total[1, rows, :] = new_min

        @pl.when((pos == 0) & is_end)
        def _():
            line_total[0, rows, :] = own_add
            line_total[1, rows, :] = own_min

        @pl.when(pos < last)
        def _():
            copy1(c).start()

        return carry

    def stage2(c, carry):
        rows = rows_of(c)

        @pl.when(is_end & first_col)
        def _():
            incoming[rows, :] = jnp.where(pos > 0, before[1, rows, :], jnp.inf)
            share(c)
            box2_out[c] = line_total[1, rows, :]

        @pl.when(is_end & jnp.logical_not(first_col))
        def _():
            copy2(c).wait_recv()
            value = box2_in[c]
            incoming[rows, :] = jnp.where(
                pos > 0, jnp.minimum(value + before[0, rows, :], before[1, rows, :]), value)
            share(c)
            box2_out[c] = jnp.minimum(value + line_total[0, rows, :], line_total[1, rows, :])

            for k, p in enumerate(ends_to):
                copy3_from_end(c, k, at(col, p)).start()

        @pl.when(is_end & (col < lines - 1))
        def _():
            copy2(c).start()

        return carry

    def stages12(c, carry):
        stage1(c, carry)
        return stage2(c, carry)

    lax.fori_loop(0, chunks, stages12, 0)

    def stage3(c, carry):
        rows = rows_of(c)

        @pl.when(first_col & jnp.logical_not(is_end))
        def _():
            incoming[rows, :] = jnp.where(pos > 0, before[1, rows, :], jnp.inf)
            share(c)

        @pl.when(jnp.logical_not(first_col) & (in_up | in_down))
        def _():
            copy3_relay(c, at(col, 0)).wait_recv()
            value = box3_in[c]
            incoming[rows, :] = jnp.where(
                pos > 0, jnp.minimum(value + before[0, rows, :], before[1, rows, :]), value)
            share(c)

            @pl.when(in_up & up_next)
            def _():
                copy3_relay(c, at(col, pos + 1)).start()

            @pl.when(in_down & down_next)
            def _():
                copy3_relay(c, at(col, pos - 1)).start()

        return carry

    lax.fori_loop(0, chunks, stage3, 0)

    def gather(c, carry):
        rows = rows_of(c)
        least = incoming[rows, :]
        for k in range(len(masks)):
            copy4(c, k).wait_recv()
            least = jnp.minimum(least, box4[k, c])
        least_in[rows, :] = least
        return carry

    lax.fori_loop(0, chunks, gather, 0)

    for k in range(len(masks)):
        copy5(k).wait_recv()

    def gather_plane(c, carry):
        rows = rows_of(c)
        least = own[rows, :]
        for k in range(len(masks)):
            least = jnp.minimum(least, box5[k, rows, :])
        least_plane[rows, :] = least
        return carry

    lax.fori_loop(0, chunks, gather_plane, 0)

    def drain(c, carry):
        @pl.when(pos < last)
        def _():
            copy1(c).wait_send()

        @pl.when(is_end & (col < lines - 1))
        def _():
            copy2(c).wait_send()

        @pl.when(is_end & jnp.logical_not(first_col))
        def _():
            for k, p in enumerate(ends_to):
                copy3_from_end(c, k, at(col, p)).wait_send()

        @pl.when(jnp.logical_not(first_col) & ((in_up & up_next) | (in_down & down_next)))
        def _():
            copy3_relay(c, at(col, 0)).wait_send()

        for k in range(len(masks)):
            copy4(c, k).wait_send()
        return carry

    lax.fori_loop(0, chunks, drain, 0)
    for k in range(len(masks)):
        copy5(k).wait_send()


def relay(totals, own, slabs, orders):
    cells_y, cells_z = own.shape
    chunks = cells_y // RELAY_ROWS
    sharers = len(range(2, orders, 2))
    plane = jax.ShapeDtypeStruct(own.shape, jnp.float32)
    line = LINE if slabs % LINE == 0 else slabs
    vmem = pl.BlockSpec(memory_space=pltpu.VMEM)
    box = pltpu.VMEM((chunks, RELAY_ROWS, cells_z), jnp.float32)
    pair_box = pltpu.VMEM((chunks, 2, RELAY_ROWS, cells_z), jnp.float32)
    return pl.pallas_call(
        functools.partial(relay_kernel, line=line),
        out_shape=(plane, plane, plane),
        in_specs=[vmem, vmem],
        out_specs=(vmem, vmem, vmem),
        scratch_shapes=[
            pltpu.VMEM((2, cells_y, cells_z), jnp.float32),
            pltpu.VMEM((2, cells_y, cells_z), jnp.float32),
            pair_box,
            pair_box,
            box,
            box,
            box,
            pltpu.VMEM((max(sharers, 1), chunks, RELAY_ROWS, cells_z), jnp.float32),
            pltpu.VMEM((max(sharers, 1), cells_y, cells_z), jnp.float32),
            pltpu.SemaphoreType.DMA((chunks,)),
            pltpu.SemaphoreType.DMA((chunks,)),
            pltpu.SemaphoreType.DMA((chunks,)),
            pltpu.SemaphoreType.DMA((chunks,)),
            pltpu.SemaphoreType.DMA((chunks, 4)),
            pltpu.SemaphoreType.DMA((chunks,)),
            pltpu.SemaphoreType.DMA((chunks, max(sharers, 1))),
            pltpu.SemaphoreType.DMA((chunks, max(sharers, 1))),
            pltpu.SemaphoreType.DMA((max(sharers, 1),)),
            pltpu.SemaphoreType.DMA((max(sharers, 1),)),
        ],
        compiler_params=pltpu.CompilerParams(collective_id=0, has_side_effects=True),
    )(totals, own)


def shards(previous, fibre_tensor, tissue, stim_sites, stim_times):
    planes, cells_y, cells_z = previous.shape
    slabs = lax.axis_size("slab")
    orders = lax.axis_size("order")
    slab_index = lax.axis_index("slab")
    group_index = lax.axis_index("order")
    grid_step = 2.0 / (planes * slabs)

    plane_index = stim_sites // (cells_y * cells_z) - slab_index * planes
    row_index = stim_sites // cells_z % cells_y
    column_index = stim_sites % cells_z
    stims = jnp.stack([plane_index, row_index, column_index]).astype(jnp.int32)

    bits = jnp.stack([group_index % 2, group_index // 2 % 2, group_index // 4 % 2]).astype(jnp.int32)
    cost_x, field, totals, own_plane = local_sweeps(
        bits, stims, stim_times, fibre_tensor, tissue, previous, grid_step)

    core = group_index % 2
    incoming, least_in, least_plane = relay(totals, own_plane, slabs, orders)
    other = lax.ppermute(jnp.stack([least_plane, least_in]), "order", [(g, g ^ 1) for g in range(orders)])

    least0 = jnp.where(core == 0, least_plane, other[0])
    least1 = jnp.where(core == 0, other[0], least_plane)
    up_in = jnp.where(core == 0, least_in, other[1])
    down_in = jnp.where(core == 0, other[1], least_in)

    up_add = jnp.stack([cost_x[0], cost_x[0] + cost_x[1]])
    up_min = jnp.stack([field[0], jnp.minimum(field[0] + cost_x[1], field[1])])
    down_add = jnp.stack([cost_x[1] + cost_x[0], cost_x[1]])
    down_min = jnp.stack([jnp.minimum(field[1] + cost_x[0], field[0]), field[1]])
    backward_x = core == 1
    line_add = jnp.where(backward_x, down_add, up_add)
    line_min = jnp.where(backward_x, down_min, up_min)
    sweep_field = jnp.minimum(incoming[None] + line_add, line_min)

    least_local = jnp.stack([
        jnp.minimum(least0, least1 + cost_x[0]),
        jnp.minimum(least1, least0 + cost_x[1]),
    ])
    merged = jnp.minimum(
        least_local,
        jnp.minimum(up_in[None] + up_add, down_in[None] + down_add),
    )
    return (merged, sweep_field[None])


def solution(mesh):
    placed = (P("slab", None, None), P(None, "slab", None, None), P("slab", None, None), P(), P())
    return jax.shard_map(
        shards,
        mesh=mesh,
        in_specs=placed,
        out_specs=(P("slab", None, None), P("order", "slab", None, None)),
        check_vma=False,
    )
```

```python
import functools

import jax
import jax.numpy as jnp
from jax import lax
from jax.experimental import pallas as pl
from jax.experimental.pallas import tpu as pltpu
from jax.sharding import PartitionSpec as P

ROWS = 8
CHUNK = 32


def scan_step(a, m, k, axis, reverse, last):
    n = a.shape[axis]
    index = lax.broadcasted_iota(jnp.int32, a.shape, axis)
    shift = n - k if reverse else k
    valid = index < n - k if reverse else index >= k
    a_src = pltpu.roll(a, shift, axis)
    m_src = pltpu.roll(m, shift, axis)
    m = jnp.where(valid, jnp.minimum(m_src + a, m), m)
    if not last:
        a = jnp.where(valid, a_src + a, a)
    return a, m


def block_scan(a, m, axis, reverse, need_sum):
    n = a.shape[axis]
    k = 1
    while k < n:
        a, m = scan_step(a, m, k, axis, reverse, last=(2 * k >= n) and not need_sum)
        k *= 2
    return a, m


def lane_scan(step, seeded, reverse):
    width = step.shape[1]
    if width % 128 or width == 128:
        return block_scan(step, seeded, 1, reverse, False)[1]
    parts = []
    for i in range(width // 128):
        lanes = slice(i * 128, (i + 1) * 128)
        parts.append(block_scan(step[:, lanes], seeded[:, lanes], 1, reverse, True))
    order = range(len(parts) - 1, -1, -1) if reverse else range(len(parts))
    carry = None
    out = [None] * len(parts)
    for i in order:
        a, m = parts[i]
        if carry is not None:
            m = jnp.minimum(carry + a, m)
        edge = m[:, 0:1] if reverse else m[:, 127:128]
        carry = jnp.broadcast_to(edge, m.shape)
        out[i] = m
    return jnp.concatenate(out, axis=1)


def local_kernel(flags, stims, stim_times, fibre, tissue, previous, cost_x, field, totals, own,
                 cost_y, *, grid_step):
    planes, cells_y, cells_z = previous.shape
    chunks = cells_y // CHUNK
    inf = jnp.float32(jnp.inf)

    field[...] = previous[...]

    def seed(k, carry):
        p = stims[0, k]
        r = stims[1, k]
        c = stims[2, k]

        @pl.when((p >= 0) & (p < planes))
        def _():
            base = pl.multiple_of(r // ROWS * ROWS, ROWS)
            block = field[p, pl.ds(base, ROWS), :]
            row = lax.broadcasted_iota(jnp.int32, block.shape, 0)
            lane = lax.broadcasted_iota(jnp.int32, block.shape, 1)
            hit = (row == r - base) & (lane == c)
            field[p, pl.ds(base, ROWS), :] = jnp.where(hit, jnp.minimum(block, stim_times[k]), block)

        return carry

    lax.fori_loop(0, stims.shape[1], seed, 0)

    def costs_and_z(reverse):
        def body(i, carry):
            p = i // chunks
            rows = pl.ds(pl.multiple_of((i % chunks) * CHUNK, CHUNK), CHUNK)
            xx = fibre[0, p, rows, :]
            yy = fibre[1, p, rows, :]
            zz = fibre[2, p, rows, :]
            xy = fibre[3, p, rows, :]
            xz = fibre[4, p, rows, :]
            yz = fibre[5, p, rows, :]
            cx = yy * zz - yz * yz
            cy = xx * zz - xz * xz
            cz = xx * yy - xy * xy
            det = xx * cx - xy * (xy * zz - yz * xz) + xz * (xy * yz - yy * xz)
            factor = jnp.where(tissue[p, rows, :] == 1, 1.0, 4.0).astype(jnp.float32) * grid_step
            inverse = 1.0 / det
            cost_x[p, rows, :] = jnp.sqrt(cx * inverse) * factor
            cost_y[p, rows, :] = jnp.sqrt(cy * inverse) * factor
            step_z = jnp.sqrt(cz * inverse) * factor
            u = lane_scan(step_z, field[p, rows, :], reverse)
            field[p, rows, :] = u
            return carry

        lax.fori_loop(0, planes * chunks, body, 0, unroll=2)

    def sweep_y(reverse):
        def body(j, carry):
            i = chunks - 1 - j if reverse else j
            rows = pl.ds(pl.multiple_of(i * CHUNK, CHUNK), CHUNK)
            out = []
            for p in range(planes):
                a, m = block_scan(cost_y[p, rows, :], field[p, rows, :], 0, reverse, True)
                u = jnp.minimum(carry[p] + a, m)
                field[p, rows, :] = u
                edge = u[0:1, :] if reverse else u[CHUNK - 1:CHUNK, :]
                out.append(jnp.broadcast_to(edge, u.shape))
            return tuple(out)

        start = tuple(jnp.full((CHUNK, cells_z), inf, jnp.float32) for _ in range(planes))
        lax.fori_loop(0, chunks, body, start, unroll=2)

    for flag, fn in ((flags[2], costs_and_z), (flags[1], sweep_y)):
        pl.when(flag == 1)(functools.partial(fn, True))
        pl.when(flag != 1)(functools.partial(fn, False))

    def edge(i, carry):
        rows = pl.ds(pl.multiple_of(i * CHUNK, CHUNK), CHUNK)
        c0 = cost_x[0, rows, :]
        c1 = cost_x[1, rows, :]
        u0 = field[0, rows, :]
        u1 = field[1, rows, :]
        down = flags[0] == 1
        totals[0, rows, :] = jnp.where(down, c1 + c0, c0 + c1)
        totals[1, rows, :] = jnp.where(down, jnp.minimum(u1 + c0, u0), jnp.minimum(u0 + c1, u1))
        own[rows, :] = jnp.where(down, u1, u0)
        return carry

    lax.fori_loop(0, chunks, edge, 0)


def local_sweeps(flags, stims, stim_times, fibre, tissue, previous, grid_step):
    planes, cells_y, cells_z = previous.shape
    field = jax.ShapeDtypeStruct(previous.shape, jnp.float32)
    totals = jax.ShapeDtypeStruct((2, cells_y, cells_z), jnp.float32)
    own = jax.ShapeDtypeStruct((cells_y, cells_z), jnp.float32)
    vmem = pl.BlockSpec(memory_space=pltpu.VMEM)
    smem = pl.BlockSpec(memory_space=pltpu.SMEM)
    elements = planes * cells_y * cells_z
    return pl.pallas_call(
        functools.partial(local_kernel, grid_step=grid_step),
        out_shape=(field, field, totals, own),
        in_specs=[smem, smem, smem, vmem, vmem, vmem],
        out_specs=(vmem, vmem, vmem, vmem),
        scratch_shapes=[pltpu.VMEM(previous.shape, jnp.float32)],
        compiler_params=pltpu.CompilerParams(vmem_limit_bytes=48 * 1024 * 1024),
        cost_estimate=pl.CostEstimate(
            flops=300 * elements, transcendentals=6 * elements, bytes_accessed=40 * elements
        ),
    )(flags, stims, stim_times, fibre, tissue, previous)


RELAY_ROWS = 16
LINE = 8


def flip_bits(value, mask, bits):
    out = 0
    for j in range(bits):
        out = out + (2 ** j) * ((value // 2 ** j + (mask >> j) % 2) % 2)
    return out


def relay_kernel(totals, own, incoming, least_in, least_plane, before, line_total, box1_in,
                 box1_out, box2_in, box2_out, box3_in, box4, box5, send1, recv1, send2, recv2, send3,
                 recv3, send4, recv4, send5, recv5, *, line):
    total_add = totals.at[0]
    total_min = totals.at[1]
    cells_y, cells_z = incoming.shape
    chunks = cells_y // RELAY_ROWS
    slabs = lax.axis_size("slab")
    lines = slabs // line
    half = line // 2
    slab = lax.axis_index("slab")
    group = lax.axis_index("order")
    odd = group % 2
    rank = slab + odd * (slabs - 1 - 2 * slab)
    col = rank // line
    pos = rank % line
    last = line - 1
    mesh_id = pl.DeviceIdType.MESH

    def device(r):
        return (group, r + odd * (slabs - 1 - 2 * r))

    def at(c, p):
        return device(c * line + p)

    orders = lax.axis_size("order")
    masks = list(range(2, orders, 2))
    order_bits = max(orders - 1, 1).bit_length()
    first_col = col == 0
    is_end = pos == last
    in_up = pos < half
    in_down = (pos >= half) & (pos < last)
    up_next = (pos >= 1) & (pos + 1 < half)
    down_next = (pos <= last - 2) & (pos > half)
    ends_to = [p for p in (0, 1) if p < half] + [p for p in (last - 1, last - 2) if half <= p < last]

    barrier = pltpu.get_barrier_semaphore()
    neighbours = []
    neighbours.append((pos > 0, at(col, pos - 1)))
    neighbours.append((pos < last, at(col, pos + 1)))
    for p in ends_to:
        if p not in (last - 1,):
            neighbours.append(((pos == p) & (col > 0), at(col, last)))
            neighbours.append((is_end & (col > 0), at(col, p)))
    neighbours.append((is_end & (col > 0), at(col - 1, last)))
    neighbours.append((is_end & (col < lines - 1), at(col + 1, last)))
    for m in masks:
        neighbours.append((slab >= 0, (flip_bits(group, m, order_bits), slab)))
    count = jnp.int32(0)
    for cond, dev in neighbours:
        @pl.when(cond)
        def _():
            pl.semaphore_signal(barrier, 1, device_id=dev, device_id_type=mesh_id)

        count = count + cond.astype(jnp.int32)
    pl.semaphore_wait(barrier, count)

    def copy1(c):
        return pltpu.make_async_remote_copy(box1_out.at[c], box1_in.at[c], send1.at[c], recv1.at[c],
                                            device_id=at(col, pos + 1), device_id_type=mesh_id)

    def copy2(c):
        return pltpu.make_async_remote_copy(box2_out.at[c], box2_in.at[c], send2.at[c], recv2.at[c],
                                            device_id=at(col + 1, last), device_id_type=mesh_id)

    def copy3_from_end(c, k, target):
        return pltpu.make_async_remote_copy(box2_in.at[c], box3_in.at[c], send3.at[c, k], recv3.at[c],
                                            device_id=target, device_id_type=mesh_id)

    def copy3_relay(c, target):
        return pltpu.make_async_remote_copy(box3_in.at[c], box3_in.at[c], send3.at[c, 0], recv3.at[c],
                                            device_id=target, device_id_type=mesh_id)

    def rows_of(c):
        return pl.ds(pl.multiple_of(c * RELAY_ROWS, RELAY_ROWS), RELAY_ROWS)

    def copy5(k):
        return pltpu.make_async_remote_copy(own, box5.at[k], send5.at[k], recv5.at[k],
                                            device_id=(flip_bits(group, masks[k], order_bits), slab),
                                            device_id_type=mesh_id)

    for k in range(len(masks)):
        copy5(k).start()

    def copy4(c, k):
        return pltpu.make_async_remote_copy(incoming.at[rows_of(c)], box4.at[k, c], send4.at[c, k],
                                            recv4.at[c, k], device_id=(flip_bits(group, masks[k], order_bits), slab),
                                            device_id_type=mesh_id)

    def share(c):
        for k in range(len(masks)):
            copy4(c, k).start()

    def stage1(c, carry):
        rows = rows_of(c)
        own_add = total_add[rows, :]
        own_min = total_min[rows, :]

        @pl.when(pos == 0)
        def _():
            box1_out[c, 0] = own_add
            box1_out[c, 1] = own_min
            if last > 0:
                copy1(c).start()

        @pl.when(pos > 0)
        def _():
            copy1(c).wait_recv()
            got_add = box1_in[c, 0]
            got_min = box1_in[c, 1]
            new_add = got_add + own_add
            new_min = jnp.minimum(got_min + own_add, own_min)

            @pl.when(pos < last)
            def _():
                box1_out[c, 0] = new_add
                box1_out[c, 1] = new_min
                copy1(c).start()

            before[0, rows, :] = got_add
            before[1, rows, :] = got_min

            @pl.when(is_end)
            def _():
                line_total[0, rows, :] = new_add
                line_total[1, rows, :] = new_min

        @pl.when((pos == 0) & is_end)
        def _():
            line_total[0, rows, :] = own_add
            line_total[1, rows, :] = own_min

        return carry

    def stage2(c, carry):
        rows = rows_of(c)

        @pl.when(is_end & first_col)
        def _():
            incoming[rows, :] = jnp.where(pos > 0, before[1, rows, :], jnp.inf)
            share(c)
            box2_out[c] = line_total[1, rows, :]

        @pl.when(is_end & jnp.logical_not(first_col))
        def _():
            copy2(c).wait_recv()
            value = box2_in[c]
            incoming[rows, :] = jnp.where(
                pos > 0, jnp.minimum(value + before[0, rows, :], before[1, rows, :]), value)
            share(c)
            box2_out[c] = jnp.minimum(value + line_total[0, rows, :], line_total[1, rows, :])

            for k, p in enumerate(ends_to):
                copy3_from_end(c, k, at(col, p)).start()

        @pl.when(is_end & (col < lines - 1))
        def _():
            copy2(c).start()

        return carry

    def stages12(c, carry):
        stage1(c, carry)
        return stage2(c, carry)

    lax.fori_loop(0, chunks, stages12, 0)

    def stage3(c, carry):
        rows = rows_of(c)

        @pl.when(first_col & jnp.logical_not(is_end))
        def _():
            incoming[rows, :] = jnp.where(pos > 0, before[1, rows, :], jnp.inf)
            share(c)

        @pl.when(jnp.logical_not(first_col) & (in_up | in_down))
        def _():
            copy3_relay(c, at(col, 0)).wait_recv()
            value = box3_in[c]
            incoming[rows, :] = jnp.where(
                pos > 0, jnp.minimum(value + before[0, rows, :], before[1, rows, :]), value)
            share(c)

            @pl.when(in_up & up_next)
            def _():
                copy3_relay(c, at(col, pos + 1)).start()

            @pl.when(in_down & down_next)
            def _():
                copy3_relay(c, at(col, pos - 1)).start()

        return carry

    lax.fori_loop(0, chunks, stage3, 0)

    def gather(c, carry):
        rows = rows_of(c)
        least = incoming[rows, :]
        for k in range(len(masks)):
            copy4(c, k).wait_recv()
            least = jnp.minimum(least, box4[k, c])
        least_in[rows, :] = least
        return carry

    lax.fori_loop(0, chunks, gather, 0)

    for k in range(len(masks)):
        copy5(k).wait_recv()

    def gather_plane(c, carry):
        rows = rows_of(c)
        least = own[rows, :]
        for k in range(len(masks)):
            least = jnp.minimum(least, box5[k, rows, :])
        least_plane[rows, :] = least
        return carry

    lax.fori_loop(0, chunks, gather_plane, 0)

    def drain(c, carry):
        @pl.when(pos < last)
        def _():
            copy1(c).wait_send()

        @pl.when(is_end & (col < lines - 1))
        def _():
            copy2(c).wait_send()

        @pl.when(is_end & jnp.logical_not(first_col))
        def _():
            for k, p in enumerate(ends_to):
                copy3_from_end(c, k, at(col, p)).wait_send()

        @pl.when(jnp.logical_not(first_col) & ((in_up & up_next) | (in_down & down_next)))
        def _():
            copy3_relay(c, at(col, 0)).wait_send()

        for k in range(len(masks)):
            copy4(c, k).wait_send()
        return carry

    lax.fori_loop(0, chunks, drain, 0)
    for k in range(len(masks)):
        copy5(k).wait_send()


def relay(totals, own, slabs, orders):
    cells_y, cells_z = own.shape
    chunks = cells_y // RELAY_ROWS
    sharers = len(range(2, orders, 2))
    plane = jax.ShapeDtypeStruct(own.shape, jnp.float32)
    line = LINE if slabs % LINE == 0 else slabs
    vmem = pl.BlockSpec(memory_space=pltpu.VMEM)
    box = pltpu.VMEM((chunks, RELAY_ROWS, cells_z), jnp.float32)
    pair_box = pltpu.VMEM((chunks, 2, RELAY_ROWS, cells_z), jnp.float32)
    return pl.pallas_call(
        functools.partial(relay_kernel, line=line),
        out_shape=(plane, plane, plane),
        in_specs=[vmem, vmem],
        out_specs=(vmem, vmem, vmem),
        scratch_shapes=[
            pltpu.VMEM((2, cells_y, cells_z), jnp.float32),
            pltpu.VMEM((2, cells_y, cells_z), jnp.float32),
            pair_box,
            pair_box,
            box,
            box,
            box,
            pltpu.VMEM((max(sharers, 1), chunks, RELAY_ROWS, cells_z), jnp.float32),
            pltpu.VMEM((max(sharers, 1), cells_y, cells_z), jnp.float32),
            pltpu.SemaphoreType.DMA((chunks,)),
            pltpu.SemaphoreType.DMA((chunks,)),
            pltpu.SemaphoreType.DMA((chunks,)),
            pltpu.SemaphoreType.DMA((chunks,)),
            pltpu.SemaphoreType.DMA((chunks, 4)),
            pltpu.SemaphoreType.DMA((chunks,)),
            pltpu.SemaphoreType.DMA((chunks, max(sharers, 1))),
            pltpu.SemaphoreType.DMA((chunks, max(sharers, 1))),
            pltpu.SemaphoreType.DMA((max(sharers, 1),)),
            pltpu.SemaphoreType.DMA((max(sharers, 1),)),
        ],
        compiler_params=pltpu.CompilerParams(collective_id=0, has_side_effects=True),
    )(totals, own)


def shards(previous, fibre_tensor, tissue, stim_sites, stim_times):
    planes, cells_y, cells_z = previous.shape
    slabs = lax.axis_size("slab")
    orders = lax.axis_size("order")
    slab_index = lax.axis_index("slab")
    group_index = lax.axis_index("order")
    grid_step = 2.0 / (planes * slabs)

    plane_index = stim_sites // (cells_y * cells_z) - slab_index * planes
    row_index = stim_sites // cells_z % cells_y
    column_index = stim_sites % cells_z
    stims = jnp.stack([plane_index, row_index, column_index]).astype(jnp.int32)

    bits = jnp.stack([group_index % 2, group_index // 2 % 2, group_index // 4 % 2]).astype(jnp.int32)
    cost_x, field, totals, own_plane = local_sweeps(
        bits, stims, stim_times, fibre_tensor, tissue, previous, grid_step)

    core = group_index % 2
    incoming, least_in, least_plane = relay(totals, own_plane, slabs, orders)
    other = lax.ppermute(jnp.stack([least_plane, least_in]), "order", [(g, g ^ 1) for g in range(orders)])

    least0 = jnp.where(core == 0, least_plane, other[0])
    least1 = jnp.where(core == 0, other[0], least_plane)
    up_in = jnp.where(core == 0, least_in, other[1])
    down_in = jnp.where(core == 0, other[1], least_in)

    up_add = jnp.stack([cost_x[0], cost_x[0] + cost_x[1]])
    up_min = jnp.stack([field[0], jnp.minimum(field[0] + cost_x[1], field[1])])
    down_add = jnp.stack([cost_x[1] + cost_x[0], cost_x[1]])
    down_min = jnp.stack([jnp.minimum(field[1] + cost_x[0], field[0]), field[1]])
    backward_x = core == 1
    line_add = jnp.where(backward_x, down_add, up_add)
    line_min = jnp.where(backward_x, down_min, up_min)
    sweep_field = jnp.minimum(incoming[None] + line_add, line_min)

    least_local = jnp.stack([
        jnp.minimum(least0, least1 + cost_x[0]),
        jnp.minimum(least1, least0 + cost_x[1]),
    ])
    merged = jnp.minimum(
        least_local,
        jnp.minimum(up_in[None] + up_add, down_in[None] + down_add),
    )
    return (merged, sweep_field[None])


def solution(mesh):
    placed = (P("slab", None, None), P(None, "slab", None, None), P("slab", None, None), P(), P())
    return jax.shard_map(
        shards,
        mesh=mesh,
        in_specs=placed,
        out_specs=(P("slab", None, None), P("order", "slab", None, None)),
        check_vma=False,
    )
```

```python
import functools

import jax
import jax.numpy as jnp
from jax import lax
from jax.experimental import pallas as pl
from jax.experimental.pallas import tpu as pltpu
from jax.sharding import PartitionSpec as P

ROWS = 8
CHUNK = 16


def scan_step(a, m, k, axis, reverse, last):
    n = a.shape[axis]
    index = lax.broadcasted_iota(jnp.int32, a.shape, axis)
    shift = n - k if reverse else k
    valid = index < n - k if reverse else index >= k
    a_src = pltpu.roll(a, shift, axis)
    m_src = pltpu.roll(m, shift, axis)
    m = jnp.where(valid, jnp.minimum(m_src + a, m), m)
    if not last:
        a = jnp.where(valid, a_src + a, a)
    return a, m


def block_scan(a, m, axis, reverse, need_sum):
    n = a.shape[axis]
    k = 1
    while k < n:
        a, m = scan_step(a, m, k, axis, reverse, last=(2 * k >= n) and not need_sum)
        k *= 2
    return a, m


def lane_scan(step, seeded, reverse):
    width = step.shape[1]
    if width % 128 or width == 128:
        return block_scan(step, seeded, 1, reverse, False)[1]
    parts = []
    for i in range(width // 128):
        lanes = slice(i * 128, (i + 1) * 128)
        parts.append(block_scan(step[:, lanes], seeded[:, lanes], 1, reverse, True))
    order = range(len(parts) - 1, -1, -1) if reverse else range(len(parts))
    carry = None
    out = [None] * len(parts)
    for i in order:
        a, m = parts[i]
        if carry is not None:
            m = jnp.minimum(carry + a, m)
        edge = m[:, 0:1] if reverse else m[:, 127:128]
        carry = jnp.broadcast_to(edge, m.shape)
        out[i] = m
    return jnp.concatenate(out, axis=1)


def local_kernel(flags, stims, stim_times, fibre, tissue, previous, cost_x, field, totals, own,
                 cost_y, *, grid_step):
    planes, cells_y, cells_z = previous.shape
    chunks = cells_y // CHUNK
    inf = jnp.float32(jnp.inf)

    field[...] = previous[...]

    def seed(k, carry):
        p = stims[0, k]
        r = stims[1, k]
        c = stims[2, k]

        @pl.when((p >= 0) & (p < planes))
        def _():
            base = pl.multiple_of(r // ROWS * ROWS, ROWS)
            block = field[p, pl.ds(base, ROWS), :]
            row = lax.broadcasted_iota(jnp.int32, block.shape, 0)
            lane = lax.broadcasted_iota(jnp.int32, block.shape, 1)
            hit = (row == r - base) & (lane == c)
            field[p, pl.ds(base, ROWS), :] = jnp.where(hit, jnp.minimum(block, stim_times[k]), block)

        return carry

    lax.fori_loop(0, stims.shape[1], seed, 0)

    def costs_and_z(reverse):
        def body(i, carry):
            p = i // chunks
            rows = pl.ds(pl.multiple_of((i % chunks) * CHUNK, CHUNK), CHUNK)
            xx = fibre[0, p, rows, :]
            yy = fibre[1, p, rows, :]
            zz = fibre[2, p, rows, :]
            xy = fibre[3, p, rows, :]
            xz = fibre[4, p, rows, :]
            yz = fibre[5, p, rows, :]
            cx = yy * zz - yz * yz
            cy = xx * zz - xz * xz
            cz = xx * yy - xy * xy
            det = xx * cx - xy * (xy * zz - yz * xz) + xz * (xy * yz - yy * xz)
            factor = jnp.where(tissue[p, rows, :] == 1, 1.0, 4.0).astype(jnp.float32) * grid_step
            inverse = 1.0 / det
            cost_x[p, rows, :] = jnp.sqrt(cx * inverse) * factor
            cost_y[p, rows, :] = jnp.sqrt(cy * inverse) * factor
            step_z = jnp.sqrt(cz * inverse) * factor
            u = lane_scan(step_z, field[p, rows, :], reverse)
            field[p, rows, :] = u
            return carry

        lax.fori_loop(0, planes * chunks, body, 0, unroll=2)

    def sweep_y(reverse):
        def body(j, carry):
            i = chunks - 1 - j if reverse else j
            rows = pl.ds(pl.multiple_of(i * CHUNK, CHUNK), CHUNK)
            out = []
            for p in range(planes):
                a, m = block_scan(cost_y[p, rows, :], field[p, rows, :], 0, reverse, True)
                u = jnp.minimum(carry[p] + a, m)
                field[p, rows, :] = u
                edge = u[0:1, :] if reverse else u[CHUNK - 1:CHUNK, :]
                out.append(jnp.broadcast_to(edge, u.shape))
            return tuple(out)

        start = tuple(jnp.full((CHUNK, cells_z), inf, jnp.float32) for _ in range(planes))
        lax.fori_loop(0, chunks, body, start, unroll=2)

    for flag, fn in ((flags[2], costs_and_z), (flags[1], sweep_y)):
        pl.when(flag == 1)(functools.partial(fn, True))
        pl.when(flag != 1)(functools.partial(fn, False))

    def edge(i, carry):
        rows = pl.ds(pl.multiple_of(i * CHUNK, CHUNK), CHUNK)
        c0 = cost_x[0, rows, :]
        c1 = cost_x[1, rows, :]
        u0 = field[0, rows, :]
        u1 = field[1, rows, :]
        down = flags[0] == 1
        totals[0, rows, :] = jnp.where(down, c1 + c0, c0 + c1)
        totals[1, rows, :] = jnp.where(down, jnp.minimum(u1 + c0, u0), jnp.minimum(u0 + c1, u1))
        own[rows, :] = jnp.where(down, u1, u0)
        return carry

    lax.fori_loop(0, chunks, edge, 0)


def local_sweeps(flags, stims, stim_times, fibre, tissue, previous, grid_step):
    planes, cells_y, cells_z = previous.shape
    field = jax.ShapeDtypeStruct(previous.shape, jnp.float32)
    totals = jax.ShapeDtypeStruct((2, cells_y, cells_z), jnp.float32)
    own = jax.ShapeDtypeStruct((cells_y, cells_z), jnp.float32)
    vmem = pl.BlockSpec(memory_space=pltpu.VMEM)
    smem = pl.BlockSpec(memory_space=pltpu.SMEM)
    elements = planes * cells_y * cells_z
    return pl.pallas_call(
        functools.partial(local_kernel, grid_step=grid_step),
        out_shape=(field, field, totals, own),
        in_specs=[smem, smem, smem, vmem, vmem, vmem],
        out_specs=(vmem, vmem, vmem, vmem),
        scratch_shapes=[pltpu.VMEM(previous.shape, jnp.float32)],
        compiler_params=pltpu.CompilerParams(vmem_limit_bytes=48 * 1024 * 1024),
        cost_estimate=pl.CostEstimate(
            flops=300 * elements, transcendentals=6 * elements, bytes_accessed=40 * elements
        ),
    )(flags, stims, stim_times, fibre, tissue, previous)


RELAY_ROWS = 16
LINE = 8


def flip_bits(value, mask, bits):
    out = 0
    for j in range(bits):
        out = out + (2 ** j) * ((value // 2 ** j + (mask >> j) % 2) % 2)
    return out


def relay_kernel(totals, own, incoming, least_in, least_plane, before, line_total, box1_in,
                 box1_out, box2_in, box2_out, box3_in, box4, box5, send1, recv1, send2, recv2, send3,
                 recv3, send4, recv4, send5, recv5, *, line):
    total_add = totals.at[0]
    total_min = totals.at[1]
    cells_y, cells_z = incoming.shape
    chunks = cells_y // RELAY_ROWS
    slabs = lax.axis_size("slab")
    lines = slabs // line
    half = line // 2
    slab = lax.axis_index("slab")
    group = lax.axis_index("order")
    odd = group % 2
    rank = slab + odd * (slabs - 1 - 2 * slab)
    col = rank // line
    pos = rank % line
    last = line - 1
    mesh_id = pl.DeviceIdType.MESH

    def device(r):
        return (group, r + odd * (slabs - 1 - 2 * r))

    def at(c, p):
        return device(c * line + p)

    orders = lax.axis_size("order")
    masks = list(range(2, orders, 2))
    order_bits = max(orders - 1, 1).bit_length()
    first_col = col == 0
    is_end = pos == last
    in_up = pos < half
    in_down = (pos >= half) & (pos < last)
    up_next = (pos >= 1) & (pos + 1 < half)
    down_next = (pos <= last - 2) & (pos > half)
    ends_to = [p for p in (0, 1) if p < half] + [p for p in (last - 1, last - 2) if half <= p < last]

    barrier = pltpu.get_barrier_semaphore()
    neighbours = []
    neighbours.append((pos > 0, at(col, pos - 1)))
    neighbours.append((pos < last, at(col, pos + 1)))
    for p in ends_to:
        if p not in (last - 1,):
            neighbours.append(((pos == p) & (col > 0), at(col, last)))
            neighbours.append((is_end & (col > 0), at(col, p)))
    neighbours.append((is_end & (col > 0), at(col - 1, last)))
    neighbours.append((is_end & (col < lines - 1), at(col + 1, last)))
    for m in masks:
        neighbours.append((slab >= 0, (flip_bits(group, m, order_bits), slab)))
    count = jnp.int32(0)
    for cond, dev in neighbours:
        @pl.when(cond)
        def _():
            pl.semaphore_signal(barrier, 1, device_id=dev, device_id_type=mesh_id)

        count = count + cond.astype(jnp.int32)
    pl.semaphore_wait(barrier, count)

    def copy1(c):
        return pltpu.make_async_remote_copy(box1_out.at[c], box1_in.at[c], send1.at[c], recv1.at[c],
                                            device_id=at(col, pos + 1), device_id_type=mesh_id)

    def copy2(c):
        return pltpu.make_async_remote_copy(box2_out.at[c], box2_in.at[c], send2.at[c], recv2.at[c],
                                            device_id=at(col + 1, last), device_id_type=mesh_id)

    def copy3_from_end(c, k, target):
        return pltpu.make_async_remote_copy(box2_in.at[c], box3_in.at[c], send3.at[c, k], recv3.at[c],
                                            device_id=target, device_id_type=mesh_id)

    def copy3_relay(c, target):
        return pltpu.make_async_remote_copy(box3_in.at[c], box3_in.at[c], send3.at[c, 0], recv3.at[c],
                                            device_id=target, device_id_type=mesh_id)

    def rows_of(c):
        return pl.ds(pl.multiple_of(c * RELAY_ROWS, RELAY_ROWS), RELAY_ROWS)

    def copy5(k):
        return pltpu.make_async_remote_copy(own, box5.at[k], send5.at[k], recv5.at[k],
                                            device_id=(flip_bits(group, masks[k], order_bits), slab),
                                            device_id_type=mesh_id)

    for k in range(len(masks)):
        copy5(k).start()

    def copy4(c, k):
        return pltpu.make_async_remote_copy(incoming.at[rows_of(c)], box4.at[k, c], send4.at[c, k],
                                            recv4.at[c, k], device_id=(flip_bits(group, masks[k], order_bits), slab),
                                            device_id_type=mesh_id)

    def share(c):
        for k in range(len(masks)):
            copy4(c, k).start()

    def stage1(c, carry):
        rows = rows_of(c)
        own_add = total_add[rows, :]
        own_min = total_min[rows, :]

        @pl.when(pos == 0)
        def _():
            box1_out[c, 0] = own_add
            box1_out[c, 1] = own_min

        @pl.when(pos > 0)
        def _():
            copy1(c).wait_recv()
            got_add = box1_in[c, 0]
            got_min = box1_in[c, 1]
            before[0, rows, :] = got_add
            before[1, rows, :] = got_min
            new_add = got_add + own_add
            new_min = jnp.minimum(got_min + own_add, own_min)

            @pl.when(pos < last)
            def _():
                box1_out[c, 0] = new_add
                box1_out[c, 1] = new_min

            @pl.when(is_end)
            def _():
                line_total[0, rows, :] = new_add
                line_total[1, rows, :] = new_min

        @pl.when((pos == 0) & is_end)
        def _():
            line_total[0, rows, :] = own_add
            line_total[1, rows, :] = own_min

        @pl.when(pos < last)
        def _():
            copy1(c).start()

        return carry

    def stage2(c, carry):
        rows = rows_of(c)

        @pl.when(is_end & first_col)
        def _():
            incoming[rows, :] = jnp.where(pos > 0, before[1, rows, :], jnp.inf)
            share(c)
            box2_out[c] = line_total[1, rows, :]

        @pl.when(is_end & jnp.logical_not(first_col))
        def _():
            copy2(c).wait_recv()
            value = box2_in[c]
            incoming[rows, :] = jnp.where(
                pos > 0, jnp.minimum(value + before[0, rows, :], before[1, rows, :]), value)
            share(c)
            box2_out[c] = jnp.minimum(value + line_total[0, rows, :], line_total[1, rows, :])

            for k, p in enumerate(ends_to):
                copy3_from_end(c, k, at(col, p)).start()

        @pl.when(is_end & (col < lines - 1))
        def _():
            copy2(c).start()

        return carry

    def stages12(c, carry):
        stage1(c, carry)
        return stage2(c, carry)

    lax.fori_loop(0, chunks, stages12, 0)

    def stage3(c, carry):
        rows = rows_of(c)

        @pl.when(first_col & jnp.logical_not(is_end))
        def _():
            incoming[rows, :] = jnp.where(pos > 0, before[1, rows, :], jnp.inf)
            share(c)

        @pl.when(jnp.logical_not(first_col) & (in_up | in_down))
        def _():
            copy3_relay(c, at(col, 0)).wait_recv()
            value = box3_in[c]
            incoming[rows, :] = jnp.where(
                pos > 0, jnp.minimum(value + before[0, rows, :], before[1, rows, :]), value)
            share(c)

            @pl.when(in_up & up_next)
            def _():
                copy3_relay(c, at(col, pos + 1)).start()

            @pl.when(in_down & down_next)
            def _():
                copy3_relay(c, at(col, pos - 1)).start()

        return carry

    lax.fori_loop(0, chunks, stage3, 0)

    def gather(c, carry):
        rows = rows_of(c)
        least = incoming[rows, :]
        for k in range(len(masks)):
            copy4(c, k).wait_recv()
            least = jnp.minimum(least, box4[k, c])
        least_in[rows, :] = least
        return carry

    lax.fori_loop(0, chunks, gather, 0)

    for k in range(len(masks)):
        copy5(k).wait_recv()

    def gather_plane(c, carry):
        rows = rows_of(c)
        least = own[rows, :]
        for k in range(len(masks)):
            least = jnp.minimum(least, box5[k, rows, :])
        least_plane[rows, :] = least
        return carry

    lax.fori_loop(0, chunks, gather_plane, 0)

    def drain(c, carry):
        @pl.when(pos < last)
        def _():
            copy1(c).wait_send()

        @pl.when(is_end & (col < lines - 1))
        def _():
            copy2(c).wait_send()

        @pl.when(is_end & jnp.logical_not(first_col))
        def _():
            for k, p in enumerate(ends_to):
                copy3_from_end(c, k, at(col, p)).wait_send()

        @pl.when(jnp.logical_not(first_col) & ((in_up & up_next) | (in_down & down_next)))
        def _():
            copy3_relay(c, at(col, 0)).wait_send()

        for k in range(len(masks)):
            copy4(c, k).wait_send()
        return carry

    lax.fori_loop(0, chunks, drain, 0)
    for k in range(len(masks)):
        copy5(k).wait_send()


def relay(totals, own, slabs, orders):
    cells_y, cells_z = own.shape
    chunks = cells_y // RELAY_ROWS
    sharers = len(range(2, orders, 2))
    plane = jax.ShapeDtypeStruct(own.shape, jnp.float32)
    line = LINE if slabs % LINE == 0 else slabs
    vmem = pl.BlockSpec(memory_space=pltpu.VMEM)
    box = pltpu.VMEM((chunks, RELAY_ROWS, cells_z), jnp.float32)
    pair_box = pltpu.VMEM((chunks, 2, RELAY_ROWS, cells_z), jnp.float32)
    return pl.pallas_call(
        functools.partial(relay_kernel, line=line),
        out_shape=(plane, plane, plane),
        in_specs=[vmem, vmem],
        out_specs=(vmem, vmem, vmem),
        scratch_shapes=[
            pltpu.VMEM((2, cells_y, cells_z), jnp.float32),
            pltpu.VMEM((2, cells_y, cells_z), jnp.float32),
            pair_box,
            pair_box,
            box,
            box,
            box,
            pltpu.VMEM((max(sharers, 1), chunks, RELAY_ROWS, cells_z), jnp.float32),
            pltpu.VMEM((max(sharers, 1), cells_y, cells_z), jnp.float32),
            pltpu.SemaphoreType.DMA((chunks,)),
            pltpu.SemaphoreType.DMA((chunks,)),
            pltpu.SemaphoreType.DMA((chunks,)),
            pltpu.SemaphoreType.DMA((chunks,)),
            pltpu.SemaphoreType.DMA((chunks, 4)),
            pltpu.SemaphoreType.DMA((chunks,)),
            pltpu.SemaphoreType.DMA((chunks, max(sharers, 1))),
            pltpu.SemaphoreType.DMA((chunks, max(sharers, 1))),
            pltpu.SemaphoreType.DMA((max(sharers, 1),)),
            pltpu.SemaphoreType.DMA((max(sharers, 1),)),
        ],
        compiler_params=pltpu.CompilerParams(collective_id=0, has_side_effects=True),
    )(totals, own)


def shards(previous, fibre_tensor, tissue, stim_sites, stim_times):
    planes, cells_y, cells_z = previous.shape
    slabs = lax.axis_size("slab")
    orders = lax.axis_size("order")
    slab_index = lax.axis_index("slab")
    group_index = lax.axis_index("order")
    grid_step = 2.0 / (planes * slabs)

    plane_index = stim_sites // (cells_y * cells_z) - slab_index * planes
    row_index = stim_sites // cells_z % cells_y
    column_index = stim_sites % cells_z
    stims = jnp.stack([plane_index, row_index, column_index]).astype(jnp.int32)

    bits = jnp.stack([group_index % 2, group_index // 2 % 2, group_index // 4 % 2]).astype(jnp.int32)
    cost_x, field, totals, own_plane = local_sweeps(
        bits, stims, stim_times, fibre_tensor, tissue, previous, grid_step)

    core = group_index % 2
    incoming, least_in, least_plane = relay(totals, own_plane, slabs, orders)
    other = lax.ppermute(jnp.stack([least_plane, least_in]), "order", [(g, g ^ 1) for g in range(orders)])

    least0 = jnp.where(core == 0, least_plane, other[0])
    least1 = jnp.where(core == 0, other[0], least_plane)
    up_in = jnp.where(core == 0, least_in, other[1])
    down_in = jnp.where(core == 0, other[1], least_in)

    up_add = jnp.stack([cost_x[0], cost_x[0] + cost_x[1]])
    up_min = jnp.stack([field[0], jnp.minimum(field[0] + cost_x[1], field[1])])
    down_add = jnp.stack([cost_x[1] + cost_x[0], cost_x[1]])
    down_min = jnp.stack([jnp.minimum(field[1] + cost_x[0], field[0]), field[1]])
    backward_x = core == 1
    line_add = jnp.where(backward_x, down_add, up_add)
    line_min = jnp.where(backward_x, down_min, up_min)
    sweep_field = jnp.minimum(incoming[None] + line_add, line_min)

    least_local = jnp.stack([
        jnp.minimum(least0, least1 + cost_x[0]),
        jnp.minimum(least1, least0 + cost_x[1]),
    ])
    merged = jnp.minimum(
        least_local,
        jnp.minimum(up_in[None] + up_add, down_in[None] + down_add),
    )
    return (merged, sweep_field[None])


def solution(mesh):
    placed = (P("slab", None, None), P(None, "slab", None, None), P("slab", None, None), P(), P())
    return jax.shard_map(
        shards,
        mesh=mesh,
        in_specs=placed,
        out_specs=(P("slab", None, None), P("order", "slab", None, None)),
        check_vma=False,
    )
```

```python
import functools

import jax
import jax.numpy as jnp
from jax import lax
from jax.experimental import pallas as pl
from jax.experimental.pallas import tpu as pltpu
from jax.sharding import PartitionSpec as P

ROWS = 8
CHUNK = 64


def scan_step(a, m, k, axis, reverse, last):
    n = a.shape[axis]
    index = lax.broadcasted_iota(jnp.int32, a.shape, axis)
    shift = n - k if reverse else k
    valid = index < n - k if reverse else index >= k
    a_src = pltpu.roll(a, shift, axis)
    m_src = pltpu.roll(m, shift, axis)
    m = jnp.where(valid, jnp.minimum(m_src + a, m), m)
    if not last:
        a = jnp.where(valid, a_src + a, a)
    return a, m


def block_scan(a, m, axis, reverse, need_sum):
    n = a.shape[axis]
    k = 1
    while k < n:
        a, m = scan_step(a, m, k, axis, reverse, last=(2 * k >= n) and not need_sum)
        k *= 2
    return a, m


def lane_scan(step, seeded, reverse):
    width = step.shape[1]
    if width % 128 or width == 128:
        return block_scan(step, seeded, 1, reverse, False)[1]
    parts = []
    for i in range(width // 128):
        lanes = slice(i * 128, (i + 1) * 128)
        parts.append(block_scan(step[:, lanes], seeded[:, lanes], 1, reverse, True))
    order = range(len(parts) - 1, -1, -1) if reverse else range(len(parts))
    carry = None
    out = [None] * len(parts)
    for i in order:
        a, m = parts[i]
        if carry is not None:
            m = jnp.minimum(carry + a, m)
        edge = m[:, 0:1] if reverse else m[:, 127:128]
        carry = jnp.broadcast_to(edge, m.shape)
        out[i] = m
    return jnp.concatenate(out, axis=1)


def local_kernel(flags, stims, stim_times, fibre, tissue, previous, cost_x, field, totals, own,
                 cost_y, *, grid_step):
    planes, cells_y, cells_z = previous.shape
    chunks = cells_y // CHUNK
    inf = jnp.float32(jnp.inf)

    field[...] = previous[...]

    def seed(k, carry):
        p = stims[0, k]
        r = stims[1, k]
        c = stims[2, k]

        @pl.when((p >= 0) & (p < planes))
        def _():
            base = pl.multiple_of(r // ROWS * ROWS, ROWS)
            block = field[p, pl.ds(base, ROWS), :]
            row = lax.broadcasted_iota(jnp.int32, block.shape, 0)
            lane = lax.broadcasted_iota(jnp.int32, block.shape, 1)
            hit = (row == r - base) & (lane == c)
            field[p, pl.ds(base, ROWS), :] = jnp.where(hit, jnp.minimum(block, stim_times[k]), block)

        return carry

    lax.fori_loop(0, stims.shape[1], seed, 0)

    def costs_and_z(reverse):
        def body(i, carry):
            p = i // chunks
            rows = pl.ds(pl.multiple_of((i % chunks) * CHUNK, CHUNK), CHUNK)
            xx = fibre[0, p, rows, :]
            yy = fibre[1, p, rows, :]
            zz = fibre[2, p, rows, :]
            xy = fibre[3, p, rows, :]
            xz = fibre[4, p, rows, :]
            yz = fibre[5, p, rows, :]
            cx = yy * zz - yz * yz
            cy = xx * zz - xz * xz
            cz = xx * yy - xy * xy
            det = xx * cx - xy * (xy * zz - yz * xz) + xz * (xy * yz - yy * xz)
            factor = jnp.where(tissue[p, rows, :] == 1, 1.0, 4.0).astype(jnp.float32) * grid_step
            inverse = 1.0 / det
            cost_x[p, rows, :] = jnp.sqrt(cx * inverse) * factor
            cost_y[p, rows, :] = jnp.sqrt(cy * inverse) * factor
            step_z = jnp.sqrt(cz * inverse) * factor
            u = lane_scan(step_z, field[p, rows, :], reverse)
            field[p, rows, :] = u
            return carry

        lax.fori_loop(0, planes * chunks, body, 0, unroll=2)

    def sweep_y(reverse):
        def body(j, carry):
            i = chunks - 1 - j if reverse else j
            rows = pl.ds(pl.multiple_of(i * CHUNK, CHUNK), CHUNK)
            out = []
            for p in range(planes):
                a, m = block_scan(cost_y[p, rows, :], field[p, rows, :], 0, reverse, True)
                u = jnp.minimum(carry[p] + a, m)
                field[p, rows, :] = u
                edge = u[0:1, :] if reverse else u[CHUNK - 1:CHUNK, :]
                out.append(jnp.broadcast_to(edge, u.shape))
            return tuple(out)

        start = tuple(jnp.full((CHUNK, cells_z), inf, jnp.float32) for _ in range(planes))
        lax.fori_loop(0, chunks, body, start, unroll=2)

    for flag, fn in ((flags[2], costs_and_z), (flags[1], sweep_y)):
        pl.when(flag == 1)(functools.partial(fn, True))
        pl.when(flag != 1)(functools.partial(fn, False))

    def edge(i, carry):
        rows = pl.ds(pl.multiple_of(i * CHUNK, CHUNK), CHUNK)
        c0 = cost_x[0, rows, :]
        c1 = cost_x[1, rows, :]
        u0 = field[0, rows, :]
        u1 = field[1, rows, :]
        down = flags[0] == 1
        totals[0, rows, :] = jnp.where(down, c1 + c0, c0 + c1)
        totals[1, rows, :] = jnp.where(down, jnp.minimum(u1 + c0, u0), jnp.minimum(u0 + c1, u1))
        own[rows, :] = jnp.where(down, u1, u0)
        return carry

    lax.fori_loop(0, chunks, edge, 0)


def local_sweeps(flags, stims, stim_times, fibre, tissue, previous, grid_step):
    planes, cells_y, cells_z = previous.shape
    field = jax.ShapeDtypeStruct(previous.shape, jnp.float32)
    totals = jax.ShapeDtypeStruct((2, cells_y, cells_z), jnp.float32)
    own = jax.ShapeDtypeStruct((cells_y, cells_z), jnp.float32)
    vmem = pl.BlockSpec(memory_space=pltpu.VMEM)
    smem = pl.BlockSpec(memory_space=pltpu.SMEM)
    elements = planes * cells_y * cells_z
    return pl.pallas_call(
        functools.partial(local_kernel, grid_step=grid_step),
        out_shape=(field, field, totals, own),
        in_specs=[smem, smem, smem, vmem, vmem, vmem],
        out_specs=(vmem, vmem, vmem, vmem),
        scratch_shapes=[pltpu.VMEM(previous.shape, jnp.float32)],
        compiler_params=pltpu.CompilerParams(vmem_limit_bytes=48 * 1024 * 1024),
        cost_estimate=pl.CostEstimate(
            flops=300 * elements, transcendentals=6 * elements, bytes_accessed=40 * elements
        ),
    )(flags, stims, stim_times, fibre, tissue, previous)


RELAY_ROWS = 16
LINE = 8


def flip_bits(value, mask, bits):
    out = 0
    for j in range(bits):
        out = out + (2 ** j) * ((value // 2 ** j + (mask >> j) % 2) % 2)
    return out


def relay_kernel(totals, own, incoming, least_in, least_plane, before, line_total, box1_in,
                 box1_out, box2_in, box2_out, box3_in, box4, box5, send1, recv1, send2, recv2, send3,
                 recv3, send4, recv4, send5, recv5, *, line):
    total_add = totals.at[0]
    total_min = totals.at[1]
    cells_y, cells_z = incoming.shape
    chunks = cells_y // RELAY_ROWS
    slabs = lax.axis_size("slab")
    lines = slabs // line
    half = line // 2
    slab = lax.axis_index("slab")
    group = lax.axis_index("order")
    odd = group % 2
    rank = slab + odd * (slabs - 1 - 2 * slab)
    col = rank // line
    pos = rank % line
    last = line - 1
    mesh_id = pl.DeviceIdType.MESH

    def device(r):
        return (group, r + odd * (slabs - 1 - 2 * r))

    def at(c, p):
        return device(c * line + p)

    orders = lax.axis_size("order")
    masks = list(range(2, orders, 2))
    order_bits = max(orders - 1, 1).bit_length()
    first_col = col == 0
    is_end = pos == last
    in_up = pos < half
    in_down = (pos >= half) & (pos < last)
    up_next = (pos >= 1) & (pos + 1 < half)
    down_next = (pos <= last - 2) & (pos > half)
    ends_to = [p for p in (0, 1) if p < half] + [p for p in (last - 1, last - 2) if half <= p < last]

    barrier = pltpu.get_barrier_semaphore()
    neighbours = []
    neighbours.append((pos > 0, at(col, pos - 1)))
    neighbours.append((pos < last, at(col, pos + 1)))
    for p in ends_to:
        if p not in (last - 1,):
            neighbours.append(((pos == p) & (col > 0), at(col, last)))
            neighbours.append((is_end & (col > 0), at(col, p)))
    neighbours.append((is_end & (col > 0), at(col - 1, last)))
    neighbours.append((is_end & (col < lines - 1), at(col + 1, last)))
    for m in masks:
        neighbours.append((slab >= 0, (flip_bits(group, m, order_bits), slab)))
    count = jnp.int32(0)
    for cond, dev in neighbours:
        @pl.when(cond)
        def _():
            pl.semaphore_signal(barrier, 1, device_id=dev, device_id_type=mesh_id)

        count = count + cond.astype(jnp.int32)
    pl.semaphore_wait(barrier, count)

    def copy1(c):
        return pltpu.make_async_remote_copy(box1_out.at[c], box1_in.at[c], send1.at[c], recv1.at[c],
                                            device_id=at(col, pos + 1), device_id_type=mesh_id)

    def copy2(c):
        return pltpu.make_async_remote_copy(box2_out.at[c], box2_in.at[c], send2.at[c], recv2.at[c],
                                            device_id=at(col + 1, last), device_id_type=mesh_id)

    def copy3_from_end(c, k, target):
        return pltpu.make_async_remote_copy(box2_in.at[c], box3_in.at[c], send3.at[c, k], recv3.at[c],
                                            device_id=target, device_id_type=mesh_id)

    def copy3_relay(c, target):
        return pltpu.make_async_remote_copy(box3_in.at[c], box3_in.at[c], send3.at[c, 0], recv3.at[c],
                                            device_id=target, device_id_type=mesh_id)

    def rows_of(c):
        return pl.ds(pl.multiple_of(c * RELAY_ROWS, RELAY_ROWS), RELAY_ROWS)

    def copy5(k):
        return pltpu.make_async_remote_copy(own, box5.at[k], send5.at[k], recv5.at[k],
                                            device_id=(flip_bits(group, masks[k], order_bits), slab),
                                            device_id_type=mesh_id)

    for k in range(len(masks)):
        copy5(k).start()

    def copy4(c, k):
        return pltpu.make_async_remote_copy(incoming.at[rows_of(c)], box4.at[k, c], send4.at[c, k],
                                            recv4.at[c, k], device_id=(flip_bits(group, masks[k], order_bits), slab),
                                            device_id_type=mesh_id)

    def share(c):
        for k in range(len(masks)):
            copy4(c, k).start()

    def stage1(c, carry):
        rows = rows_of(c)
        own_add = total_add[rows, :]
        own_min = total_min[rows, :]

        @pl.when(pos == 0)
        def _():
            box1_out[c, 0] = own_add
            box1_out[c, 1] = own_min

        @pl.when(pos > 0)
        def _():
            copy1(c).wait_recv()
            got_add = box1_in[c, 0]
            got_min = box1_in[c, 1]
            before[0, rows, :] = got_add
            before[1, rows, :] = got_min
            new_add = got_add + own_add
            new_min = jnp.minimum(got_min + own_add, own_min)

            @pl.when(pos < last)
            def _():
                box1_out[c, 0] = new_add
                box1_out[c, 1] = new_min

            @pl.when(is_end)
            def _():
                line_total[0, rows, :] = new_add
                line_total[1, rows, :] = new_min

        @pl.when((pos == 0) & is_end)
        def _():
            line_total[0, rows, :] = own_add
            line_total[1, rows, :] = own_min

        @pl.when(pos < last)
        def _():
            copy1(c).start()

        return carry

    def stage2(c, carry):
        rows = rows_of(c)

        @pl.when(is_end & first_col)
        def _():
            incoming[rows, :] = jnp.where(pos > 0, before[1, rows, :], jnp.inf)
            share(c)
            box2_out[c] = line_total[1, rows, :]

        @pl.when(is_end & jnp.logical_not(first_col))
        def _():
            copy2(c).wait_recv()
            value = box2_in[c]
            incoming[rows, :] = jnp.where(
                pos > 0, jnp.minimum(value + before[0, rows, :], before[1, rows, :]), value)
            share(c)
            box2_out[c] = jnp.minimum(value + line_total[0, rows, :], line_total[1, rows, :])

            for k, p in enumerate(ends_to):
                copy3_from_end(c, k, at(col, p)).start()

        @pl.when(is_end & (col < lines - 1))
        def _():
            copy2(c).start()

        return carry

    def stages12(c, carry):
        stage1(c, carry)
        return stage2(c, carry)

    lax.fori_loop(0, chunks, stages12, 0)

    def stage3(c, carry):
        rows = rows_of(c)

        @pl.when(first_col & jnp.logical_not(is_end))
        def _():
            incoming[rows, :] = jnp.where(pos > 0, before[1, rows, :], jnp.inf)
            share(c)

        @pl.when(jnp.logical_not(first_col) & (in_up | in_down))
        def _():
            copy3_relay(c, at(col, 0)).wait_recv()
            value = box3_in[c]
            incoming[rows, :] = jnp.where(
                pos > 0, jnp.minimum(value + before[0, rows, :], before[1, rows, :]), value)
            share(c)

            @pl.when(in_up & up_next)
            def _():
                copy3_relay(c, at(col, pos + 1)).start()

            @pl.when(in_down & down_next)
            def _():
                copy3_relay(c, at(col, pos - 1)).start()

        return carry

    lax.fori_loop(0, chunks, stage3, 0)

    def gather(c, carry):
        rows = rows_of(c)
        least = incoming[rows, :]
        for k in range(len(masks)):
            copy4(c, k).wait_recv()
            least = jnp.minimum(least, box4[k, c])
        least_in[rows, :] = least
        return carry

    lax.fori_loop(0, chunks, gather, 0)

    for k in range(len(masks)):
        copy5(k).wait_recv()

    def gather_plane(c, carry):
        rows = rows_of(c)
        least = own[rows, :]
        for k in range(len(masks)):
            least = jnp.minimum(least, box5[k, rows, :])
        least_plane[rows, :] = least
        return carry

    lax.fori_loop(0, chunks, gather_plane, 0)

    def drain(c, carry):
        @pl.when(pos < last)
        def _():
            copy1(c).wait_send()

        @pl.when(is_end & (col < lines - 1))
        def _():
            copy2(c).wait_send()

        @pl.when(is_end & jnp.logical_not(first_col))
        def _():
            for k, p in enumerate(ends_to):
                copy3_from_end(c, k, at(col, p)).wait_send()

        @pl.when(jnp.logical_not(first_col) & ((in_up & up_next) | (in_down & down_next)))
        def _():
            copy3_relay(c, at(col, 0)).wait_send()

        for k in range(len(masks)):
            copy4(c, k).wait_send()
        return carry

    lax.fori_loop(0, chunks, drain, 0)
    for k in range(len(masks)):
        copy5(k).wait_send()


def relay(totals, own, slabs, orders):
    cells_y, cells_z = own.shape
    chunks = cells_y // RELAY_ROWS
    sharers = len(range(2, orders, 2))
    plane = jax.ShapeDtypeStruct(own.shape, jnp.float32)
    line = LINE if slabs % LINE == 0 else slabs
    vmem = pl.BlockSpec(memory_space=pltpu.VMEM)
    box = pltpu.VMEM((chunks, RELAY_ROWS, cells_z), jnp.float32)
    pair_box = pltpu.VMEM((chunks, 2, RELAY_ROWS, cells_z), jnp.float32)
    return pl.pallas_call(
        functools.partial(relay_kernel, line=line),
        out_shape=(plane, plane, plane),
        in_specs=[vmem, vmem],
        out_specs=(vmem, vmem, vmem),
        scratch_shapes=[
            pltpu.VMEM((2, cells_y, cells_z), jnp.float32),
            pltpu.VMEM((2, cells_y, cells_z), jnp.float32),
            pair_box,
            pair_box,
            box,
            box,
            box,
            pltpu.VMEM((max(sharers, 1), chunks, RELAY_ROWS, cells_z), jnp.float32),
            pltpu.VMEM((max(sharers, 1), cells_y, cells_z), jnp.float32),
            pltpu.SemaphoreType.DMA((chunks,)),
            pltpu.SemaphoreType.DMA((chunks,)),
            pltpu.SemaphoreType.DMA((chunks,)),
            pltpu.SemaphoreType.DMA((chunks,)),
            pltpu.SemaphoreType.DMA((chunks, 4)),
            pltpu.SemaphoreType.DMA((chunks,)),
            pltpu.SemaphoreType.DMA((chunks, max(sharers, 1))),
            pltpu.SemaphoreType.DMA((chunks, max(sharers, 1))),
            pltpu.SemaphoreType.DMA((max(sharers, 1),)),
            pltpu.SemaphoreType.DMA((max(sharers, 1),)),
        ],
        compiler_params=pltpu.CompilerParams(collective_id=0, has_side_effects=True),
    )(totals, own)


def shards(previous, fibre_tensor, tissue, stim_sites, stim_times):
    planes, cells_y, cells_z = previous.shape
    slabs = lax.axis_size("slab")
    orders = lax.axis_size("order")
    slab_index = lax.axis_index("slab")
    group_index = lax.axis_index("order")
    grid_step = 2.0 / (planes * slabs)

    plane_index = stim_sites // (cells_y * cells_z) - slab_index * planes
    row_index = stim_sites // cells_z % cells_y
    column_index = stim_sites % cells_z
    stims = jnp.stack([plane_index, row_index, column_index]).astype(jnp.int32)

    bits = jnp.stack([group_index % 2, group_index // 2 % 2, group_index // 4 % 2]).astype(jnp.int32)
    cost_x, field, totals, own_plane = local_sweeps(
        bits, stims, stim_times, fibre_tensor, tissue, previous, grid_step)

    core = group_index % 2
    incoming, least_in, least_plane = relay(totals, own_plane, slabs, orders)
    other = lax.ppermute(jnp.stack([least_plane, least_in]), "order", [(g, g ^ 1) for g in range(orders)])

    least0 = jnp.where(core == 0, least_plane, other[0])
    least1 = jnp.where(core == 0, other[0], least_plane)
    up_in = jnp.where(core == 0, least_in, other[1])
    down_in = jnp.where(core == 0, other[1], least_in)

    up_add = jnp.stack([cost_x[0], cost_x[0] + cost_x[1]])
    up_min = jnp.stack([field[0], jnp.minimum(field[0] + cost_x[1], field[1])])
    down_add = jnp.stack([cost_x[1] + cost_x[0], cost_x[1]])
    down_min = jnp.stack([jnp.minimum(field[1] + cost_x[0], field[0]), field[1]])
    backward_x = core == 1
    line_add = jnp.where(backward_x, down_add, up_add)
    line_min = jnp.where(backward_x, down_min, up_min)
    sweep_field = jnp.minimum(incoming[None] + line_add, line_min)

    least_local = jnp.stack([
        jnp.minimum(least0, least1 + cost_x[0]),
        jnp.minimum(least1, least0 + cost_x[1]),
    ])
    merged = jnp.minimum(
        least_local,
        jnp.minimum(up_in[None] + up_add, down_in[None] + down_add),
    )
    return (merged, sweep_field[None])


def solution(mesh):
    placed = (P("slab", None, None), P(None, "slab", None, None), P("slab", None, None), P(), P())
    return jax.shard_map(
        shards,
        mesh=mesh,
        in_specs=placed,
        out_specs=(P("slab", None, None), P("order", "slab", None, None)),
        check_vma=False,
    )
```

```python
import functools

import jax
import jax.numpy as jnp
from jax import lax
from jax.experimental import pallas as pl
from jax.experimental.pallas import tpu as pltpu
from jax.sharding import PartitionSpec as P

ROWS = 8
CHUNK = 128


def scan_step(a, m, k, axis, reverse, last):
    n = a.shape[axis]
    index = lax.broadcasted_iota(jnp.int32, a.shape, axis)
    shift = n - k if reverse else k
    valid = index < n - k if reverse else index >= k
    a_src = pltpu.roll(a, shift, axis)
    m_src = pltpu.roll(m, shift, axis)
    m = jnp.where(valid, jnp.minimum(m_src + a, m), m)
    if not last:
        a = jnp.where(valid, a_src + a, a)
    return a, m


def block_scan(a, m, axis, reverse, need_sum):
    n = a.shape[axis]
    k = 1
    while k < n:
        a, m = scan_step(a, m, k, axis, reverse, last=(2 * k >= n) and not need_sum)
        k *= 2
    return a, m


def lane_scan(step, seeded, reverse):
    width = step.shape[1]
    if width % 128 or width == 128:
        return block_scan(step, seeded, 1, reverse, False)[1]
    parts = []
    for i in range(width // 128):
        lanes = slice(i * 128, (i + 1) * 128)
        parts.append(block_scan(step[:, lanes], seeded[:, lanes], 1, reverse, True))
    order = range(len(parts) - 1, -1, -1) if reverse else range(len(parts))
    carry = None
    out = [None] * len(parts)
    for i in order:
        a, m = parts[i]
        if carry is not None:
            m = jnp.minimum(carry + a, m)
        edge = m[:, 0:1] if reverse else m[:, 127:128]
        carry = jnp.broadcast_to(edge, m.shape)
        out[i] = m
    return jnp.concatenate(out, axis=1)


def local_kernel(flags, stims, stim_times, fibre, tissue, previous, cost_x, field, totals, own,
                 cost_y, *, grid_step):
    planes, cells_y, cells_z = previous.shape
    chunks = cells_y // CHUNK
    inf = jnp.float32(jnp.inf)

    field[...] = previous[...]

    def seed(k, carry):
        p = stims[0, k]
        r = stims[1, k]
        c = stims[2, k]

        @pl.when((p >= 0) & (p < planes))
        def _():
            base = pl.multiple_of(r // ROWS * ROWS, ROWS)
            block = field[p, pl.ds(base, ROWS), :]
            row = lax.broadcasted_iota(jnp.int32, block.shape, 0)
            lane = lax.broadcasted_iota(jnp.int32, block.shape, 1)
            hit = (row == r - base) & (lane == c)
            field[p, pl.ds(base, ROWS), :] = jnp.where(hit, jnp.minimum(block, stim_times[k]), block)

        return carry

    lax.fori_loop(0, stims.shape[1], seed, 0)

    def costs_and_z(reverse):
        def body(i, carry):
            p = i // chunks
            rows = pl.ds(pl.multiple_of((i % chunks) * CHUNK, CHUNK), CHUNK)
            xx = fibre[0, p, rows, :]
            yy = fibre[1, p, rows, :]
            zz = fibre[2, p, rows, :]
            xy = fibre[3, p, rows, :]
            xz = fibre[4, p, rows, :]
            yz = fibre[5, p, rows, :]
            cx = yy * zz - yz * yz
            cy = xx * zz - xz * xz
            cz = xx * yy - xy * xy
            det = xx * cx - xy * (xy * zz - yz * xz) + xz * (xy * yz - yy * xz)
            factor = jnp.where(tissue[p, rows, :] == 1, 1.0, 4.0).astype(jnp.float32) * grid_step
            inverse = 1.0 / det
            cost_x[p, rows, :] = jnp.sqrt(cx * inverse) * factor
            cost_y[p, rows, :] = jnp.sqrt(cy * inverse) * factor
            step_z = jnp.sqrt(cz * inverse) * factor
            u = lane_scan(step_z, field[p, rows, :], reverse)
            field[p, rows, :] = u
            return carry

        lax.fori_loop(0, planes * chunks, body, 0, unroll=2)

    def sweep_y(reverse):
        def body(j, carry):
            i = chunks - 1 - j if reverse else j
            rows = pl.ds(pl.multiple_of(i * CHUNK, CHUNK), CHUNK)
            out = []
            for p in range(planes):
                a, m = block_scan(cost_y[p, rows, :], field[p, rows, :], 0, reverse, True)
                u = jnp.minimum(carry[p] + a, m)
                field[p, rows, :] = u
                edge = u[0:1, :] if reverse else u[CHUNK - 1:CHUNK, :]
                out.append(jnp.broadcast_to(edge, u.shape))
            return tuple(out)

        start = tuple(jnp.full((CHUNK, cells_z), inf, jnp.float32) for _ in range(planes))
        lax.fori_loop(0, chunks, body, start, unroll=2)

    for flag, fn in ((flags[2], costs_and_z), (flags[1], sweep_y)):
        pl.when(flag == 1)(functools.partial(fn, True))
        pl.when(flag != 1)(functools.partial(fn, False))

    def edge(i, carry):
        rows = pl.ds(pl.multiple_of(i * CHUNK, CHUNK), CHUNK)
        c0 = cost_x[0, rows, :]
        c1 = cost_x[1, rows, :]
        u0 = field[0, rows, :]
        u1 = field[1, rows, :]
        down = flags[0] == 1
        totals[0, rows, :] = jnp.where(down, c1 + c0, c0 + c1)
        totals[1, rows, :] = jnp.where(down, jnp.minimum(u1 + c0, u0), jnp.minimum(u0 + c1, u1))
        own[rows, :] = jnp.where(down, u1, u0)
        return carry

    lax.fori_loop(0, chunks, edge, 0)


def local_sweeps(flags, stims, stim_times, fibre, tissue, previous, grid_step):
    planes, cells_y, cells_z = previous.shape
    field = jax.ShapeDtypeStruct(previous.shape, jnp.float32)
    totals = jax.ShapeDtypeStruct((2, cells_y, cells_z), jnp.float32)
    own = jax.ShapeDtypeStruct((cells_y, cells_z), jnp.float32)
    vmem = pl.BlockSpec(memory_space=pltpu.VMEM)
    smem = pl.BlockSpec(memory_space=pltpu.SMEM)
    elements = planes * cells_y * cells_z
    return pl.pallas_call(
        functools.partial(local_kernel, grid_step=grid_step),
        out_shape=(field, field, totals, own),
        in_specs=[smem, smem, smem, vmem, vmem, vmem],
        out_specs=(vmem, vmem, vmem, vmem),
        scratch_shapes=[pltpu.VMEM(previous.shape, jnp.float32)],
        compiler_params=pltpu.CompilerParams(vmem_limit_bytes=48 * 1024 * 1024),
        cost_estimate=pl.CostEstimate(
            flops=300 * elements, transcendentals=6 * elements, bytes_accessed=40 * elements
        ),
    )(flags, stims, stim_times, fibre, tissue, previous)


RELAY_ROWS = 16
LINE = 8


def flip_bits(value, mask, bits):
    out = 0
    for j in range(bits):
        out = out + (2 ** j) * ((value // 2 ** j + (mask >> j) % 2) % 2)
    return out


def relay_kernel(totals, own, incoming, least_in, least_plane, before, line_total, box1_in,
                 box1_out, box2_in, box2_out, box3_in, box4, box5, send1, recv1, send2, recv2, send3,
                 recv3, send4, recv4, send5, recv5, *, line):
    total_add = totals.at[0]
    total_min = totals.at[1]
    cells_y, cells_z = incoming.shape
    chunks = cells_y // RELAY_ROWS
    slabs = lax.axis_size("slab")
    lines = slabs // line
    half = line // 2
    slab = lax.axis_index("slab")
    group = lax.axis_index("order")
    odd = group % 2
    rank = slab + odd * (slabs - 1 - 2 * slab)
    col = rank // line
    pos = rank % line
    last = line - 1
    mesh_id = pl.DeviceIdType.MESH

    def device(r):
        return (group, r + odd * (slabs - 1 - 2 * r))

    def at(c, p):
        return device(c * line + p)

    orders = lax.axis_size("order")
    masks = list(range(2, orders, 2))
    order_bits = max(orders - 1, 1).bit_length()
    first_col = col == 0
    is_end = pos == last
    in_up = pos < half
    in_down = (pos >= half) & (pos < last)
    up_next = (pos >= 1) & (pos + 1 < half)
    down_next = (pos <= last - 2) & (pos > half)
    ends_to = [p for p in (0, 1) if p < half] + [p for p in (last - 1, last - 2) if half <= p < last]

    barrier = pltpu.get_barrier_semaphore()
    neighbours = []
    neighbours.append((pos > 0, at(col, pos - 1)))
    neighbours.append((pos < last, at(col, pos + 1)))
    for p in ends_to:
        if p not in (last - 1,):
            neighbours.append(((pos == p) & (col > 0), at(col, last)))
            neighbours.append((is_end & (col > 0), at(col, p)))
    neighbours.append((is_end & (col > 0), at(col - 1, last)))
    neighbours.append((is_end & (col < lines - 1), at(col + 1, last)))
    for m in masks:
        neighbours.append((slab >= 0, (flip_bits(group, m, order_bits), slab)))
    count = jnp.int32(0)
    for cond, dev in neighbours:
        @pl.when(cond)
        def _():
            pl.semaphore_signal(barrier, 1, device_id=dev, device_id_type=mesh_id)

        count = count + cond.astype(jnp.int32)
    pl.semaphore_wait(barrier, count)

    def copy1(c):
        return pltpu.make_async_remote_copy(box1_out.at[c], box1_in.at[c], send1.at[c], recv1.at[c],
                                            device_id=at(col, pos + 1), device_id_type=mesh_id)

    def copy2(c):
        return pltpu.make_async_remote_copy(box2_out.at[c], box2_in.at[c], send2.at[c], recv2.at[c],
                                            device_id=at(col + 1, last), device_id_type=mesh_id)

    def copy3_from_end(c, k, target):
        return pltpu.make_async_remote_copy(box2_in.at[c], box3_in.at[c], send3.at[c, k], recv3.at[c],
                                            device_id=target, device_id_type=mesh_id)

    def copy3_relay(c, target):
        return pltpu.make_async_remote_copy(box3_in.at[c], box3_in.at[c], send3.at[c, 0], recv3.at[c],
                                            device_id=target, device_id_type=mesh_id)

    def rows_of(c):
        return pl.ds(pl.multiple_of(c * RELAY_ROWS, RELAY_ROWS), RELAY_ROWS)

    def copy5(k):
        return pltpu.make_async_remote_copy(own, box5.at[k], send5.at[k], recv5.at[k],
                                            device_id=(flip_bits(group, masks[k], order_bits), slab),
                                            device_id_type=mesh_id)

    for k in range(len(masks)):
        copy5(k).start()

    def copy4(c, k):
        return pltpu.make_async_remote_copy(incoming.at[rows_of(c)], box4.at[k, c], send4.at[c, k],
                                            recv4.at[c, k], device_id=(flip_bits(group, masks[k], order_bits), slab),
                                            device_id_type=mesh_id)

    def share(c):
        for k in range(len(masks)):
            copy4(c, k).start()

    def stage1(c, carry):
        rows = rows_of(c)
        own_add = total_add[rows, :]
        own_min = total_min[rows, :]

        @pl.when(pos == 0)
        def _():
            box1_out[c, 0] = own_add
            box1_out[c, 1] = own_min

        @pl.when(pos > 0)
        def _():
            copy1(c).wait_recv()
            got_add = box1_in[c, 0]
            got_min = box1_in[c, 1]
            before[0, rows, :] = got_add
            before[1, rows, :] = got_min
            new_add = got_add + own_add
            new_min = jnp.minimum(got_min + own_add, own_min)

            @pl.when(pos < last)
            def _():
                box1_out[c, 0] = new_add
                box1_out[c, 1] = new_min

            @pl.when(is_end)
            def _():
                line_total[0, rows, :] = new_add
                line_total[1, rows, :] = new_min

        @pl.when((pos == 0) & is_end)
        def _():
            line_total[0, rows, :] = own_add
            line_total[1, rows, :] = own_min

        @pl.when(pos < last)
        def _():
            copy1(c).start()

        return carry

    def stage2(c, carry):
        rows = rows_of(c)

        @pl.when(is_end & first_col)
        def _():
            incoming[rows, :] = jnp.where(pos > 0, before[1, rows, :], jnp.inf)
            share(c)
            box2_out[c] = line_total[1, rows, :]

        @pl.when(is_end & jnp.logical_not(first_col))
        def _():
            copy2(c).wait_recv()
            value = box2_in[c]
            incoming[rows, :] = jnp.where(
                pos > 0, jnp.minimum(value + before[0, rows, :], before[1, rows, :]), value)
            share(c)
            box2_out[c] = jnp.minimum(value + line_total[0, rows, :], line_total[1, rows, :])

            for k, p in enumerate(ends_to):
                copy3_from_end(c, k, at(col, p)).start()

        @pl.when(is_end & (col < lines - 1))
        def _():
            copy2(c).start()

        return carry

    def stages12(c, carry):
        stage1(c, carry)
        return stage2(c, carry)

    lax.fori_loop(0, chunks, stages12, 0)

    def stage3(c, carry):
        rows = rows_of(c)

        @pl.when(first_col & jnp.logical_not(is_end))
        def _():
            incoming[rows, :] = jnp.where(pos > 0, before[1, rows, :], jnp.inf)
            share(c)

        @pl.when(jnp.logical_not(first_col) & (in_up | in_down))
        def _():
            copy3_relay(c, at(col, 0)).wait_recv()
            value = box3_in[c]
            incoming[rows, :] = jnp.where(
                pos > 0, jnp.minimum(value + before[0, rows, :], before[1, rows, :]), value)
            share(c)

            @pl.when(in_up & up_next)
            def _():
                copy3_relay(c, at(col, pos + 1)).start()

            @pl.when(in_down & down_next)
            def _():
                copy3_relay(c, at(col, pos - 1)).start()

        return carry

    lax.fori_loop(0, chunks, stage3, 0)

    def gather(c, carry):
        rows = rows_of(c)
        least = incoming[rows, :]
        for k in range(len(masks)):
            copy4(c, k).wait_recv()
            least = jnp.minimum(least, box4[k, c])
        least_in[rows, :] = least
        return carry

    lax.fori_loop(0, chunks, gather, 0)

    for k in range(len(masks)):
        copy5(k).wait_recv()

    def gather_plane(c, carry):
        rows = rows_of(c)
        least = own[rows, :]
        for k in range(len(masks)):
            least = jnp.minimum(least, box5[k, rows, :])
        least_plane[rows, :] = least
        return carry

    lax.fori_loop(0, chunks, gather_plane, 0)

    def drain(c, carry):
        @pl.when(pos < last)
        def _():
            copy1(c).wait_send()

        @pl.when(is_end & (col < lines - 1))
        def _():
            copy2(c).wait_send()

        @pl.when(is_end & jnp.logical_not(first_col))
        def _():
            for k, p in enumerate(ends_to):
                copy3_from_end(c, k, at(col, p)).wait_send()

        @pl.when(jnp.logical_not(first_col) & ((in_up & up_next) | (in_down & down_next)))
        def _():
            copy3_relay(c, at(col, 0)).wait_send()

        for k in range(len(masks)):
            copy4(c, k).wait_send()
        return carry

    lax.fori_loop(0, chunks, drain, 0)
    for k in range(len(masks)):
        copy5(k).wait_send()


def relay(totals, own, slabs, orders):
    cells_y, cells_z = own.shape
    chunks = cells_y // RELAY_ROWS
    sharers = len(range(2, orders, 2))
    plane = jax.ShapeDtypeStruct(own.shape, jnp.float32)
    line = LINE if slabs % LINE == 0 else slabs
    vmem = pl.BlockSpec(memory_space=pltpu.VMEM)
    box = pltpu.VMEM((chunks, RELAY_ROWS, cells_z), jnp.float32)
    pair_box = pltpu.VMEM((chunks, 2, RELAY_ROWS, cells_z), jnp.float32)
    return pl.pallas_call(
        functools.partial(relay_kernel, line=line),
        out_shape=(plane, plane, plane),
        in_specs=[vmem, vmem],
        out_specs=(vmem, vmem, vmem),
        scratch_shapes=[
            pltpu.VMEM((2, cells_y, cells_z), jnp.float32),
            pltpu.VMEM((2, cells_y, cells_z), jnp.float32),
            pair_box,
            pair_box,
            box,
            box,
            box,
            pltpu.VMEM((max(sharers, 1), chunks, RELAY_ROWS, cells_z), jnp.float32),
            pltpu.VMEM((max(sharers, 1), cells_y, cells_z), jnp.float32),
            pltpu.SemaphoreType.DMA((chunks,)),
            pltpu.SemaphoreType.DMA((chunks,)),
            pltpu.SemaphoreType.DMA((chunks,)),
            pltpu.SemaphoreType.DMA((chunks,)),
            pltpu.SemaphoreType.DMA((chunks, 4)),
            pltpu.SemaphoreType.DMA((chunks,)),
            pltpu.SemaphoreType.DMA((chunks, max(sharers, 1))),
            pltpu.SemaphoreType.DMA((chunks, max(sharers, 1))),
            pltpu.SemaphoreType.DMA((max(sharers, 1),)),
            pltpu.SemaphoreType.DMA((max(sharers, 1),)),
        ],
        compiler_params=pltpu.CompilerParams(collective_id=0, has_side_effects=True),
    )(totals, own)


def shards(previous, fibre_tensor, tissue, stim_sites, stim_times):
    planes, cells_y, cells_z = previous.shape
    slabs = lax.axis_size("slab")
    orders = lax.axis_size("order")
    slab_index = lax.axis_index("slab")
    group_index = lax.axis_index("order")
    grid_step = 2.0 / (planes * slabs)

    plane_index = stim_sites // (cells_y * cells_z) - slab_index * planes
    row_index = stim_sites // cells_z % cells_y
    column_index = stim_sites % cells_z
    stims = jnp.stack([plane_index, row_index, column_index]).astype(jnp.int32)

    bits = jnp.stack([group_index % 2, group_index // 2 % 2, group_index // 4 % 2]).astype(jnp.int32)
    cost_x, field, totals, own_plane = local_sweeps(
        bits, stims, stim_times, fibre_tensor, tissue, previous, grid_step)

    core = group_index % 2
    incoming, least_in, least_plane = relay(totals, own_plane, slabs, orders)
    other = lax.ppermute(jnp.stack([least_plane, least_in]), "order", [(g, g ^ 1) for g in range(orders)])

    least0 = jnp.where(core == 0, least_plane, other[0])
    least1 = jnp.where(core == 0, other[0], least_plane)
    up_in = jnp.where(core == 0, least_in, other[1])
    down_in = jnp.where(core == 0, other[1], least_in)

    up_add = jnp.stack([cost_x[0], cost_x[0] + cost_x[1]])
    up_min = jnp.stack([field[0], jnp.minimum(field[0] + cost_x[1], field[1])])
    down_add = jnp.stack([cost_x[1] + cost_x[0], cost_x[1]])
    down_min = jnp.stack([jnp.minimum(field[1] + cost_x[0], field[0]), field[1]])
    backward_x = core == 1
    line_add = jnp.where(backward_x, down_add, up_add)
    line_min = jnp.where(backward_x, down_min, up_min)
    sweep_field = jnp.minimum(incoming[None] + line_add, line_min)

    least_local = jnp.stack([
        jnp.minimum(least0, least1 + cost_x[0]),
        jnp.minimum(least1, least0 + cost_x[1]),
    ])
    merged = jnp.minimum(
        least_local,
        jnp.minimum(up_in[None] + up_add, down_in[None] + down_add),
    )
    return (merged, sweep_field[None])


def solution(mesh):
    placed = (P("slab", None, None), P(None, "slab", None, None), P("slab", None, None), P(), P())
    return jax.shard_map(
        shards,
        mesh=mesh,
        in_specs=placed,
        out_specs=(P("slab", None, None), P("order", "slab", None, None)),
        check_vma=False,
    )
```
